128 devices in a mesh: req: 8 (over y, core), hist: 16 (over x, z).
Axes of the slice: x: 4, y: 4, z: 4, core: 2. Of those that a mesh axis runs over, the one named last changes fastest.
Arguments:
- cand_x: bfloat16 [16, 2048, 1024], P('req', 'hist'), may hold values from -6 to 6
- kv_cache: bfloat16 [1024, 128, 2048], P(('req', 'hist')), may hold values from -6 to 6
- w_uvqk: bfloat16 [1024, 4096], replicated, may hold values from -0.1875 to 0.1875
- w_out: bfloat16 [1024, 1024], replicated, may hold values from -0.1875 to 0.1875
- self_bias: float32 [8], replicated, may hold values from 1 to 5
- user_rank: int32 [16], replicated, may hold values from 0 to 15, each once
- hist_len: int32 [16], replicated, may hold values from 1 to 8192, 32768 in all
- cand_count: int32 [16], replicated, may hold values from 1 to 2048, 24576 in all
- tile_slot: int32 [16, 64], replicated, may hold values from 0 to 63, as said below
Outputs:
- ranked: bfloat16 [16, 2048, 1024], P('req', 'hist')
The draws below stay inside these ranges and needn't reach their ends.
Inputs may be any that keep to these rules, and one draw needn't show every extreme that they name: Ranking slot g holds the candidates of user user_rank[g]. `tile_slot`: value o * 8 + s: the tile is slot s of the cache block of the device with req index o and hist index j mod 16; every slot of every block holds exactly one tile; one block holds at most 2 tiles of the slots of one req index, exactly 2 for some.
All inputs are finite; a program needn't handle non-finite values.
Results may differ from the reference program's by a relative error of at most 0.014.
Values may be sent and summed in bfloat16 or wider, within the bound.
A program may use at most 128 MiB of HBM per device.

```python
import math
import jax
import jax.numpy as jnp
import numpy as np
from jax import lax

D = 1024
HEADS = 8
TILE = 128
HIST_MAX = 8192
USERS_DEV = 2
CANDS = 2048
NU = 16
TMAX = 64
TPH = 4
OWN = 8
N_REQ = 8
N_HIST = 16


def draw_tile_slot(key, part):
    count_k = OWN
    base_key = jax.random.fold_in(key, 11)
    shift_keys = jax.random.split(jax.random.fold_in(base_key, 1), N_HIST)
    shift_perm = jax.vmap(lambda one_key: jax.random.permutation(one_key, N_REQ))(shift_keys)
    positions = jnp.arange(count_k)
    which_shift = jnp.where(positions == count_k - 1, 0, positions % N_REQ)
    shifts = shift_perm[:, which_shift]
    order_keys = jax.random.split(jax.random.fold_in(base_key, 2), N_HIST * N_REQ)
    orders = jax.vmap(lambda one_key: jax.random.permutation(one_key, count_k))(order_keys)
    orders = orders.reshape(N_HIST, N_REQ * count_k)
    requester = jnp.arange(N_REQ)
    owners = (requester[None, :, None] + shifts[:, None, :]) % N_REQ
    flat_owner = owners.reshape(N_HIST, N_REQ * count_k)
    entries = N_REQ * count_k
    earlier = jnp.arange(entries)[:, None] > jnp.arange(entries)[None, :]
    same_owner = flat_owner[:, :, None] == flat_owner[:, None, :]
    rank_in = jnp.sum(jnp.where(same_owner & earlier[None, :, :], 1, 0), axis=2)
    slot_keys = jax.random.split(jax.random.fold_in(base_key, 3), N_HIST * N_REQ)
    slot_perm = jax.vmap(lambda one_key: jax.random.permutation(one_key, count_k))(slot_keys)
    slot_perm = slot_perm.reshape(N_HIST, N_REQ, count_k)
    column_ids = jnp.arange(N_HIST)[:, None]
    local_slot = slot_perm[column_ids, flat_owner, rank_in]
    codes = flat_owner * count_k + local_slot
    req_of = jnp.repeat(requester, count_k)[None, :]
    slot_g = req_of * USERS_DEV + orders // TPH
    tile_j = column_ids + N_HIST * (orders % TPH)
    result = jnp.zeros((NU, TMAX), jnp.int32)
    return result.at[slot_g.reshape(-1), tile_j.reshape(-1)].set(codes.reshape(-1).astype(jnp.int32))


def block_levels(own_key, extent, shards, least, top_value):
    loudness, own = 1.0, jax.random.fold_in(own_key, 6)
    for position, blocks in shards:
        draws = jnp.exp(jax.random.uniform(jax.random.fold_in(own, position), (blocks,), jnp.float32, least / len(shards), top_value / len(shards)))
        loudness = loudness * jnp.repeat(draws, extent[position] // blocks).reshape([-1 if axis == position else 1 for axis in range(len(extent))])
    return loudness


def length_profile(count, total, bound, lean):
    loads = [(1 << 20) // math.isqrt(grade ** lean) + 1 for grade in range(2, count + 1)]
    rest, holding = total - bound - (count - 1), [1] * (count - 1)
    while rest > 0:
        candidates = [i for i in range(count - 1) if holding[i] < bound]
        pool, left = sum([loads[i] for i in candidates]), rest
        for i in candidates:
            extra = min(bound - holding[i], max(1, left * loads[i] // pool), rest)
            holding[i] = holding[i] + extra
            rest = rest - extra
    return np.array([bound] + holding)


def uneven(key, number_of, total, limit, lean):
    if number_of == 2:
        one = jax.random.randint(key, (), max(1, total - limit), min(limit, total - 1) + 1)
        return jnp.stack([one, total - one])
    lengths = jnp.asarray(length_profile(number_of, total, limit, lean), jnp.int32)
    twos = (number_of - 1) // 2
    donor, receiver = lengths[1:1 + 2 * twos:2], lengths[2:2 + 2 * twos:2]
    room = jnp.minimum(donor - 1, limit - receiver)
    shifted = jax.random.randint(jax.random.fold_in(key, 1), (twos,), 0, 1 << 20) % (room + 1)
    lengths = lengths.at[1:1 + 2 * twos:2].set(donor - shifted).at[2:2 + 2 * twos:2].set(receiver + shifted)
    return lengths[jax.random.permutation(jax.random.fold_in(key, 2), number_of)]


def noise(rng, dims, scale, bound, pieces=(), kind=jnp.bfloat16):
    array = jax.random.normal(rng, dims, jnp.float32) * scale
    if len(pieces) > 0:
        array = block_levels(rng, dims, pieces, -0.22, 0.18) * array
    return jnp.clip(array, min=-bound, max=bound).astype(kind)


def setup_inputs(seed: int = 0) -> dict:
    streams_of = jax.random.split(jax.random.key(seed), 10)
    return {
        "cand_x": noise(streams_of[0], (NU, CANDS, D), 1.0, 6.0, ((0, 8), (1, 16))),
        "kv_cache": noise(streams_of[1], (N_REQ * N_HIST * OWN, TILE, 2 * D), 1.0, 6.0, ((0, 128),)),
        "w_uvqk": noise(streams_of[2], (D, 4 * D), D ** -0.5, 0.1875),
        "w_out": noise(streams_of[3], (D, D), D ** -0.5, 0.1875),
        "self_bias": jnp.clip(jax.random.uniform(streams_of[4], (HEADS,), jnp.float32, 1.0, 5.0), 1.0, 5.0),
        "user_rank": jax.random.permutation(streams_of[5], NU).astype(jnp.int32),
        "hist_len": uneven(streams_of[6], NU, NU * HIST_MAX // 4, HIST_MAX, 2).astype(jnp.int32),
        "cand_count": uneven(streams_of[7], NU, NU * CANDS * 3 // 4, CANDS, 1).astype(jnp.int32),
        "tile_slot": draw_tile_slot(jax.random.fold_in(streams_of[9], 71), 0),
    }


def layer_norm(values):
    mean_value = lax.optimization_barrier(jnp.mean(values, axis=-1, keepdims=True))
    centred = values - mean_value
    spread = lax.optimization_barrier(jnp.mean(centred * centred, axis=-1, keepdims=True))
    return centred * lax.rsqrt(spread + 1e-05)

def reference(cand_x, kv_cache, w_uvqk, w_out, self_bias, user_rank, hist_len, cand_count, tile_slot):
    head_dim = D // HEADS
    score_scale = 1.0 / head_dim ** 0.5
    class_len = TPH * TILE
    key_local = jnp.arange(class_len, dtype=jnp.int32)

    def one_slot(inputs):
        slot_index, rows_in, codes = inputs
        user_id = user_rank[slot_index]
        hist_length = hist_len[user_id]
        live_count = cand_count[user_id]
        normed = layer_norm(rows_in.astype(jnp.float32)).astype(jnp.bfloat16)
        projected = jax.nn.silu(jnp.dot(normed, w_uvqk, preferred_element_type=jnp.float32)).astype(jnp.bfloat16)
        u_gate = projected[:, :D].astype(jnp.float32)
        v_self = projected[:, D:2 * D].astype(jnp.float32).reshape(CANDS, HEADS, head_dim)
        queries = projected[:, 2 * D:3 * D].astype(jnp.float32).reshape(CANDS, HEADS, head_dim)
        k_self = projected[:, 3 * D:].astype(jnp.float32).reshape(CANDS, HEADS, head_dim)
        tile_index = jnp.arange(TMAX, dtype=jnp.int32)
        row_index = (codes // OWN * N_HIST + tile_index % N_HIST) * OWN + codes % OWN
        tiles = jnp.take(kv_cache, row_index.astype(jnp.int32), axis=0)
        by_class = tiles.reshape(TPH, N_HIST, TILE, HEADS, 2, head_dim).transpose(1, 0, 2, 3, 4, 5)
        by_class = by_class.reshape(N_HIST, class_len, HEADS, 2, head_dim)

        def add_class(running, inputs):
            source_class, key_block = inputs
            key_pos = (source_class + N_HIST * (key_local // TILE)) * TILE + key_local % TILE
            block_wide = key_block.astype(jnp.float32)
            scores = jnp.einsum('nhd,khd->hnk', queries, block_wide[:, :, 0, :]) * score_scale
            weights = jnp.where(key_pos[None, None, :] < hist_length, jax.nn.silu(scores), 0.0)
            weights = lax.optimization_barrier(weights.astype(jnp.bfloat16)).astype(jnp.float32)
            class_sum = jnp.einsum('hnk,khd->nhd', weights, block_wide[:, :, 1, :])
            class_sum = lax.optimization_barrier(class_sum.astype(jnp.bfloat16)).astype(jnp.float32)
            return (running + class_sum, None)
        history, _ = lax.scan(add_class, jnp.zeros((CANDS, HEADS, head_dim), jnp.float32), (jnp.arange(N_HIST, dtype=jnp.int32), by_class))
        self_scores = lax.optimization_barrier(jnp.sum(queries * k_self, axis=-1)) * score_scale + self_bias[None, :]
        own_term = jax.nn.silu(self_scores)[:, :, None] * v_self
        attended = (history + own_term) / (hist_length + 1).astype(jnp.float32)
        gated = (layer_norm(attended.reshape(CANDS, D)) * u_gate).astype(jnp.bfloat16)
        result = rows_in.astype(jnp.float32) + jnp.dot(gated, w_out, preferred_element_type=jnp.float32)
        live_rows = jnp.arange(CANDS, dtype=jnp.int32) < live_count
        return jnp.where(live_rows[:, None], result, 0.0).astype(jnp.bfloat16)
    return lax.map(one_slot, (jnp.arange(NU, dtype=jnp.int32), cand_x, tile_slot))
```

```python
import functools
import math

import jax
import jax.numpy as jnp
from jax import lax
from jax.experimental import pallas as pl
from jax.experimental.pallas import tpu as pltpu
from jax.sharding import PartitionSpec as P


def layer_norm(values):
    mean_value = jnp.mean(values, axis=-1, keepdims=True)
    centred = values - mean_value
    spread = jnp.mean(centred * centred, axis=-1, keepdims=True)
    return centred * lax.rsqrt(spread + 1e-05)


def silu_tanh(values):
    return values * (0.5 + 0.5 * jnp.tanh(0.5 * values))


def attend_kernel(len_ref, q_ref, kv_ref, o_ref, acc_ref, *, score_scale, chunk):
    length = len_ref[0]
    n_cls, n_tiles, tile_len, _ = kv_ref.shape
    head_dim = q_ref.shape[1]
    o_ref[...] = jnp.zeros_like(o_ref)

    def one_class(c, carry):
        for ci in range(q_ref.shape[0] // chunk):
            rows = pl.ds(ci * chunk, chunk)
            acc_ref[...] = jnp.zeros_like(acc_ref)
            q_chunk = q_ref[rows, :]
            for t in range(n_tiles):
                remaining = length - (c + n_cls * t) * tile_len

                @pl.when(remaining > 0)
                def _():
                    keys = kv_ref[c, t, :, pl.ds(0, head_dim)]
                    values = kv_ref[c, t, :, pl.ds(head_dim, head_dim)]
                    scores = lax.dot_general(
                        q_chunk, keys, (((1,), (1,)), ((), ())), preferred_element_type=jnp.float32
                    ) * score_scale
                    token = lax.broadcasted_iota(jnp.int32, scores.shape, 1)
                    weights = jnp.where(token < remaining, silu_tanh(scores), 0.0).astype(jnp.bfloat16)
                    acc_ref[...] += jnp.dot(weights, values, preferred_element_type=jnp.float32)

            o_ref[rows, :] += acc_ref[...].astype(jnp.bfloat16).astype(jnp.float32)
        return carry

    lax.fori_loop(0, n_cls, one_class, 0)


def attend(length, q_all, head_tiles, score_scale):
    rows, head_dim = q_all.shape
    chunk = 512
    return pl.pallas_call(
        functools.partial(attend_kernel, score_scale=score_scale, chunk=chunk),
        out_shape=jax.ShapeDtypeStruct((rows, head_dim), jnp.float32),
        in_specs=[
            pl.BlockSpec(memory_space=pltpu.SMEM),
            pl.BlockSpec(memory_space=pltpu.VMEM),
            pl.BlockSpec(memory_space=pltpu.VMEM),
        ],
        out_specs=pl.BlockSpec(memory_space=pltpu.VMEM),
        scratch_shapes=[pltpu.VMEM((chunk, head_dim), jnp.float32)],
    )(length, q_all, head_tiles)


def local(cand_x, kv_cache, w_uvqk, w_out, self_bias, user_rank, hist_len, cand_count, tile_slot):
    users_here, cand_rows, width = cand_x.shape
    heads = self_bias.shape[0]
    head_dim = width // heads
    score_scale = 1.0 / math.sqrt(head_dim)
    slots_own, tile_len, _ = kv_cache.shape
    user_total, tiles_max = tile_slot.shape
    req_count = lax.axis_size("req")
    hist_count = lax.axis_size("hist")
    req_index = lax.axis_index("req")
    hist_index = lax.axis_index("hist")
    per_hist = tiles_max // hist_count
    capacity = slots_own // req_count + 1
    first_slot = req_index * users_here
    user_ids = lax.dynamic_slice_in_dim(user_rank, first_slot, users_here)
    match_user = user_ids[:, None] == jnp.arange(user_total)[None, :]
    lengths = jnp.sum(jnp.where(match_user, hist_len[None, :], 0), axis=1)
    live_counts = jnp.sum(jnp.where(match_user, cand_count[None, :], 0), axis=1)
    column = lax.dynamic_index_in_dim(
        tile_slot.reshape(user_total, per_hist, hist_count), hist_index, axis=2, keepdims=False
    )
    codes = column.reshape(-1)
    owners = codes // slots_own
    local_slot = codes % slots_own
    dests = jnp.repeat(jnp.arange(user_total) // users_here, per_hist)
    entry_ids = jnp.arange(codes.shape[0])
    same_pair = (
        (owners[:, None] == owners[None, :])
        & (dests[:, None] == dests[None, :])
        & (entry_ids[:, None] > entry_ids[None, :])
    )
    places = jnp.sum(jnp.where(same_pair, 1, 0), axis=1)
    picked = (
        (owners[None, None, :] == req_index)
        & (dests[None, None, :] == jnp.arange(req_count)[:, None, None])
        & (places[None, None, :] == jnp.arange(capacity)[None, :, None])
    )
    source_slot = jnp.sum(jnp.where(picked, local_slot[None, None, :], 0), axis=2).reshape(-1)
    filled = jnp.any(picked, axis=2).reshape(-1)
    outgoing = jnp.take(kv_cache, source_slot, axis=0)
    outgoing = jnp.where(filled[:, None, None], outgoing, jnp.zeros((), kv_cache.dtype))
    outgoing = outgoing.reshape(req_count, capacity, tile_len, 2 * width)
    incoming = lax.all_to_all(outgoing, "req", split_axis=0, concat_axis=0, tiled=True)
    first_entry = first_slot * per_hist
    my_owner = lax.dynamic_slice_in_dim(owners, first_entry, users_here * per_hist)
    my_place = lax.dynamic_slice_in_dim(places, first_entry, users_here * per_hist)
    tiles = jnp.take(
        incoming.reshape(req_count * capacity, tile_len, 2 * width),
        my_owner * capacity + my_place,
        axis=0,
    )
    tiles = tiles.reshape(users_here, per_hist, tile_len, heads, 2 * head_dim)
    by_head = tiles.transpose(0, 3, 1, 2, 4).reshape(users_here * heads, per_hist, tile_len, 2 * head_dim)
    head_tiles = lax.all_to_all(by_head, "hist", split_axis=0, concat_axis=0, tiled=True)
    normed = layer_norm(cand_x.astype(jnp.float32)).astype(jnp.bfloat16)
    mixed_in = jnp.dot(normed.reshape(-1, width), w_uvqk, preferred_element_type=jnp.float32)
    projected = jax.nn.silu(mixed_in).astype(jnp.bfloat16).reshape(users_here, cand_rows, 4, width)
    u_gate = projected[:, :, 0]
    v_self = projected[:, :, 1]
    queries = projected[:, :, 2]
    k_self = projected[:, :, 3]
    q_by_head = queries.reshape(users_here, cand_rows, heads, head_dim).transpose(0, 2, 1, 3)
    q_by_head = q_by_head.reshape(users_here * heads, cand_rows, head_dim)
    q_all = lax.all_to_all(q_by_head, "hist", split_axis=0, concat_axis=0, tiled=True)
    q_all = q_all.reshape(hist_count * cand_rows, head_dim)
    my_user = hist_index // heads
    my_length = lax.dynamic_slice_in_dim(lengths, my_user, 1)
    history_mine = attend(my_length, q_all, head_tiles, score_scale)
    history_back = lax.all_to_all(
        history_mine.reshape(hist_count, cand_rows, head_dim), "hist", split_axis=0, concat_axis=0, tiled=True
    )
    combined = history_back.reshape(users_here, heads, cand_rows, head_dim).transpose(0, 2, 1, 3)
    query_wide = queries.astype(jnp.float32).reshape(users_here, cand_rows, heads, head_dim)
    key_wide = k_self.astype(jnp.float32).reshape(users_here, cand_rows, heads, head_dim)
    value_wide = v_self.astype(jnp.float32).reshape(users_here, cand_rows, heads, head_dim)
    self_scores = jnp.sum(query_wide * key_wide, axis=-1) * score_scale + self_bias
    own_term = jax.nn.silu(self_scores)[..., None] * value_wide
    divisor = (lengths + 1).astype(jnp.float32)[:, None, None, None]
    attended = (combined + own_term) / divisor
    gated = (
        layer_norm(attended.reshape(users_here, cand_rows, width)) * u_gate.astype(jnp.float32)
    ).astype(jnp.bfloat16)
    update = jnp.dot(gated.reshape(-1, width), w_out, preferred_element_type=jnp.float32)
    result = cand_x.astype(jnp.float32) + update.reshape(users_here, cand_rows, width)
    cand_index = hist_index * cand_rows + jnp.arange(cand_rows)
    live_rows = cand_index[None, :] < live_counts[:, None]
    return jnp.where(live_rows[:, :, None], result, 0.0).astype(jnp.bfloat16)


def solution(mesh):
    return jax.shard_map(
        local,
        mesh=mesh,
        in_specs=(
            P("req", "hist", None),
            P(("req", "hist"), None, None),
            P(),
            P(),
            P(),
            P(),
            P(),
            P(),
            P(),
        ),
        out_specs=P("req", "hist", None),
        check_vma=False,
    )
```

```python
import functools
import math

import jax
import jax.numpy as jnp
from jax import lax
from jax.experimental import pallas as pl
from jax.experimental.pallas import tpu as pltpu
from jax.sharding import PartitionSpec as P


def layer_norm(values):
    mean_value = jnp.mean(values, axis=-1, keepdims=True)
    centred = values - mean_value
    spread = jnp.mean(centred * centred, axis=-1, keepdims=True)
    return centred * lax.rsqrt(spread + 1e-05)


def silu_tanh(values):
    return values * (0.5 + 0.5 * jnp.tanh(0.5 * values))


def attend_kernel(len_ref, q_ref, kv_ref, o_ref, *, score_scale, chunk):
    length = len_ref[0]
    n_cls, n_tiles, tile_len, _ = kv_ref.shape
    head_dim = q_ref.shape[1]
    span = n_tiles * tile_len
    half_scale = 0.5 * score_scale
    o_ref[...] = jnp.zeros_like(o_ref)

    def one_class(c, carry):
        key_index = lax.broadcasted_iota(jnp.int32, (1, span), 1)
        position = (c + n_cls * (key_index // tile_len)) * tile_len + key_index % tile_len
        live = position < length

        @pl.when(c * tile_len < length)
        def _():
            keys = kv_ref[c, :, :, pl.ds(0, head_dim)].reshape(span, head_dim)
            values = kv_ref[c, :, :, pl.ds(head_dim, head_dim)].reshape(span, head_dim)
            for ci in range(q_ref.shape[0] // chunk):
                rows = pl.ds(ci * chunk, chunk)
                scores = lax.dot_general(
                    q_ref[rows, :], keys, (((1,), (1,)), ((), ())), preferred_element_type=jnp.float32
                )
                half = scores * half_scale
                weights = jnp.where(live, half + half * jnp.tanh(half), 0.0).astype(jnp.bfloat16)
                part = jnp.dot(weights, values, preferred_element_type=jnp.float32)
                o_ref[rows, :] += part.astype(jnp.bfloat16).astype(jnp.float32)

        return carry

    lax.fori_loop(0, n_cls, one_class, 0)


def attend(length, q_all, head_tiles, score_scale):
    rows, head_dim = q_all.shape
    chunk = 512
    return pl.pallas_call(
        functools.partial(attend_kernel, score_scale=score_scale, chunk=chunk),
        out_shape=jax.ShapeDtypeStruct((rows, head_dim), jnp.float32),
        in_specs=[
            pl.BlockSpec(memory_space=pltpu.SMEM),
            pl.BlockSpec(memory_space=pltpu.VMEM),
            pl.BlockSpec(memory_space=pltpu.VMEM),
        ],
        out_specs=pl.BlockSpec(memory_space=pltpu.VMEM),
    )(length, q_all, head_tiles)


def local(cand_x, kv_cache, w_uvqk, w_out, self_bias, user_rank, hist_len, cand_count, tile_slot):
    users_here, cand_rows, width = cand_x.shape
    heads = self_bias.shape[0]
    head_dim = width // heads
    score_scale = 1.0 / math.sqrt(head_dim)
    slots_own, tile_len, _ = kv_cache.shape
    user_total, tiles_max = tile_slot.shape
    req_count = lax.axis_size("req")
    hist_count = lax.axis_size("hist")
    req_index = lax.axis_index("req")
    hist_index = lax.axis_index("hist")
    per_hist = tiles_max // hist_count
    capacity = slots_own // req_count + 1
    first_slot = req_index * users_here
    user_ids = lax.dynamic_slice_in_dim(user_rank, first_slot, users_here)
    match_user = user_ids[:, None] == jnp.arange(user_total)[None, :]
    lengths = jnp.sum(jnp.where(match_user, hist_len[None, :], 0), axis=1)
    live_counts = jnp.sum(jnp.where(match_user, cand_count[None, :], 0), axis=1)
    column = lax.dynamic_index_in_dim(
        tile_slot.reshape(user_total, per_hist, hist_count), hist_index, axis=2, keepdims=False
    )
    codes = column.reshape(-1)
    owners = codes // slots_own
    local_slot = codes % slots_own
    dests = jnp.repeat(jnp.arange(user_total) // users_here, per_hist)
    entry_ids = jnp.arange(codes.shape[0])
    same_pair = (
        (owners[:, None] == owners[None, :])
        & (dests[:, None] == dests[None, :])
        & (entry_ids[:, None] > entry_ids[None, :])
    )
    places = jnp.sum(jnp.where(same_pair, 1, 0), axis=1)
    picked = (
        (owners[None, None, :] == req_index)
        & (dests[None, None, :] == jnp.arange(req_count)[:, None, None])
        & (places[None, None, :] == jnp.arange(capacity)[None, :, None])
    )
    source_slot = jnp.sum(jnp.where(picked, local_slot[None, None, :], 0), axis=2).reshape(-1)
    kv_by_head = kv_cache.reshape(slots_own, tile_len, heads, 2 * head_dim)
    outgoing = jnp.take(kv_by_head, source_slot, axis=0).transpose(0, 2, 1, 3)
    outgoing = outgoing.reshape(req_count, capacity, heads, tile_len, 2 * head_dim)
    incoming = lax.all_to_all(outgoing, "req", split_axis=0, concat_axis=0, tiled=True)
    first_entry = first_slot * per_hist
    my_owner = lax.dynamic_slice_in_dim(owners, first_entry, users_here * per_hist)
    my_place = lax.dynamic_slice_in_dim(places, first_entry, users_here * per_hist)
    picked_slot = (my_owner * capacity + my_place).reshape(users_here, per_hist)
    tiles = incoming.reshape(req_count * capacity, heads, tile_len, 2 * head_dim)[picked_slot]
    by_head = tiles.transpose(0, 2, 1, 3, 4).reshape(users_here * heads, per_hist, tile_len, 2 * head_dim)
    head_tiles = lax.all_to_all(by_head, "hist", split_axis=0, concat_axis=0, tiled=True)
    normed = layer_norm(cand_x.astype(jnp.float32)).astype(jnp.bfloat16)
    mixed_in = jnp.dot(normed.reshape(-1, width), w_uvqk, preferred_element_type=jnp.float32)
    projected = jax.nn.silu(mixed_in).astype(jnp.bfloat16).reshape(users_here, cand_rows, 4, width)
    u_gate = projected[:, :, 0]
    v_self = projected[:, :, 1]
    queries = projected[:, :, 2]
    k_self = projected[:, :, 3]
    q_by_head = queries.reshape(users_here, cand_rows, heads, head_dim).transpose(0, 2, 1, 3)
    q_by_head = q_by_head.reshape(users_here * heads, cand_rows, head_dim)
    q_all = lax.all_to_all(q_by_head, "hist", split_axis=0, concat_axis=0, tiled=True)
    q_all = q_all.reshape(hist_count * cand_rows, head_dim)
    my_user = hist_index // heads
    my_length = lax.dynamic_slice_in_dim(lengths, my_user, 1)
    history_mine = attend(my_length, q_all, head_tiles, score_scale)
    history_back = lax.all_to_all(
        history_mine.reshape(hist_count, cand_rows, head_dim), "hist", split_axis=0, concat_axis=0, tiled=True
    )
    combined = history_back.reshape(users_here, heads, cand_rows, head_dim).transpose(0, 2, 1, 3)
    query_wide = queries.astype(jnp.float32).reshape(users_here, cand_rows, heads, head_dim)
    key_wide = k_self.astype(jnp.float32).reshape(users_here, cand_rows, heads, head_dim)
    value_wide = v_self.astype(jnp.float32).reshape(users_here, cand_rows, heads, head_dim)
    self_scores = jnp.sum(query_wide * key_wide, axis=-1) * score_scale + self_bias
    own_term = jax.nn.silu(self_scores)[..., None] * value_wide
    divisor = (lengths + 1).astype(jnp.float32)[:, None, None, None]
    attended = (combined + own_term) / divisor
    gated = (
        layer_norm(attended.reshape(users_here, cand_rows, width)) * u_gate.astype(jnp.float32)
    ).astype(jnp.bfloat16)
    update = jnp.dot(gated.reshape(-1, width), w_out, preferred_element_type=jnp.float32)
    result = cand_x.astype(jnp.float32) + update.reshape(users_here, cand_rows, width)
    cand_index = hist_index * cand_rows + jnp.arange(cand_rows)
    live_rows = cand_index[None, :] < live_counts[:, None]
    return jnp.where(live_rows[:, :, None], result, 0.0).astype(jnp.bfloat16)


def solution(mesh):
    return jax.shard_map(
        local,
        mesh=mesh,
        in_specs=(
            P("req", "hist", None),
            P(("req", "hist"), None, None),
            P(),
            P(),
            P(),
            P(),
            P(),
            P(),
            P(),
        ),
        out_specs=P("req", "hist", None),
        check_vma=False,
    )
```

```python
import functools
import math

import jax
import jax.numpy as jnp
from jax import lax
from jax.experimental import pallas as pl
from jax.experimental.pallas import tpu as pltpu
from jax.sharding import PartitionSpec as P


def layer_norm(values):
    mean_value = jnp.mean(values, axis=-1, keepdims=True)
    centred = values - mean_value
    spread = jnp.mean(centred * centred, axis=-1, keepdims=True)
    return centred * lax.rsqrt(spread + 1e-05)


def silu_tanh(values):
    return values * (0.5 + 0.5 * jnp.tanh(0.5 * values))


def attend_kernel(len_ref, packed_ref, o_ref, q_ref, *, span, tile_len, score_scale, chunk):
    length = len_ref[0]
    n_cls, _, head_dim = packed_ref.shape
    block = q_ref.shape[0] // n_cls
    half_scale = 0.5 * score_scale
    for b in range(n_cls):
        q_ref[pl.ds(b * block, block), :] = packed_ref[b, pl.ds(2 * span, block), :]
    o_ref[...] = jnp.zeros_like(o_ref)

    def one_class(c, carry):
        key_index = lax.broadcasted_iota(jnp.int32, (1, span), 1)
        position = (c + n_cls * (key_index // tile_len)) * tile_len + key_index % tile_len
        live = position < length

        @pl.when(c * tile_len < length)
        def _():
            keys = packed_ref[c, pl.ds(0, span), :]
            values = packed_ref[c, pl.ds(span, span), :]
            for ci in range(q_ref.shape[0] // chunk):
                rows = pl.ds(ci * chunk, chunk)
                scores = lax.dot_general(
                    q_ref[rows, :], keys, (((1,), (1,)), ((), ())), preferred_element_type=jnp.float32
                )
                half = scores * half_scale
                weights = jnp.where(live, half + half * jnp.tanh(half), 0.0).astype(jnp.bfloat16)
                part = jnp.dot(weights, values, preferred_element_type=jnp.float32)
                o_ref[rows, :] += part.astype(jnp.bfloat16).astype(jnp.float32)

        return carry

    lax.fori_loop(0, n_cls, one_class, 0)


def attend(length, packed, per_hist, tile_len, score_scale):
    span = per_hist * tile_len
    n_cls, packed_rows, head_dim = packed.shape
    rows = n_cls * (packed_rows - 2 * span)
    chunk = 512
    kernel = functools.partial(
        attend_kernel, span=span, tile_len=tile_len, score_scale=score_scale, chunk=chunk
    )
    return pl.pallas_call(
        kernel,
        out_shape=jax.ShapeDtypeStruct((rows, head_dim), jnp.float32),
        in_specs=[
            pl.BlockSpec(memory_space=pltpu.SMEM),
            pl.BlockSpec(memory_space=pltpu.VMEM),
        ],
        out_specs=pl.BlockSpec(memory_space=pltpu.VMEM),
        scratch_shapes=[pltpu.VMEM((rows, head_dim), jnp.bfloat16)],
    )(length, packed)


def local(cand_x, kv_cache, w_uvqk, w_out, self_bias, user_rank, hist_len, cand_count, tile_slot):
    users_here, cand_rows, width = cand_x.shape
    heads = self_bias.shape[0]
    head_dim = width // heads
    score_scale = 1.0 / math.sqrt(head_dim)
    slots_own, tile_len, _ = kv_cache.shape
    user_total, tiles_max = tile_slot.shape
    req_count = lax.axis_size("req")
    hist_count = lax.axis_size("hist")
    req_index = lax.axis_index("req")
    hist_index = lax.axis_index("hist")
    per_hist = tiles_max // hist_count
    capacity = slots_own // req_count + 1
    first_slot = req_index * users_here
    user_ids = lax.dynamic_slice_in_dim(user_rank, first_slot, users_here)
    match_user = user_ids[:, None] == jnp.arange(user_total)[None, :]
    lengths = jnp.sum(jnp.where(match_user, hist_len[None, :], 0), axis=1)
    live_counts = jnp.sum(jnp.where(match_user, cand_count[None, :], 0), axis=1)
    column = lax.dynamic_index_in_dim(
        tile_slot.reshape(user_total, per_hist, hist_count), hist_index, axis=2, keepdims=False
    )
    codes = column.reshape(-1)
    owners = codes // slots_own
    local_slot = codes % slots_own
    dests = jnp.repeat(jnp.arange(user_total) // users_here, per_hist)
    entry_ids = jnp.arange(codes.shape[0])
    same_pair = (
        (owners[:, None] == owners[None, :])
        & (dests[:, None] == dests[None, :])
        & (entry_ids[:, None] > entry_ids[None, :])
    )
    places = jnp.sum(jnp.where(same_pair, 1, 0), axis=1)
    picked = (
        (owners[None, None, :] == req_index)
        & (dests[None, None, :] == jnp.arange(req_count)[:, None, None])
        & (places[None, None, :] == jnp.arange(capacity)[None, :, None])
    )
    source_slot = jnp.sum(jnp.where(picked, local_slot[None, None, :], 0), axis=2).reshape(-1)
    outgoing = kv_cache.at[source_slot].get(mode="promise_in_bounds")
    outgoing = outgoing.reshape(req_count, capacity, tile_len, 2 * width)
    incoming = lax.all_to_all(outgoing, "req", split_axis=0, concat_axis=0, tiled=True)
    first_entry = first_slot * per_hist
    my_owner = lax.dynamic_slice_in_dim(owners, first_entry, users_here * per_hist)
    my_place = lax.dynamic_slice_in_dim(places, first_entry, users_here * per_hist)
    picked_slot = my_owner * capacity + my_place
    tiles = incoming.reshape(req_count * capacity, tile_len, 2 * width)
    tiles = tiles.at[picked_slot].get(mode="promise_in_bounds")
    tiles = tiles.reshape(users_here, per_hist, tile_len, heads, 2, head_dim)
    by_head = tiles.transpose(0, 3, 4, 1, 2, 5).reshape(users_here * heads, 2 * per_hist * tile_len, head_dim)
    normed = layer_norm(cand_x.astype(jnp.float32)).astype(jnp.bfloat16)
    mixed_in = jnp.dot(normed.reshape(-1, width), w_uvqk, preferred_element_type=jnp.float32)
    projected = jax.nn.silu(mixed_in).astype(jnp.bfloat16).reshape(users_here, cand_rows, 4, width)
    u_gate = projected[:, :, 0]
    v_self = projected[:, :, 1]
    queries = projected[:, :, 2]
    k_self = projected[:, :, 3]
    q_by_head = queries.reshape(users_here, cand_rows, heads, head_dim).transpose(0, 2, 1, 3)
    q_by_head = q_by_head.reshape(users_here * heads, cand_rows, head_dim)
    packed = lax.all_to_all(
        jnp.concatenate([by_head, q_by_head], axis=1), "hist", split_axis=0, concat_axis=0, tiled=True
    )
    my_user = hist_index // heads
    my_length = lax.dynamic_slice_in_dim(lengths, my_user, 1)
    history_mine = attend(my_length, packed, per_hist, tile_len, score_scale)
    history_back = lax.all_to_all(
        history_mine.reshape(hist_count, cand_rows, head_dim), "hist", split_axis=0, concat_axis=0, tiled=True
    )
    combined = history_back.reshape(users_here, heads, cand_rows, head_dim).transpose(0, 2, 1, 3)
    query_wide = queries.astype(jnp.float32).reshape(users_here, cand_rows, heads, head_dim)
    key_wide = k_self.astype(jnp.float32).reshape(users_here, cand_rows, heads, head_dim)
    value_wide = v_self.astype(jnp.float32).reshape(users_here, cand_rows, heads, head_dim)
    self_scores = jnp.sum(query_wide * key_wide, axis=-1) * score_scale + self_bias
    own_term = jax.nn.silu(self_scores)[..., None] * value_wide
    divisor = (lengths + 1).astype(jnp.float32)[:, None, None, None]
    attended = (combined + own_term) / divisor
    gated = (
        layer_norm(attended.reshape(users_here, cand_rows, width)) * u_gate.astype(jnp.float32)
    ).astype(jnp.bfloat16)
    update = jnp.dot(gated.reshape(-1, width), w_out, preferred_element_type=jnp.float32)
    result = cand_x.astype(jnp.float32) + update.reshape(users_here, cand_rows, width)
    cand_index = hist_index * cand_rows + jnp.arange(cand_rows)
    live_rows = cand_index[None, :] < live_counts[:, None]
    return jnp.where(live_rows[:, :, None], result, 0.0).astype(jnp.bfloat16)


def solution(mesh):
    return jax.shard_map(
        local,
        mesh=mesh,
        in_specs=(
            P("req", "hist", None),
            P(("req", "hist"), None, None),
            P(),
            P(),
            P(),
            P(),
            P(),
            P(),
            P(),
        ),
        out_specs=P("req", "hist", None),
        check_vma=False,
    )
```

```python
import functools
import math

import jax
import jax.numpy as jnp
from jax import lax
from jax.experimental import pallas as pl
from jax.experimental.pallas import tpu as pltpu
from jax.sharding import PartitionSpec as P


def layer_norm(values):
    mean_value = jnp.mean(values, axis=-1, keepdims=True)
    centred = values - mean_value
    spread = jnp.mean(centred * centred, axis=-1, keepdims=True)
    return centred * lax.rsqrt(spread + 1e-05)


def silu_tanh(values):
    return values * (0.5 + 0.5 * jnp.tanh(0.5 * values))


def attend_kernel(len_ref, packed_ref, o_ref, q_ref, *, span, tile_len, score_scale, chunk):
    length = len_ref[0]
    n_cls, _, head_dim = packed_ref.shape
    block = q_ref.shape[0] // n_cls
    half_scale = 0.5 * score_scale
    for b in range(n_cls):
        q_ref[pl.ds(b * block, block), :] = packed_ref[b, pl.ds(2 * span, block), :]
    o_ref[...] = jnp.zeros_like(o_ref)

    def one_class(c, carry):
        key_index = lax.broadcasted_iota(jnp.int32, (1, span), 1)
        position = (c + n_cls * (key_index // tile_len)) * tile_len + key_index % tile_len
        live = position < length

        @pl.when(c * tile_len < length)
        def _():
            keys = packed_ref[c, pl.ds(0, span), :]
            values = packed_ref[c, pl.ds(span, span), :]
            for ci in range(q_ref.shape[0] // chunk):
                rows = pl.ds(ci * chunk, chunk)
                scores = lax.dot_general(
                    q_ref[rows, :], keys, (((1,), (1,)), ((), ())), preferred_element_type=jnp.float32
                )
                half = scores * half_scale
                weights = jnp.where(live, half + half * jnp.tanh(half), 0.0).astype(jnp.bfloat16)
                part = jnp.dot(weights, values, preferred_element_type=jnp.float32)
                o_ref[rows, :] += part.astype(jnp.bfloat16).astype(jnp.float32)

        return carry

    lax.fori_loop(0, n_cls, one_class, 0)


def attend(length, packed, per_hist, tile_len, score_scale):
    span = per_hist * tile_len
    n_cls, packed_rows, head_dim = packed.shape
    rows = n_cls * (packed_rows - 2 * span)
    chunk = 512
    kernel = functools.partial(
        attend_kernel, span=span, tile_len=tile_len, score_scale=score_scale, chunk=chunk
    )
    return pl.pallas_call(
        kernel,
        out_shape=jax.ShapeDtypeStruct((rows, head_dim), jnp.float32),
        in_specs=[
            pl.BlockSpec(memory_space=pltpu.SMEM),
            pl.BlockSpec(memory_space=pltpu.VMEM),
        ],
        out_specs=pl.BlockSpec(memory_space=pltpu.VMEM),
        scratch_shapes=[pltpu.VMEM((rows, head_dim), jnp.bfloat16)],
    )(length, packed)


def pack_kernel(picked_ref, tiles_hbm, q_hbm, out_hbm, staged, in_sem, out_sem, q_sem, *, heads, per_hist):
    users, cand_rows, width = q_hbm.shape
    head_dim = width // heads
    tile_len = tiles_hbm.shape[1]
    span = per_hist * tile_len
    n_in = users * per_hist
    reads = []
    for i in range(n_in):
        read = pltpu.make_async_copy(tiles_hbm.at[picked_ref[i]], staged.at[i], in_sem.at[i])
        read.start()
        reads.append(read)
    writes = []
    for u in range(users):
        for e in range(heads):
            write = pltpu.make_async_copy(
                q_hbm.at[u, :, pl.ds(e * head_dim, head_dim)],
                out_hbm.at[u * heads + e, pl.ds(2 * span, cand_rows), :],
                q_sem.at[u * heads + e],
            )
            write.start()
            writes.append(write)
    for i in range(n_in):
        u, t = divmod(i, per_hist)
        reads[i].wait()
        for piece in range(2 * heads):
            e, kv = divmod(piece, 2)
            write = pltpu.make_async_copy(
                staged.at[i, :, pl.ds(piece * head_dim, head_dim)],
                out_hbm.at[u * heads + e, pl.ds(kv * span + t * tile_len, tile_len), :],
                out_sem.at[i, piece],
            )
            write.start()
            writes.append(write)
    for write in writes:
        write.wait()


def pack_for_heads(picked_slot, tiles, queries, heads):
    users, cand_rows, width = queries.shape
    head_dim = width // heads
    n_in = picked_slot.shape[0]
    per_hist = n_in // users
    tile_len = tiles.shape[1]
    rows = 2 * per_hist * tile_len + cand_rows
    return pl.pallas_call(
        functools.partial(pack_kernel, heads=heads, per_hist=per_hist),
        out_shape=jax.ShapeDtypeStruct((users * heads, rows, head_dim), tiles.dtype),
        in_specs=[
            pl.BlockSpec(memory_space=pltpu.SMEM),
            pl.BlockSpec(memory_space=pl.ANY),
            pl.BlockSpec(memory_space=pl.ANY),
        ],
        out_specs=pl.BlockSpec(memory_space=pl.ANY),
        scratch_shapes=[
            pltpu.VMEM((n_in, tile_len, tiles.shape[2]), tiles.dtype),
            pltpu.SemaphoreType.DMA((n_in,)),
            pltpu.SemaphoreType.DMA((n_in, 2 * heads)),
            pltpu.SemaphoreType.DMA((users * heads,)),
        ],
    )(picked_slot, tiles, queries)


def local(cand_x, kv_cache, w_uvqk, w_out, self_bias, user_rank, hist_len, cand_count, tile_slot):
    users_here, cand_rows, width = cand_x.shape
    heads = self_bias.shape[0]
    head_dim = width // heads
    score_scale = 1.0 / math.sqrt(head_dim)
    slots_own, tile_len, _ = kv_cache.shape
    user_total, tiles_max = tile_slot.shape
    req_count = lax.axis_size("req")
    hist_count = lax.axis_size("hist")
    req_index = lax.axis_index("req")
    hist_index = lax.axis_index("hist")
    per_hist = tiles_max // hist_count
    capacity = slots_own // req_count + 1
    first_slot = req_index * users_here
    user_ids = lax.dynamic_slice_in_dim(user_rank, first_slot, users_here)
    match_user = user_ids[:, None] == jnp.arange(user_total)[None, :]
    lengths = jnp.sum(jnp.where(match_user, hist_len[None, :], 0), axis=1)
    live_counts = jnp.sum(jnp.where(match_user, cand_count[None, :], 0), axis=1)
    column = lax.dynamic_index_in_dim(
        tile_slot.reshape(user_total, per_hist, hist_count), hist_index, axis=2, keepdims=False
    )
    codes = column.reshape(-1)
    owners = codes // slots_own
    local_slot = codes % slots_own
    dests = jnp.repeat(jnp.arange(user_total) // users_here, per_hist)
    entry_ids = jnp.arange(codes.shape[0])
    same_pair = (
        (owners[:, None] == owners[None, :])
        & (dests[:, None] == dests[None, :])
        & (entry_ids[:, None] > entry_ids[None, :])
    )
    places = jnp.sum(jnp.where(same_pair, 1, 0), axis=1)
    picked = (
        (owners[None, None, :] == req_index)
        & (dests[None, None, :] == jnp.arange(req_count)[:, None, None])
        & (places[None, None, :] == jnp.arange(capacity)[None, :, None])
    )
    source_slot = jnp.sum(jnp.where(picked, local_slot[None, None, :], 0), axis=2).reshape(-1)
    outgoing = kv_cache.at[source_slot].get(mode="promise_in_bounds")
    outgoing = outgoing.reshape(req_count, capacity, tile_len, 2 * width)
    incoming = lax.all_to_all(outgoing, "req", split_axis=0, concat_axis=0, tiled=True)
    first_entry = first_slot * per_hist
    my_owner = lax.dynamic_slice_in_dim(owners, first_entry, users_here * per_hist)
    my_place = lax.dynamic_slice_in_dim(places, first_entry, users_here * per_hist)
    picked_slot = (my_owner * capacity + my_place).astype(jnp.int32)
    normed = layer_norm(cand_x.astype(jnp.float32)).astype(jnp.bfloat16)
    mixed_in = jnp.dot(normed.reshape(-1, width), w_uvqk, preferred_element_type=jnp.float32)
    projected = jax.nn.silu(mixed_in).astype(jnp.bfloat16).reshape(users_here, cand_rows, 4, width)
    u_gate = projected[:, :, 0]
    v_self = projected[:, :, 1]
    queries = projected[:, :, 2]
    k_self = projected[:, :, 3]
    send = pack_for_heads(
        picked_slot, incoming.reshape(req_count * capacity, tile_len, 2 * width), queries, heads
    )
    packed = lax.all_to_all(send, "hist", split_axis=0, concat_axis=0, tiled=True)
    my_user = hist_index // heads
    my_length = lax.dynamic_slice_in_dim(lengths, my_user, 1)
    history_mine = attend(my_length, packed, per_hist, tile_len, score_scale)
    history_back = lax.all_to_all(
        history_mine.reshape(hist_count, cand_rows, head_dim), "hist", split_axis=0, concat_axis=0, tiled=True
    )
    combined = history_back.reshape(users_here, heads, cand_rows, head_dim).transpose(0, 2, 1, 3)
    query_wide = queries.astype(jnp.float32).reshape(users_here, cand_rows, heads, head_dim)
    key_wide = k_self.astype(jnp.float32).reshape(users_here, cand_rows, heads, head_dim)
    value_wide = v_self.astype(jnp.float32).reshape(users_here, cand_rows, heads, head_dim)
    self_scores = jnp.sum(query_wide * key_wide, axis=-1) * score_scale + self_bias
    own_term = jax.nn.silu(self_scores)[..., None] * value_wide
    divisor = (lengths + 1).astype(jnp.float32)[:, None, None, None]
    attended = (combined + own_term) / divisor
    gated = (
        layer_norm(attended.reshape(users_here, cand_rows, width)) * u_gate.astype(jnp.float32)
    ).astype(jnp.bfloat16)
    update = jnp.dot(gated.reshape(-1, width), w_out, preferred_element_type=jnp.float32)
    result = cand_x.astype(jnp.float32) + update.reshape(users_here, cand_rows, width)
    cand_index = hist_index * cand_rows + jnp.arange(cand_rows)
    live_rows = cand_index[None, :] < live_counts[:, None]
    return jnp.where(live_rows[:, :, None], result, 0.0).astype(jnp.bfloat16)


def solution(mesh):
    return jax.shard_map(
        local,
        mesh=mesh,
        in_specs=(
            P("req", "hist", None),
            P(("req", "hist"), None, None),
            P(),
            P(),
            P(),
            P(),
            P(),
            P(),
            P(),
        ),
        out_specs=P("req", "hist", None),
        check_vma=False,
    )
```

```python
import functools
import math

import jax
import jax.numpy as jnp
from jax import lax
from jax.experimental import pallas as pl
from jax.experimental.pallas import tpu as pltpu
from jax.sharding import PartitionSpec as P


def layer_norm(values):
    mean_value = jnp.mean(values, axis=-1, keepdims=True)
    centred = values - mean_value
    spread = jnp.mean(centred * centred, axis=-1, keepdims=True)
    return centred * lax.rsqrt(spread + 1e-05)


def silu_tanh(values):
    return values * (0.5 + 0.5 * jnp.tanh(0.5 * values))


def attend_kernel(len_ref, packed_ref, o_ref, q_ref, *, span, tile_len, score_scale, chunk):
    length = len_ref[0]
    n_cls, _, head_dim = packed_ref.shape
    block = q_ref.shape[0] // n_cls
    half_scale = 0.5 * score_scale
    for b in range(n_cls):
        q_ref[pl.ds(b * block, block), :] = packed_ref[b, pl.ds(2 * span, block), :]
    o_ref[...] = jnp.zeros_like(o_ref)

    def one_class(c, carry):
        key_index = lax.broadcasted_iota(jnp.int32, (1, span), 1)
        position = (c + n_cls * (key_index // tile_len)) * tile_len + key_index % tile_len
        live = position < length

        def add_class(masked):
            keys = packed_ref[c, pl.ds(0, span), :]
            values = packed_ref[c, pl.ds(span, span), :]
            for ci in range(q_ref.shape[0] // chunk):
                rows = pl.ds(ci * chunk, chunk)
                scores = lax.dot_general(
                    q_ref[rows, :], keys, (((1,), (1,)), ((), ())), preferred_element_type=jnp.float32
                )
                half = scores * half_scale
                weights = half + half * jnp.tanh(half)
                if masked:
                    weights = jnp.where(live, weights, 0.0)
                part = jnp.dot(weights.astype(jnp.bfloat16), values, preferred_element_type=jnp.float32)
                o_ref[rows, :] += part.astype(jnp.bfloat16).astype(jnp.float32)

        last_start = (c + n_cls * (span // tile_len - 1)) * tile_len
        whole = last_start + tile_len <= length
        pl.when(whole)(lambda: add_class(False))
        pl.when(jnp.logical_and(jnp.logical_not(whole), c * tile_len < length))(lambda: add_class(True))

        return carry

    lax.fori_loop(0, n_cls, one_class, 0)


def attend(length, packed, per_hist, tile_len, score_scale):
    span = per_hist * tile_len
    n_cls, packed_rows, head_dim = packed.shape
    rows = n_cls * (packed_rows - 2 * span)
    chunk = 512
    kernel = functools.partial(
        attend_kernel, span=span, tile_len=tile_len, score_scale=score_scale, chunk=chunk
    )
    return pl.pallas_call(
        kernel,
        out_shape=jax.ShapeDtypeStruct((rows, head_dim), jnp.float32),
        in_specs=[
            pl.BlockSpec(memory_space=pltpu.SMEM),
            pl.BlockSpec(memory_space=pltpu.VMEM),
        ],
        out_specs=pl.BlockSpec(memory_space=pltpu.VMEM),
        scratch_shapes=[pltpu.VMEM((rows, head_dim), jnp.bfloat16)],
    )(length, packed)


def pack_kernel(picked_ref, tiles_hbm, q_ref, out_ref, staged, in_sem, *, heads, per_hist):
    users, cand_rows, width = q_ref.shape
    head_dim = width // heads
    tile_len = tiles_hbm.shape[1]
    span = per_hist * tile_len
    n_in = users * per_hist
    reads = []
    for i in range(n_in):
        read = pltpu.make_async_copy(tiles_hbm.at[picked_ref[i]], staged.at[i], in_sem.at[i])
        read.start()
        reads.append(read)
    for u in range(users):
        for e in range(heads):
            out_ref[u * heads + e, pl.ds(2 * span, cand_rows), :] = q_ref[u, :, pl.ds(e * head_dim, head_dim)]
    for i in range(n_in):
        u, t = divmod(i, per_hist)
        reads[i].wait()
        for piece in range(2 * heads):
            e, kv = divmod(piece, 2)
            out_ref[u * heads + e, pl.ds(kv * span + t * tile_len, tile_len), :] = staged[
                i, :, pl.ds(piece * head_dim, head_dim)
            ]


def pack_for_heads(picked_slot, tiles, queries, heads):
    users, cand_rows, width = queries.shape
    head_dim = width // heads
    n_in = picked_slot.shape[0]
    per_hist = n_in // users
    tile_len = tiles.shape[1]
    rows = 2 * per_hist * tile_len + cand_rows
    return pl.pallas_call(
        functools.partial(pack_kernel, heads=heads, per_hist=per_hist),
        out_shape=jax.ShapeDtypeStruct((users * heads, rows, head_dim), tiles.dtype),
        in_specs=[
            pl.BlockSpec(memory_space=pltpu.SMEM),
            pl.BlockSpec(memory_space=pl.ANY),
            pl.BlockSpec(memory_space=pltpu.VMEM),
        ],
        out_specs=pl.BlockSpec(memory_space=pltpu.VMEM),
        scratch_shapes=[
            pltpu.VMEM((n_in, tile_len, tiles.shape[2]), tiles.dtype),
            pltpu.SemaphoreType.DMA((n_in,)),
        ],
    )(picked_slot, tiles, queries)


def local(cand_x, kv_cache, w_uvqk, w_out, self_bias, user_rank, hist_len, cand_count, tile_slot):
    users_here, cand_rows, width = cand_x.shape
    heads = self_bias.shape[0]
    head_dim = width // heads
    score_scale = 1.0 / math.sqrt(head_dim)
    slots_own, tile_len, _ = kv_cache.shape
    user_total, tiles_max = tile_slot.shape
    req_count = lax.axis_size("req")
    hist_count = lax.axis_size("hist")
    req_index = lax.axis_index("req")
    hist_index = lax.axis_index("hist")
    per_hist = tiles_max // hist_count
    capacity = slots_own // req_count + 1
    first_slot = req_index * users_here
    user_ids = lax.dynamic_slice_in_dim(user_rank, first_slot, users_here)
    match_user = user_ids[:, None] == jnp.arange(user_total)[None, :]
    lengths = jnp.sum(jnp.where(match_user, hist_len[None, :], 0), axis=1)
    live_counts = jnp.sum(jnp.where(match_user, cand_count[None, :], 0), axis=1)
    column = lax.dynamic_index_in_dim(
        tile_slot.reshape(user_total, per_hist, hist_count), hist_index, axis=2, keepdims=False
    )
    codes = column.reshape(-1)
    owners = codes // slots_own
    local_slot = codes % slots_own
    dests = jnp.repeat(jnp.arange(user_total) // users_here, per_hist)
    entry_ids = jnp.arange(codes.shape[0])
    same_pair = (
        (owners[:, None] == owners[None, :])
        & (dests[:, None] == dests[None, :])
        & (entry_ids[:, None] > entry_ids[None, :])
    )
    places = jnp.sum(jnp.where(same_pair, 1, 0), axis=1)
    picked = (
        (owners[None, None, :] == req_index)
        & (dests[None, None, :] == jnp.arange(req_count)[:, None, None])
        & (places[None, None, :] == jnp.arange(capacity)[None, :, None])
    )
    source_slot = jnp.sum(jnp.where(picked, local_slot[None, None, :], 0), axis=2).reshape(-1)
    outgoing = kv_cache.at[source_slot].get(mode="promise_in_bounds")
    outgoing = outgoing.reshape(req_count, capacity, tile_len, 2 * width)
    incoming = lax.all_to_all(outgoing, "req", split_axis=0, concat_axis=0, tiled=True)
    first_entry = first_slot * per_hist
    my_owner = lax.dynamic_slice_in_dim(owners, first_entry, users_here * per_hist)
    my_place = lax.dynamic_slice_in_dim(places, first_entry, users_here * per_hist)
    picked_slot = (my_owner * capacity + my_place).astype(jnp.int32)
    normed = layer_norm(cand_x.astype(jnp.float32)).astype(jnp.bfloat16)
    mixed_in = jnp.dot(normed.reshape(-1, width), w_uvqk, preferred_element_type=jnp.float32)
    projected = jax.nn.silu(mixed_in).astype(jnp.bfloat16).reshape(users_here, cand_rows, 4, width)
    u_gate = projected[:, :, 0]
    v_self = projected[:, :, 1]
    queries = projected[:, :, 2]
    k_self = projected[:, :, 3]
    send = pack_for_heads(
        picked_slot, incoming.reshape(req_count * capacity, tile_len, 2 * width), queries, heads
    )
    packed = lax.all_to_all(send, "hist", split_axis=0, concat_axis=0, tiled=True)
    my_user = hist_index // heads
    my_length = lax.dynamic_slice_in_dim(lengths, my_user, 1)
    history_mine = attend(my_length, packed, per_hist, tile_len, score_scale)
    history_back = lax.all_to_all(
        history_mine.reshape(hist_count, cand_rows, head_dim), "hist", split_axis=0, concat_axis=0, tiled=True
    )
    combined = history_back.reshape(users_here, heads, cand_rows, head_dim).transpose(0, 2, 1, 3)
    query_wide = queries.astype(jnp.float32).reshape(users_here, cand_rows, heads, head_dim)
    key_wide = k_self.astype(jnp.float32).reshape(users_here, cand_rows, heads, head_dim)
    value_wide = v_self.astype(jnp.float32).reshape(users_here, cand_rows, heads, head_dim)
    self_scores = jnp.sum(query_wide * key_wide, axis=-1) * score_scale + self_bias
    own_term = jax.nn.silu(self_scores)[..., None] * value_wide
    divisor = (lengths + 1).astype(jnp.float32)[:, None, None, None]
    attended = (combined + own_term) / divisor
    gated = (
        layer_norm(attended.reshape(users_here, cand_rows, width)) * u_gate.astype(jnp.float32)
    ).astype(jnp.bfloat16)
    update = jnp.dot(gated.reshape(-1, width), w_out, preferred_element_type=jnp.float32)
    result = cand_x.astype(jnp.float32) + update.reshape(users_here, cand_rows, width)
    cand_index = hist_index * cand_rows + jnp.arange(cand_rows)
    live_rows = cand_index[None, :] < live_counts[:, None]
    return jnp.where(live_rows[:, :, None], result, 0.0).astype(jnp.bfloat16)


def solution(mesh):
    return jax.shard_map(
        local,
        mesh=mesh,
        in_specs=(
            P("req", "hist", None),
            P(("req", "hist"), None, None),
            P(),
            P(),
            P(),
            P(),
            P(),
            P(),
            P(),
        ),
        out_specs=P("req", "hist", None),
        check_vma=False,
    )
```

```python
import functools
import math

import jax
import jax.numpy as jnp
from jax import lax
from jax.experimental import pallas as pl
from jax.experimental.pallas import tpu as pltpu
from jax.sharding import PartitionSpec as P


def layer_norm(values):
    mean_value = jnp.mean(values, axis=-1, keepdims=True)
    centred = values - mean_value
    spread = jnp.mean(centred * centred, axis=-1, keepdims=True)
    return centred * lax.rsqrt(spread + 1e-05)


def silu_tanh(values):
    return values * (0.5 + 0.5 * jnp.tanh(0.5 * values))


def req_a2a_kernel(send_ref, recv_ref, send_sem, recv_sem, local_sem, *, axis, other_axis):
    n = send_ref.shape[0]
    me = lax.axis_index(axis)
    other = lax.axis_index(other_axis)
    barrier = pltpu.get_barrier_semaphore()
    for k in range(1, n):
        peer = lax.rem(me + k, n)
        pl.semaphore_signal(
            barrier, inc=1, device_id={axis: peer, other_axis: other}, device_id_type=pl.DeviceIdType.MESH
        )
    pl.semaphore_wait(barrier, n - 1)
    copies = []
    for k in range(1, n):
        peer = lax.rem(me + k, n)
        copy = pltpu.make_async_remote_copy(
            src_ref=send_ref.at[peer],
            dst_ref=recv_ref.at[me],
            send_sem=send_sem.at[k],
            recv_sem=recv_sem.at[k],
            device_id={axis: peer, other_axis: other},
            device_id_type=pl.DeviceIdType.MESH,
        )
        copy.start()
        copies.append(copy)
    own = pltpu.make_async_copy(send_ref.at[me], recv_ref.at[me], local_sem)
    own.start()
    own.wait()
    for copy in copies:
        copy.wait_send()
    for k in range(1, n):
        src = lax.rem(me + n - k, n)
        pltpu.make_async_remote_copy(
            src_ref=send_ref.at[src],
            dst_ref=recv_ref.at[src],
            send_sem=send_sem.at[k],
            recv_sem=recv_sem.at[k],
            device_id={axis: src, other_axis: other},
            device_id_type=pl.DeviceIdType.MESH,
        ).wait_recv()


def req_a2a(x, collective_id):
    n = x.shape[0]
    return pl.pallas_call(
        functools.partial(req_a2a_kernel, axis="req", other_axis="hist"),
        out_shape=jax.ShapeDtypeStruct(x.shape, x.dtype),
        in_specs=[pl.BlockSpec(memory_space=pl.ANY)],
        out_specs=pl.BlockSpec(memory_space=pl.ANY),
        scratch_shapes=[
            pltpu.SemaphoreType.DMA((n,)),
            pltpu.SemaphoreType.DMA((n,)),
            pltpu.SemaphoreType.DMA(()),
        ],
        compiler_params=pltpu.CompilerParams(collective_id=collective_id, has_side_effects=True),
    )(x)


def attend_kernel(
    len_ref, kv_ref, qsrc_ref, o_ref, q_ref, *, n_tiles, sub, tile_len, offset, q_row, score_scale, chunk
):
    length = len_ref[0]
    n_cls, _, head_dim = kv_ref.shape
    span = n_tiles * sub
    block = q_ref.shape[0] // n_cls
    half_scale = 0.5 * score_scale
    for b in range(n_cls):
        q_ref[pl.ds(b * block, block), :] = qsrc_ref[b, pl.ds(q_row, block), :]
    o_ref[...] = jnp.zeros_like(o_ref)

    def one_class(c, carry):
        key_index = lax.broadcasted_iota(jnp.int32, (1, span), 1)
        position = (c + n_cls * (key_index // sub)) * tile_len + offset + key_index % sub
        live = position < length

        def add_class(masked):
            keys = kv_ref[c, pl.ds(0, span), :]
            values = kv_ref[c, pl.ds(span, span), :]
            for ci in range(q_ref.shape[0] // chunk):
                rows = pl.ds(ci * chunk, chunk)
                scores = lax.dot_general(
                    q_ref[rows, :], keys, (((1,), (1,)), ((), ())), preferred_element_type=jnp.float32
                )
                half = scores * half_scale
                weights = half + half * jnp.tanh(half)
                if masked:
                    weights = jnp.where(live, weights, 0.0)
                o_ref[rows, :] += jnp.dot(weights.astype(jnp.bfloat16), values, preferred_element_type=jnp.float32)

        last_key = (c + n_cls * (n_tiles - 1)) * tile_len + offset + sub
        whole = last_key <= length
        pl.when(whole)(lambda: add_class(False))
        pl.when(jnp.logical_and(jnp.logical_not(whole), c * tile_len + offset < length))(lambda: add_class(True))
        return carry

    lax.fori_loop(0, n_cls, one_class, 0)


def attend(length, kv_packed, q_packed, q_row, sub, tile_len, offset, score_scale):
    n_cls, _, head_dim = q_packed.shape
    rows = n_cls * (q_packed.shape[1] - q_row)
    chunk = 512
    kernel = functools.partial(
        attend_kernel,
        n_tiles=q_row // (2 * sub),
        sub=sub,
        tile_len=tile_len,
        offset=offset,
        q_row=q_row,
        score_scale=score_scale,
        chunk=chunk,
    )
    return pl.pallas_call(
        kernel,
        out_shape=jax.ShapeDtypeStruct((rows, head_dim), jnp.float32),
        in_specs=[
            pl.BlockSpec(memory_space=pltpu.SMEM),
            pl.BlockSpec(memory_space=pltpu.VMEM),
            pl.BlockSpec(memory_space=pltpu.VMEM),
        ],
        out_specs=pl.BlockSpec(memory_space=pltpu.VMEM),
        scratch_shapes=[pltpu.VMEM((rows, head_dim), jnp.bfloat16)],
    )(length, kv_packed, q_packed)


def pack_kernel(picked_ref, tiles_hbm, *rest, heads, users, per_hist, with_q):
    if with_q:
        q_ref, out_ref, staged, in_sem = rest
    else:
        out_ref, staged, in_sem = rest
    width = tiles_hbm.shape[2] // 2
    head_dim = width // heads
    sub = tiles_hbm.shape[1]
    span = per_hist * sub
    n_in = users * per_hist
    reads = []
    for i in range(n_in):
        read = pltpu.make_async_copy(tiles_hbm.at[picked_ref[i]], staged.at[i], in_sem.at[i])
        read.start()
        reads.append(read)
    if with_q:
        cand_rows = q_ref.shape[1]
        for u in range(users):
            for e in range(heads):
                out_ref[u * heads + e, pl.ds(2 * span, cand_rows), :] = q_ref[u, :, pl.ds(e * head_dim, head_dim)]
    for i in range(n_in):
        u, t = divmod(i, per_hist)
        reads[i].wait()
        for piece in range(2 * heads):
            e, kv = divmod(piece, 2)
            out_ref[u * heads + e, pl.ds(kv * span + t * sub, sub), :] = staged[
                i, :, pl.ds(piece * head_dim, head_dim)
            ]


def pack_for_heads(picked_slot, tiles, queries, users, heads):
    n_in = picked_slot.shape[0]
    per_hist = n_in // users
    sub, wide = tiles.shape[1], tiles.shape[2]
    head_dim = wide // (2 * heads)
    rows = 2 * per_hist * sub + (0 if queries is None else queries.shape[1])
    operands = [picked_slot, tiles] + ([] if queries is None else [queries])
    return pl.pallas_call(
        functools.partial(pack_kernel, heads=heads, users=users, per_hist=per_hist, with_q=queries is not None),
        out_shape=jax.ShapeDtypeStruct((users * heads, rows, head_dim), tiles.dtype),
        in_specs=[pl.BlockSpec(memory_space=pltpu.SMEM), pl.BlockSpec(memory_space=pl.ANY)]
        + ([] if queries is None else [pl.BlockSpec(memory_space=pltpu.VMEM)]),
        out_specs=pl.BlockSpec(memory_space=pltpu.VMEM),
        scratch_shapes=[
            pltpu.VMEM((n_in, sub, wide), tiles.dtype),
            pltpu.SemaphoreType.DMA((n_in,)),
        ],
    )(*operands)


def local(cand_x, kv_cache, w_uvqk, w_out, self_bias, user_rank, hist_len, cand_count, tile_slot):
    users_here, cand_rows, width = cand_x.shape
    heads = self_bias.shape[0]
    head_dim = width // heads
    score_scale = 1.0 / math.sqrt(head_dim)
    slots_own, tile_len, _ = kv_cache.shape
    user_total, tiles_max = tile_slot.shape
    req_count = lax.axis_size("req")
    hist_count = lax.axis_size("hist")
    req_index = lax.axis_index("req")
    hist_index = lax.axis_index("hist")
    per_hist = tiles_max // hist_count
    capacity = slots_own // req_count + 1
    first_slot = req_index * users_here
    user_ids = lax.dynamic_slice_in_dim(user_rank, first_slot, users_here)
    match_user = user_ids[:, None] == jnp.arange(user_total)[None, :]
    lengths = jnp.sum(jnp.where(match_user, hist_len[None, :], 0), axis=1)
    live_counts = jnp.sum(jnp.where(match_user, cand_count[None, :], 0), axis=1)
    column = lax.dynamic_index_in_dim(
        tile_slot.reshape(user_total, per_hist, hist_count), hist_index, axis=2, keepdims=False
    )
    codes = column.reshape(-1)
    owners = codes // slots_own
    local_slot = codes % slots_own
    dests = jnp.repeat(jnp.arange(user_total) // users_here, per_hist)
    entry_ids = jnp.arange(codes.shape[0])
    same_pair = (
        (owners[:, None] == owners[None, :])
        & (dests[:, None] == dests[None, :])
        & (entry_ids[:, None] > entry_ids[None, :])
    )
    places = jnp.sum(jnp.where(same_pair, 1, 0), axis=1)
    picked = (
        (owners[None, None, :] == req_index)
        & (dests[None, None, :] == jnp.arange(req_count)[:, None, None])
        & (places[None, None, :] == jnp.arange(capacity)[None, :, None])
    )
    source_slot = jnp.sum(jnp.where(picked, local_slot[None, None, :], 0), axis=2).reshape(-1)
    first_entry = first_slot * per_hist
    my_owner = lax.dynamic_slice_in_dim(owners, first_entry, users_here * per_hist)
    my_place = lax.dynamic_slice_in_dim(places, first_entry, users_here * per_hist)
    picked_slot = (my_owner * capacity + my_place).astype(jnp.int32)
    sub = tile_len // 2
    halves = []
    for half in range(2):
        kv_half = lax.slice_in_dim(kv_cache, half * sub, (half + 1) * sub, axis=1)
        outgoing = kv_half.at[source_slot].get(mode="promise_in_bounds")
        incoming = req_a2a(outgoing.reshape(req_count, capacity, sub, 2 * width), half)
        halves.append(incoming.reshape(req_count * capacity, sub, 2 * width))
    normed = layer_norm(cand_x.astype(jnp.float32)).astype(jnp.bfloat16)
    mixed_in = jnp.dot(normed.reshape(-1, width), w_uvqk, preferred_element_type=jnp.float32)
    projected = jax.nn.silu(mixed_in).astype(jnp.bfloat16).reshape(users_here, cand_rows, 4, width)
    u_gate = projected[:, :, 0]
    v_self = projected[:, :, 1]
    queries = projected[:, :, 2]
    k_self = projected[:, :, 3]
    my_user = hist_index // heads
    my_length = lax.dynamic_slice_in_dim(lengths, my_user, 1)
    q_row = 2 * per_hist * sub
    packed_a = lax.all_to_all(
        pack_for_heads(picked_slot, halves[0], queries, users_here, heads),
        "hist", split_axis=0, concat_axis=0, tiled=True,
    )
    history_mine = attend(my_length, packed_a, packed_a, q_row, sub, tile_len, 0, score_scale)
    packed_b = lax.all_to_all(
        pack_for_heads(picked_slot, halves[1], None, users_here, heads),
        "hist", split_axis=0, concat_axis=0, tiled=True,
    )
    history_mine = history_mine + attend(my_length, packed_b, packed_a, q_row, sub, tile_len, sub, score_scale)
    history_back = lax.all_to_all(
        history_mine.reshape(hist_count, cand_rows, head_dim), "hist", split_axis=0, concat_axis=0, tiled=True
    )
    combined = history_back.reshape(users_here, heads, cand_rows, head_dim).transpose(0, 2, 1, 3)
    query_wide = queries.astype(jnp.float32).reshape(users_here, cand_rows, heads, head_dim)
    key_wide = k_self.astype(jnp.float32).reshape(users_here, cand_rows, heads, head_dim)
    value_wide = v_self.astype(jnp.float32).reshape(users_here, cand_rows, heads, head_dim)
    self_scores = jnp.sum(query_wide * key_wide, axis=-1) * score_scale + self_bias
    own_term = jax.nn.silu(self_scores)[..., None] * value_wide
    divisor = (lengths + 1).astype(jnp.float32)[:, None, None, None]
    attended = (combined + own_term) / divisor
    gated = (
        layer_norm(attended.reshape(users_here, cand_rows, width)) * u_gate.astype(jnp.float32)
    ).astype(jnp.bfloat16)
    update = jnp.dot(gated.reshape(-1, width), w_out, preferred_element_type=jnp.float32)
    result = cand_x.astype(jnp.float32) + update.reshape(users_here, cand_rows, width)
    cand_index = hist_index * cand_rows + jnp.arange(cand_rows)
    live_rows = cand_index[None, :] < live_counts[:, None]
    return jnp.where(live_rows[:, :, None], result, 0.0).astype(jnp.bfloat16)


def solution(mesh):
    return jax.shard_map(
        local,
        mesh=mesh,
        in_specs=(
            P("req", "hist", None),
            P(("req", "hist"), None, None),
            P(),
            P(),
            P(),
            P(),
            P(),
            P(),
            P(),
        ),
        out_specs=P("req", "hist", None),
        check_vma=False,
    )
```

```python
import functools
import math

import jax
import jax.numpy as jnp
from jax import lax
from jax.experimental import pallas as pl
from jax.experimental.pallas import tpu as pltpu
from jax.sharding import PartitionSpec as P


def layer_norm(values):
    mean_value = jnp.mean(values, axis=-1, keepdims=True)
    centred = values - mean_value
    spread = jnp.mean(centred * centred, axis=-1, keepdims=True)
    return centred * lax.rsqrt(spread + 1e-05)


def silu_tanh(values):
    return values * (0.5 + 0.5 * jnp.tanh(0.5 * values))


def req_a2a_kernel(send_ref, recv_ref, send_sem, recv_sem, local_sem, *, axis, other_axis):
    n = send_ref.shape[0]
    me = lax.axis_index(axis)
    other = lax.axis_index(other_axis)
    barrier = pltpu.get_barrier_semaphore()
    for k in range(1, n):
        peer = lax.rem(me + k, n)
        pl.semaphore_signal(
            barrier, inc=1, device_id={axis: peer, other_axis: other}, device_id_type=pl.DeviceIdType.MESH
        )
    pl.semaphore_wait(barrier, n - 1)
    copies = []
    for k in range(1, n):
        peer = lax.rem(me + k, n)
        copy = pltpu.make_async_remote_copy(
            src_ref=send_ref.at[peer],
            dst_ref=recv_ref.at[me],
            send_sem=send_sem.at[k],
            recv_sem=recv_sem.at[k],
            device_id={axis: peer, other_axis: other},
            device_id_type=pl.DeviceIdType.MESH,
        )
        copy.start()
        copies.append(copy)
    own = pltpu.make_async_copy(send_ref.at[me], recv_ref.at[me], local_sem)
    own.start()
    own.wait()
    for copy in copies:
        copy.wait_send()
    for k in range(1, n):
        src = lax.rem(me + n - k, n)
        pltpu.make_async_remote_copy(
            src_ref=send_ref.at[src],
            dst_ref=recv_ref.at[src],
            send_sem=send_sem.at[k],
            recv_sem=recv_sem.at[k],
            device_id={axis: src, other_axis: other},
            device_id_type=pl.DeviceIdType.MESH,
        ).wait_recv()


def req_a2a(x, collective_id):
    n = x.shape[0]
    return pl.pallas_call(
        functools.partial(req_a2a_kernel, axis="req", other_axis="hist"),
        out_shape=jax.ShapeDtypeStruct(x.shape, x.dtype),
        in_specs=[pl.BlockSpec(memory_space=pl.ANY)],
        out_specs=pl.BlockSpec(memory_space=pl.ANY),
        scratch_shapes=[
            pltpu.SemaphoreType.DMA((n,)),
            pltpu.SemaphoreType.DMA((n,)),
            pltpu.SemaphoreType.DMA(()),
        ],
        compiler_params=pltpu.CompilerParams(collective_id=collective_id, has_side_effects=True),
    )(x)


def attend_kernel(
    len_ref, kv_ref, qsrc_ref, o_ref, q_ref, *, n_tiles, sub, tile_len, offset, q_row, score_scale, chunk
):
    length = len_ref[0]
    n_cls, _, head_dim = kv_ref.shape
    span = n_tiles * sub
    block = q_ref.shape[0] // n_cls
    half_scale = 0.5 * score_scale
    for b in range(n_cls):
        q_ref[pl.ds(b * block, block), :] = qsrc_ref[b, pl.ds(q_row, block), :]
    o_ref[...] = jnp.zeros_like(o_ref)

    def one_class(c, carry):
        key_index = lax.broadcasted_iota(jnp.int32, (1, span), 1)
        position = (c + n_cls * (key_index // sub)) * tile_len + offset + key_index % sub
        live = position < length

        def add_class(masked):
            keys = kv_ref[c, pl.ds(0, span), :]
            values = kv_ref[c, pl.ds(span, span), :]
            for ci in range(q_ref.shape[0] // chunk):
                rows = pl.ds(ci * chunk, chunk)
                scores = lax.dot_general(
                    q_ref[rows, :], keys, (((1,), (1,)), ((), ())), preferred_element_type=jnp.float32
                )
                half = scores * half_scale
                weights = half + half * jnp.tanh(half)
                if masked:
                    weights = jnp.where(live, weights, 0.0)
                o_ref[rows, :] += jnp.dot(weights.astype(jnp.bfloat16), values, preferred_element_type=jnp.float32)

        last_key = (c + n_cls * (n_tiles - 1)) * tile_len + offset + sub
        whole = last_key <= length
        pl.when(whole)(lambda: add_class(False))
        pl.when(jnp.logical_and(jnp.logical_not(whole), c * tile_len + offset < length))(lambda: add_class(True))
        return carry

    lax.fori_loop(0, n_cls, one_class, 0)


def attend(length, kv_packed, q_packed, q_row, sub, tile_len, offset, score_scale):
    n_cls, _, head_dim = q_packed.shape
    rows = n_cls * (q_packed.shape[1] - q_row)
    chunk = 2048
    kernel = functools.partial(
        attend_kernel,
        n_tiles=q_row // (2 * sub),
        sub=sub,
        tile_len=tile_len,
        offset=offset,
        q_row=q_row,
        score_scale=score_scale,
        chunk=chunk,
    )
    return pl.pallas_call(
        kernel,
        out_shape=jax.ShapeDtypeStruct((rows, head_dim), jnp.float32),
        in_specs=[
            pl.BlockSpec(memory_space=pltpu.SMEM),
            pl.BlockSpec(memory_space=pltpu.VMEM),
            pl.BlockSpec(memory_space=pltpu.VMEM),
        ],
        out_specs=pl.BlockSpec(memory_space=pltpu.VMEM),
        scratch_shapes=[pltpu.VMEM((rows, head_dim), jnp.bfloat16)],
    )(length, kv_packed, q_packed)


def pack_kernel(picked_ref, tiles_hbm, *rest, heads, users, per_hist, with_q):
    if with_q:
        q_ref, out_ref, staged, in_sem = rest
    else:
        out_ref, staged, in_sem = rest
    width = tiles_hbm.shape[2] // 2
    head_dim = width // heads
    sub = tiles_hbm.shape[1]
    span = per_hist * sub
    n_in = users * per_hist
    reads = []
    for i in range(n_in):
        read = pltpu.make_async_copy(tiles_hbm.at[picked_ref[i]], staged.at[i], in_sem.at[i])
        read.start()
        reads.append(read)
    if with_q:
        cand_rows = q_ref.shape[1]
        for u in range(users):
            for e in range(heads):
                out_ref[u * heads + e, pl.ds(2 * span, cand_rows), :] = q_ref[u, :, pl.ds(e * head_dim, head_dim)]
    for i in range(n_in):
        u, t = divmod(i, per_hist)
        reads[i].wait()
        for piece in range(2 * heads):
            e, kv = divmod(piece, 2)
            out_ref[u * heads + e, pl.ds(kv * span + t * sub, sub), :] = staged[
                i, :, pl.ds(piece * head_dim, head_dim)
            ]


def pack_for_heads(picked_slot, tiles, queries, users, heads):
    n_in = picked_slot.shape[0]
    per_hist = n_in // users
    sub, wide = tiles.shape[1], tiles.shape[2]
    head_dim = wide // (2 * heads)
    rows = 2 * per_hist * sub + (0 if queries is None else queries.shape[1])
    operands = [picked_slot, tiles] + ([] if queries is None else [queries])
    return pl.pallas_call(
        functools.partial(pack_kernel, heads=heads, users=users, per_hist=per_hist, with_q=queries is not None),
        out_shape=jax.ShapeDtypeStruct((users * heads, rows, head_dim), tiles.dtype),
        in_specs=[pl.BlockSpec(memory_space=pltpu.SMEM), pl.BlockSpec(memory_space=pl.ANY)]
        + ([] if queries is None else [pl.BlockSpec(memory_space=pltpu.VMEM)]),
        out_specs=pl.BlockSpec(memory_space=pltpu.VMEM),
        scratch_shapes=[
            pltpu.VMEM((n_in, sub, wide), tiles.dtype),
            pltpu.SemaphoreType.DMA((n_in,)),
        ],
    )(*operands)


def local(cand_x, kv_cache, w_uvqk, w_out, self_bias, user_rank, hist_len, cand_count, tile_slot):
    users_here, cand_rows, width = cand_x.shape
    heads = self_bias.shape[0]
    head_dim = width // heads
    score_scale = 1.0 / math.sqrt(head_dim)
    slots_own, tile_len, _ = kv_cache.shape
    user_total, tiles_max = tile_slot.shape
    req_count = lax.axis_size("req")
    hist_count = lax.axis_size("hist")
    req_index = lax.axis_index("req")
    hist_index = lax.axis_index("hist")
    per_hist = tiles_max // hist_count
    capacity = slots_own // req_count + 1
    first_slot = req_index * users_here
    user_ids = lax.dynamic_slice_in_dim(user_rank, first_slot, users_here)
    match_user = user_ids[:, None] == jnp.arange(user_total)[None, :]
    lengths = jnp.sum(jnp.where(match_user, hist_len[None, :], 0), axis=1)
    live_counts = jnp.sum(jnp.where(match_user, cand_count[None, :], 0), axis=1)
    column = lax.dynamic_index_in_dim(
        tile_slot.reshape(user_total, per_hist, hist_count), hist_index, axis=2, keepdims=False
    )
    codes = column.reshape(-1)
    owners = codes // slots_own
    local_slot = codes % slots_own
    dests = jnp.repeat(jnp.arange(user_total) // users_here, per_hist)
    entry_ids = jnp.arange(codes.shape[0])
    same_pair = (
        (owners[:, None] == owners[None, :])
        & (dests[:, None] == dests[None, :])
        & (entry_ids[:, None] > entry_ids[None, :])
    )
    places = jnp.sum(jnp.where(same_pair, 1, 0), axis=1)
    picked = (
        (owners[None, None, :] == req_index)
        & (dests[None, None, :] == jnp.arange(req_count)[:, None, None])
        & (places[None, None, :] == jnp.arange(capacity)[None, :, None])
    )
    source_slot = jnp.sum(jnp.where(picked, local_slot[None, None, :], 0), axis=2).reshape(-1)
    first_entry = first_slot * per_hist
    my_owner = lax.dynamic_slice_in_dim(owners, first_entry, users_here * per_hist)
    my_place = lax.dynamic_slice_in_dim(places, first_entry, users_here * per_hist)
    picked_slot = (my_owner * capacity + my_place).astype(jnp.int32)
    sub = tile_len // 2
    halves = []
    for half in range(2):
        kv_half = lax.slice_in_dim(kv_cache, half * sub, (half + 1) * sub, axis=1)
        outgoing = kv_half.at[source_slot].get(mode="promise_in_bounds")
        outgoing = outgoing.reshape(req_count, capacity, sub, 2 * width)
        if half == 0:
            incoming = lax.all_to_all(outgoing, "req", split_axis=0, concat_axis=0, tiled=True)
        else:
            incoming = req_a2a(outgoing, 0)
        halves.append(incoming.reshape(req_count * capacity, sub, 2 * width))
    normed = layer_norm(cand_x.astype(jnp.float32)).astype(jnp.bfloat16)
    mixed_in = jnp.dot(normed.reshape(-1, width), w_uvqk, preferred_element_type=jnp.float32)
    projected = jax.nn.silu(mixed_in).astype(jnp.bfloat16).reshape(users_here, cand_rows, 4, width)
    u_gate = projected[:, :, 0]
    v_self = projected[:, :, 1]
    queries = projected[:, :, 2]
    k_self = projected[:, :, 3]
    my_user = hist_index // heads
    my_length = lax.dynamic_slice_in_dim(lengths, my_user, 1)
    q_row = 2 * per_hist * sub
    packed_a = lax.all_to_all(
        pack_for_heads(picked_slot, halves[0], queries, users_here, heads),
        "hist", split_axis=0, concat_axis=0, tiled=True,
    )
    history_mine = attend(my_length, packed_a, packed_a, q_row, sub, tile_len, 0, score_scale)
    packed_b = lax.all_to_all(
        pack_for_heads(picked_slot, halves[1], None, users_here, heads),
        "hist", split_axis=0, concat_axis=0, tiled=True,
    )
    history_mine = history_mine + attend(my_length, packed_b, packed_a, q_row, sub, tile_len, sub, score_scale)
    history_back = lax.all_to_all(
        history_mine.reshape(hist_count, cand_rows, head_dim), "hist", split_axis=0, concat_axis=0, tiled=True
    )
    combined = history_back.reshape(users_here, heads, cand_rows, head_dim).transpose(0, 2, 1, 3)
    query_wide = queries.astype(jnp.float32).reshape(users_here, cand_rows, heads, head_dim)
    key_wide = k_self.astype(jnp.float32).reshape(users_here, cand_rows, heads, head_dim)
    value_wide = v_self.astype(jnp.float32).reshape(users_here, cand_rows, heads, head_dim)
    self_scores = jnp.sum(query_wide * key_wide, axis=-1) * score_scale + self_bias
    own_term = jax.nn.silu(self_scores)[..., None] * value_wide
    divisor = (lengths + 1).astype(jnp.float32)[:, None, None, None]
    attended = (combined + own_term) / divisor
    gated = (
        layer_norm(attended.reshape(users_here, cand_rows, width)) * u_gate.astype(jnp.float32)
    ).astype(jnp.bfloat16)
    update = jnp.dot(gated.reshape(-1, width), w_out, preferred_element_type=jnp.float32)
    result = cand_x.astype(jnp.float32) + update.reshape(users_here, cand_rows, width)
    cand_index = hist_index * cand_rows + jnp.arange(cand_rows)
    live_rows = cand_index[None, :] < live_counts[:, None]
    return jnp.where(live_rows[:, :, None], result, 0.0).astype(jnp.bfloat16)


def solution(mesh):
    return jax.shard_map(
        local,
        mesh=mesh,
        in_specs=(
            P("req", "hist", None),
            P(("req", "hist"), None, None),
            P(),
            P(),
            P(),
            P(),
            P(),
            P(),
            P(),
        ),
        out_specs=P("req", "hist", None),
        check_vma=False,
    )
```

```python
import functools
import math

import jax
import jax.numpy as jnp
from jax import lax
from jax.experimental import pallas as pl
from jax.experimental.pallas import tpu as pltpu
from jax.sharding import PartitionSpec as P


def layer_norm(values):
    mean_value = jnp.mean(values, axis=-1, keepdims=True)
    centred = values - mean_value
    spread = jnp.mean(centred * centred, axis=-1, keepdims=True)
    return centred * lax.rsqrt(spread + 1e-05)


def silu_tanh(values):
    return values * (0.5 + 0.5 * jnp.tanh(0.5 * values))


def req_a2a_kernel(send_ref, recv_ref, send_sem, recv_sem, local_sem, *, axis, other_axis):
    n = send_ref.shape[0]
    me = lax.axis_index(axis)
    other = lax.axis_index(other_axis)
    barrier = pltpu.get_barrier_semaphore()
    for k in range(1, n):
        peer = lax.rem(me + k, n)
        pl.semaphore_signal(
            barrier, inc=1, device_id={axis: peer, other_axis: other}, device_id_type=pl.DeviceIdType.MESH
        )
    pl.semaphore_wait(barrier, n - 1)
    copies = []
    for k in range(1, n):
        peer = lax.rem(me + k, n)
        copy = pltpu.make_async_remote_copy(
            src_ref=send_ref.at[peer],
            dst_ref=recv_ref.at[me],
            send_sem=send_sem.at[k],
            recv_sem=recv_sem.at[k],
            device_id={axis: peer, other_axis: other},
            device_id_type=pl.DeviceIdType.MESH,
        )
        copy.start()
        copies.append(copy)
    own = pltpu.make_async_copy(send_ref.at[me], recv_ref.at[me], local_sem)
    own.start()
    own.wait()
    for copy in copies:
        copy.wait_send()
    for k in range(1, n):
        src = lax.rem(me + n - k, n)
        pltpu.make_async_remote_copy(
            src_ref=send_ref.at[src],
            dst_ref=recv_ref.at[src],
            send_sem=send_sem.at[k],
            recv_sem=recv_sem.at[k],
            device_id={axis: src, other_axis: other},
            device_id_type=pl.DeviceIdType.MESH,
        ).wait_recv()


def req_a2a(x, collective_id):
    n = x.shape[0]
    return pl.pallas_call(
        functools.partial(req_a2a_kernel, axis="req", other_axis="hist"),
        out_shape=jax.ShapeDtypeStruct(x.shape, x.dtype),
        in_specs=[pl.BlockSpec(memory_space=pl.ANY)],
        out_specs=pl.BlockSpec(memory_space=pl.ANY),
        scratch_shapes=[
            pltpu.SemaphoreType.DMA((n,)),
            pltpu.SemaphoreType.DMA((n,)),
            pltpu.SemaphoreType.DMA(()),
        ],
        compiler_params=pltpu.CompilerParams(collective_id=collective_id, has_side_effects=True),
    )(x)


def attend_kernel(
    len_ref, kv_ref, qsrc_ref, o_ref, q_ref, *, n_tiles, sub, tile_len, offset, q_row, score_scale, chunk
):
    length = len_ref[0]
    n_cls, _, head_dim = kv_ref.shape
    span = n_tiles * sub
    block = q_ref.shape[0] // n_cls
    half_scale = 0.5 * score_scale
    for b in range(n_cls):
        q_ref[pl.ds(b * block, block), :] = qsrc_ref[b, pl.ds(q_row, block), :]
    o_ref[...] = jnp.zeros_like(o_ref)

    def one_class(c, carry):
        key_index = lax.broadcasted_iota(jnp.int32, (1, span), 1)
        position = (c + n_cls * (key_index // sub)) * tile_len + offset + key_index % sub
        live = position < length

        def add_class(masked):
            keys = kv_ref[c, pl.ds(0, span), :]
            values = kv_ref[c, pl.ds(span, span), :]
            for ci in range(q_ref.shape[0] // chunk):
                rows = pl.ds(ci * chunk, chunk)
                scores = lax.dot_general(
                    q_ref[rows, :], keys, (((1,), (1,)), ((), ())), preferred_element_type=jnp.float32
                )
                half = (scores * half_scale).astype(jnp.bfloat16)
                weights = half + half * jnp.tanh(half)
                if masked:
                    weights = jnp.where(live, weights, jnp.zeros_like(weights))
                o_ref[rows, :] += jnp.dot(weights, values, preferred_element_type=jnp.float32)

        last_key = (c + n_cls * (n_tiles - 1)) * tile_len + offset + sub
        whole = last_key <= length
        pl.when(whole)(lambda: add_class(False))
        pl.when(jnp.logical_and(jnp.logical_not(whole), c * tile_len + offset < length))(lambda: add_class(True))
        return carry

    lax.fori_loop(0, n_cls, one_class, 0)


def attend(length, kv_packed, q_packed, q_row, sub, tile_len, offset, score_scale):
    n_cls, _, head_dim = q_packed.shape
    rows = n_cls * (q_packed.shape[1] - q_row)
    chunk = 2048
    kernel = functools.partial(
        attend_kernel,
        n_tiles=q_row // (2 * sub),
        sub=sub,
        tile_len=tile_len,
        offset=offset,
        q_row=q_row,
        score_scale=score_scale,
        chunk=chunk,
    )
    return pl.pallas_call(
        kernel,
        out_shape=jax.ShapeDtypeStruct((rows, head_dim), jnp.float32),
        in_specs=[
            pl.BlockSpec(memory_space=pltpu.SMEM),
            pl.BlockSpec(memory_space=pltpu.VMEM),
            pl.BlockSpec(memory_space=pltpu.VMEM),
        ],
        out_specs=pl.BlockSpec(memory_space=pltpu.VMEM),
        scratch_shapes=[pltpu.VMEM((rows, head_dim), jnp.bfloat16)],
    )(length, kv_packed, q_packed)


def pack_kernel(picked_ref, tiles_hbm, *rest, heads, users, per_hist, with_q):
    if with_q:
        q_ref, out_ref, staged, in_sem = rest
    else:
        out_ref, staged, in_sem = rest
    width = tiles_hbm.shape[2] // 2
    head_dim = width // heads
    sub = tiles_hbm.shape[1]
    span = per_hist * sub
    n_in = users * per_hist
    reads = []
    for i in range(n_in):
        read = pltpu.make_async_copy(tiles_hbm.at[picked_ref[i]], staged.at[i], in_sem.at[i])
        read.start()
        reads.append(read)
    if with_q:
        cand_rows = q_ref.shape[1]
        for u in range(users):
            for e in range(heads):
                out_ref[u * heads + e, pl.ds(2 * span, cand_rows), :] = q_ref[u, :, pl.ds(e * head_dim, head_dim)]
    for i in range(n_in):
        u, t = divmod(i, per_hist)
        reads[i].wait()
        for piece in range(2 * heads):
            e, kv = divmod(piece, 2)
            out_ref[u * heads + e, pl.ds(kv * span + t * sub, sub), :] = staged[
                i, :, pl.ds(piece * head_dim, head_dim)
            ]


def pack_for_heads(picked_slot, tiles, queries, users, heads):
    n_in = picked_slot.shape[0]
    per_hist = n_in // users
    sub, wide = tiles.shape[1], tiles.shape[2]
    head_dim = wide // (2 * heads)
    rows = 2 * per_hist * sub + (0 if queries is None else queries.shape[1])
    operands = [picked_slot, tiles] + ([] if queries is None else [queries])
    return pl.pallas_call(
        functools.partial(pack_kernel, heads=heads, users=users, per_hist=per_hist, with_q=queries is not None),
        out_shape=jax.ShapeDtypeStruct((users * heads, rows, head_dim), tiles.dtype),
        in_specs=[pl.BlockSpec(memory_space=pltpu.SMEM), pl.BlockSpec(memory_space=pl.ANY)]
        + ([] if queries is None else [pl.BlockSpec(memory_space=pltpu.VMEM)]),
        out_specs=pl.BlockSpec(memory_space=pltpu.VMEM),
        scratch_shapes=[
            pltpu.VMEM((n_in, sub, wide), tiles.dtype),
            pltpu.SemaphoreType.DMA((n_in,)),
        ],
    )(*operands)


def local(cand_x, kv_cache, w_uvqk, w_out, self_bias, user_rank, hist_len, cand_count, tile_slot):
    users_here, cand_rows, width = cand_x.shape
    heads = self_bias.shape[0]
    head_dim = width // heads
    score_scale = 1.0 / math.sqrt(head_dim)
    slots_own, tile_len, _ = kv_cache.shape
    user_total, tiles_max = tile_slot.shape
    req_count = lax.axis_size("req")
    hist_count = lax.axis_size("hist")
    req_index = lax.axis_index("req")
    hist_index = lax.axis_index("hist")
    per_hist = tiles_max // hist_count
    capacity = slots_own // req_count + 1
    first_slot = req_index * users_here
    user_ids = lax.dynamic_slice_in_dim(user_rank, first_slot, users_here)
    match_user = user_ids[:, None] == jnp.arange(user_total)[None, :]
    lengths = jnp.sum(jnp.where(match_user, hist_len[None, :], 0), axis=1)
    live_counts = jnp.sum(jnp.where(match_user, cand_count[None, :], 0), axis=1)
    column = lax.dynamic_index_in_dim(
        tile_slot.reshape(user_total, per_hist, hist_count), hist_index, axis=2, keepdims=False
    )
    codes = column.reshape(-1)
    owners = codes // slots_own
    local_slot = codes % slots_own
    dests = jnp.repeat(jnp.arange(user_total) // users_here, per_hist)
    entry_ids = jnp.arange(codes.shape[0])
    same_pair = (
        (owners[:, None] == owners[None, :])
        & (dests[:, None] == dests[None, :])
        & (entry_ids[:, None] > entry_ids[None, :])
    )
    places = jnp.sum(jnp.where(same_pair, 1, 0), axis=1)
    picked = (
        (owners[None, None, :] == req_index)
        & (dests[None, None, :] == jnp.arange(req_count)[:, None, None])
        & (places[None, None, :] == jnp.arange(capacity)[None, :, None])
    )
    source_slot = jnp.sum(jnp.where(picked, local_slot[None, None, :], 0), axis=2).reshape(-1)
    first_entry = first_slot * per_hist
    my_owner = lax.dynamic_slice_in_dim(owners, first_entry, users_here * per_hist)
    my_place = lax.dynamic_slice_in_dim(places, first_entry, users_here * per_hist)
    picked_slot = (my_owner * capacity + my_place).astype(jnp.int32)
    sub = tile_len // 2
    halves = []
    for half in range(2):
        kv_half = lax.slice_in_dim(kv_cache, half * sub, (half + 1) * sub, axis=1)
        outgoing = kv_half.at[source_slot].get(mode="promise_in_bounds")
        outgoing = outgoing.reshape(req_count, capacity, sub, 2 * width)
        if half == 0:
            incoming = lax.all_to_all(outgoing, "req", split_axis=0, concat_axis=0, tiled=True)
        else:
            incoming = req_a2a(outgoing, 0)
        halves.append(incoming.reshape(req_count * capacity, sub, 2 * width))
    normed = layer_norm(cand_x.astype(jnp.float32)).astype(jnp.bfloat16)
    mixed_in = jnp.dot(normed.reshape(-1, width), w_uvqk, preferred_element_type=jnp.float32)
    projected = jax.nn.silu(mixed_in).astype(jnp.bfloat16).reshape(users_here, cand_rows, 4, width)
    u_gate = projected[:, :, 0]
    v_self = projected[:, :, 1]
    queries = projected[:, :, 2]
    k_self = projected[:, :, 3]
    my_user = hist_index // heads
    my_length = lax.dynamic_slice_in_dim(lengths, my_user, 1)
    q_row = 2 * per_hist * sub
    packed_a = lax.all_to_all(
        pack_for_heads(picked_slot, halves[0], queries, users_here, heads),
        "hist", split_axis=0, concat_axis=0, tiled=True,
    )
    history_mine = attend(my_length, packed_a, packed_a, q_row, sub, tile_len, 0, score_scale)
    packed_b = lax.all_to_all(
        pack_for_heads(picked_slot, halves[1], None, users_here, heads),
        "hist", split_axis=0, concat_axis=0, tiled=True,
    )
    history_mine = history_mine + attend(my_length, packed_b, packed_a, q_row, sub, tile_len, sub, score_scale)
    history_back = lax.all_to_all(
        history_mine.reshape(hist_count, cand_rows, head_dim), "hist", split_axis=0, concat_axis=0, tiled=True
    )
    combined = history_back.reshape(users_here, heads, cand_rows, head_dim).transpose(0, 2, 1, 3)
    query_wide = queries.astype(jnp.float32).reshape(users_here, cand_rows, heads, head_dim)
    key_wide = k_self.astype(jnp.float32).reshape(users_here, cand_rows, heads, head_dim)
    value_wide = v_self.astype(jnp.float32).reshape(users_here, cand_rows, heads, head_dim)
    self_scores = jnp.sum(query_wide * key_wide, axis=-1) * score_scale + self_bias
    own_term = jax.nn.silu(self_scores)[..., None] * value_wide
    divisor = (lengths + 1).astype(jnp.float32)[:, None, None, None]
    attended = (combined + own_term) / divisor
    gated = (
        layer_norm(attended.reshape(users_here, cand_rows, width)) * u_gate.astype(jnp.float32)
    ).astype(jnp.bfloat16)
    update = jnp.dot(gated.reshape(-1, width), w_out, preferred_element_type=jnp.float32)
    result = cand_x.astype(jnp.float32) + update.reshape(users_here, cand_rows, width)
    cand_index = hist_index * cand_rows + jnp.arange(cand_rows)
    live_rows = cand_index[None, :] < live_counts[:, None]
    return jnp.where(live_rows[:, :, None], result, 0.0).astype(jnp.bfloat16)


def solution(mesh):
    return jax.shard_map(
        local,
        mesh=mesh,
        in_specs=(
            P("req", "hist", None),
            P(("req", "hist"), None, None),
            P(),
            P(),
            P(),
            P(),
            P(),
            P(),
            P(),
        ),
        out_specs=P("req", "hist", None),
        check_vma=False,
    )
```

```python
import functools
import math

import jax
import jax.numpy as jnp
from jax import lax
from jax.experimental import pallas as pl
from jax.experimental.pallas import tpu as pltpu
from jax.sharding import PartitionSpec as P


def layer_norm(values):
    mean_value = jnp.mean(values, axis=-1, keepdims=True)
    centred = values - mean_value
    spread = jnp.mean(centred * centred, axis=-1, keepdims=True)
    return centred * lax.rsqrt(spread + 1e-05)


def silu_tanh(values):
    return values * (0.5 + 0.5 * jnp.tanh(0.5 * values))


def req_a2a_kernel(send_ref, recv_ref, send_sem, recv_sem, local_sem, *, axis, other_axis):
    n = send_ref.shape[0]
    me = lax.axis_index(axis)
    other = lax.axis_index(other_axis)
    barrier = pltpu.get_barrier_semaphore()
    for k in range(1, n):
        peer = lax.rem(me + k, n)
        pl.semaphore_signal(
            barrier, inc=1, device_id={axis: peer, other_axis: other}, device_id_type=pl.DeviceIdType.MESH
        )
    pl.semaphore_wait(barrier, n - 1)
    copies = []
    for k in range(1, n):
        peer = lax.rem(me + k, n)
        copy = pltpu.make_async_remote_copy(
            src_ref=send_ref.at[peer],
            dst_ref=recv_ref.at[me],
            send_sem=send_sem.at[k],
            recv_sem=recv_sem.at[k],
            device_id={axis: peer, other_axis: other},
            device_id_type=pl.DeviceIdType.MESH,
        )
        copy.start()
        copies.append(copy)
    own = pltpu.make_async_copy(send_ref.at[me], recv_ref.at[me], local_sem)
    own.start()
    own.wait()
    for copy in copies:
        copy.wait_send()
    for k in range(1, n):
        src = lax.rem(me + n - k, n)
        pltpu.make_async_remote_copy(
            src_ref=send_ref.at[src],
            dst_ref=recv_ref.at[src],
            send_sem=send_sem.at[k],
            recv_sem=recv_sem.at[k],
            device_id={axis: src, other_axis: other},
            device_id_type=pl.DeviceIdType.MESH,
        ).wait_recv()


def req_a2a(x, collective_id):
    n = x.shape[0]
    return pl.pallas_call(
        functools.partial(req_a2a_kernel, axis="req", other_axis="hist"),
        out_shape=jax.ShapeDtypeStruct(x.shape, x.dtype),
        in_specs=[pl.BlockSpec(memory_space=pl.ANY)],
        out_specs=pl.BlockSpec(memory_space=pl.ANY),
        scratch_shapes=[
            pltpu.SemaphoreType.DMA((n,)),
            pltpu.SemaphoreType.DMA((n,)),
            pltpu.SemaphoreType.DMA(()),
        ],
        compiler_params=pltpu.CompilerParams(collective_id=collective_id, has_side_effects=True),
    )(x)


def attend_kernel(
    len_ref, kv_ref, qsrc_ref, o_ref, q_ref, *, n_tiles, sub, tile_len, offset, q_row, score_scale, chunk
):
    length = len_ref[0]
    n_cls, _, head_dim = kv_ref.shape
    span = n_tiles * sub
    block = q_ref.shape[0] // n_cls
    half_scale = 0.5 * score_scale
    for b in range(n_cls):
        q_ref[pl.ds(b * block, block), :] = qsrc_ref[b, pl.ds(q_row, block), :]
    o_ref[...] = jnp.zeros_like(o_ref)

    def one_class(c, carry):
        key_index = lax.broadcasted_iota(jnp.int32, (1, span), 1)
        position = (c + n_cls * (key_index // sub)) * tile_len + offset + key_index % sub
        live = position < length

        def add_class(masked):
            keys = kv_ref[c, pl.ds(0, span), :]
            values = kv_ref[c, pl.ds(span, span), :]
            for ci in range(q_ref.shape[0] // chunk):
                rows = pl.ds(ci * chunk, chunk)
                scores = lax.dot_general(
                    q_ref[rows, :], keys, (((1,), (1,)), ((), ())), preferred_element_type=jnp.float32
                )
                half = scores * half_scale
                weights = half + half * jnp.tanh(half)
                if masked:
                    weights = jnp.where(live, weights, 0.0)
                o_ref[rows, :] += jnp.dot(weights.astype(jnp.bfloat16), values, preferred_element_type=jnp.float32)

        last_key = (c + n_cls * (n_tiles - 1)) * tile_len + offset + sub
        whole = last_key <= length
        pl.when(whole)(lambda: add_class(False))
        pl.when(jnp.logical_and(jnp.logical_not(whole), c * tile_len + offset < length))(lambda: add_class(True))
        return carry

    lax.fori_loop(0, n_cls, one_class, 0)


def attend(length, kv_packed, q_packed, q_row, sub, tile_len, offset, score_scale):
    n_cls, _, head_dim = q_packed.shape
    rows = n_cls * (q_packed.shape[1] - q_row)
    chunk = 2048
    kernel = functools.partial(
        attend_kernel,
        n_tiles=q_row // (2 * sub),
        sub=sub,
        tile_len=tile_len,
        offset=offset,
        q_row=q_row,
        score_scale=score_scale,
        chunk=chunk,
    )
    return pl.pallas_call(
        kernel,
        out_shape=jax.ShapeDtypeStruct((rows, head_dim), jnp.float32),
        in_specs=[
            pl.BlockSpec(memory_space=pltpu.SMEM),
            pl.BlockSpec(memory_space=pltpu.VMEM),
            pl.BlockSpec(memory_space=pltpu.VMEM),
        ],
        out_specs=pl.BlockSpec(memory_space=pltpu.VMEM),
        scratch_shapes=[pltpu.VMEM((rows, head_dim), jnp.bfloat16)],
    )(length, kv_packed, q_packed)


def pack_kernel(picked_ref, tiles_hbm, *rest, heads, users, per_hist, with_q):
    if with_q:
        q_ref, out_ref, staged, in_sem = rest
    else:
        out_ref, staged, in_sem = rest
    width = tiles_hbm.shape[2] // 2
    head_dim = width // heads
    sub = tiles_hbm.shape[1]
    span = per_hist * sub
    n_in = users * per_hist
    reads = []
    for i in range(n_in):
        read = pltpu.make_async_copy(tiles_hbm.at[picked_ref[i]], staged.at[i], in_sem.at[i])
        read.start()
        reads.append(read)
    if with_q:
        cand_rows = q_ref.shape[1]
        for u in range(users):
            for e in range(heads):
                out_ref[u * heads + e, pl.ds(2 * span, cand_rows), :] = q_ref[u, :, pl.ds(e * head_dim, head_dim)]
    for i in range(n_in):
        u, t = divmod(i, per_hist)
        reads[i].wait()
        for piece in range(2 * heads):
            e, kv = divmod(piece, 2)
            out_ref[u * heads + e, pl.ds(kv * span + t * sub, sub), :] = staged[
                i, :, pl.ds(piece * head_dim, head_dim)
            ]


def pack_for_heads(picked_slot, tiles, queries, users, heads):
    n_in = picked_slot.shape[0]
    per_hist = n_in // users
    sub, wide = tiles.shape[1], tiles.shape[2]
    head_dim = wide // (2 * heads)
    rows = 2 * per_hist * sub + (0 if queries is None else queries.shape[1])
    operands = [picked_slot, tiles] + ([] if queries is None else [queries])
    return pl.pallas_call(
        functools.partial(pack_kernel, heads=heads, users=users, per_hist=per_hist, with_q=queries is not None),
        out_shape=jax.ShapeDtypeStruct((users * heads, rows, head_dim), tiles.dtype),
        in_specs=[pl.BlockSpec(memory_space=pltpu.SMEM), pl.BlockSpec(memory_space=pl.ANY)]
        + ([] if queries is None else [pl.BlockSpec(memory_space=pltpu.VMEM)]),
        out_specs=pl.BlockSpec(memory_space=pltpu.VMEM),
        scratch_shapes=[
            pltpu.VMEM((n_in, sub, wide), tiles.dtype),
            pltpu.SemaphoreType.DMA((n_in,)),
        ],
    )(*operands)


def finish_kernel(
    bias_ref, len_ref, limit_ref, hist_ref, proj_ref, x_ref, w_ref, out_ref, att_ref, *, heads, score_scale
):
    users, rows, width = x_ref.shape
    head_dim = width // heads
    for u in range(users):
        divisor = (len_ref[u] + 1).astype(jnp.float32)
        for e in range(heads):
            value = proj_ref[u, :, pl.ds(width + e * head_dim, head_dim)].astype(jnp.float32)
            query = proj_ref[u, :, pl.ds(2 * width + e * head_dim, head_dim)].astype(jnp.float32)
            key = proj_ref[u, :, pl.ds(3 * width + e * head_dim, head_dim)].astype(jnp.float32)
            self_score = jnp.sum(query * key, axis=-1, keepdims=True) * score_scale + bias_ref[e]
            own = self_score * (0.5 + 0.5 * jnp.tanh(0.5 * self_score)) * value
            att_ref[:, pl.ds(e * head_dim, head_dim)] = (hist_ref[u * heads + e] + own) / divisor
        attended = att_ref[...]
        centred = attended - jnp.mean(attended, axis=-1, keepdims=True)
        spread = jnp.mean(centred * centred, axis=-1, keepdims=True)
        gate = proj_ref[u, :, pl.ds(0, width)].astype(jnp.float32)
        gated = (centred * lax.rsqrt(spread + 1e-05) * gate).astype(jnp.bfloat16)
        result = x_ref[u].astype(jnp.float32) + jnp.dot(gated, w_ref[...], preferred_element_type=jnp.float32)
        row = lax.broadcasted_iota(jnp.int32, (rows, 1), 0)
        out_ref[u] = jnp.where(row < limit_ref[u], result, 0.0).astype(out_ref.dtype)


def finish(history_back, projected, cand_x, w_out, self_bias, lengths, row_limit, heads, score_scale):
    users, rows, width = cand_x.shape
    smem = pl.BlockSpec(memory_space=pltpu.SMEM)
    vmem = pl.BlockSpec(memory_space=pltpu.VMEM)
    return pl.pallas_call(
        functools.partial(finish_kernel, heads=heads, score_scale=score_scale),
        out_shape=jax.ShapeDtypeStruct(cand_x.shape, cand_x.dtype),
        in_specs=[smem, smem, smem, vmem, vmem, vmem, vmem],
        out_specs=vmem,
        scratch_shapes=[pltpu.VMEM((rows, width), jnp.float32)],
    )(self_bias, lengths, row_limit, history_back, projected, cand_x, w_out)


def local(cand_x, kv_cache, w_uvqk, w_out, self_bias, user_rank, hist_len, cand_count, tile_slot):
    users_here, cand_rows, width = cand_x.shape
    heads = self_bias.shape[0]
    head_dim = width // heads
    score_scale = 1.0 / math.sqrt(head_dim)
    slots_own, tile_len, _ = kv_cache.shape
    user_total, tiles_max = tile_slot.shape
    req_count = lax.axis_size("req")
    hist_count = lax.axis_size("hist")
    req_index = lax.axis_index("req")
    hist_index = lax.axis_index("hist")
    per_hist = tiles_max // hist_count
    capacity = slots_own // req_count + 1
    first_slot = req_index * users_here
    user_ids = lax.dynamic_slice_in_dim(user_rank, first_slot, users_here)
    match_user = user_ids[:, None] == jnp.arange(user_total)[None, :]
    lengths = jnp.sum(jnp.where(match_user, hist_len[None, :], 0), axis=1)
    live_counts = jnp.sum(jnp.where(match_user, cand_count[None, :], 0), axis=1)
    column = lax.dynamic_index_in_dim(
        tile_slot.reshape(user_total, per_hist, hist_count), hist_index, axis=2, keepdims=False
    )
    codes = column.reshape(-1)
    owners = codes // slots_own
    local_slot = codes % slots_own
    dests = jnp.repeat(jnp.arange(user_total) // users_here, per_hist)
    entry_ids = jnp.arange(codes.shape[0])
    same_pair = (
        (owners[:, None] == owners[None, :])
        & (dests[:, None] == dests[None, :])
        & (entry_ids[:, None] > entry_ids[None, :])
    )
    places = jnp.sum(jnp.where(same_pair, 1, 0), axis=1)
    picked = (
        (owners[None, None, :] == req_index)
        & (dests[None, None, :] == jnp.arange(req_count)[:, None, None])
        & (places[None, None, :] == jnp.arange(capacity)[None, :, None])
    )
    source_slot = jnp.sum(jnp.where(picked, local_slot[None, None, :], 0), axis=2).reshape(-1)
    first_entry = first_slot * per_hist
    my_owner = lax.dynamic_slice_in_dim(owners, first_entry, users_here * per_hist)
    my_place = lax.dynamic_slice_in_dim(places, first_entry, users_here * per_hist)
    picked_slot = (my_owner * capacity + my_place).astype(jnp.int32)
    sub = tile_len // 2
    halves = []
    for half in range(2):
        kv_half = lax.slice_in_dim(kv_cache, half * sub, (half + 1) * sub, axis=1)
        outgoing = kv_half.at[source_slot].get(mode="promise_in_bounds")
        outgoing = outgoing.reshape(req_count, capacity, sub, 2 * width)
        if half == 0:
            incoming = lax.all_to_all(outgoing, "req", split_axis=0, concat_axis=0, tiled=True)
        else:
            incoming = req_a2a(outgoing, 0)
        halves.append(incoming.reshape(req_count * capacity, sub, 2 * width))
    normed = layer_norm(cand_x.astype(jnp.float32)).astype(jnp.bfloat16)
    mixed_in = jnp.dot(normed.reshape(-1, width), w_uvqk, preferred_element_type=jnp.float32)
    projected = jax.nn.silu(mixed_in).astype(jnp.bfloat16).reshape(users_here, cand_rows, 4, width)
    u_gate = projected[:, :, 0]
    v_self = projected[:, :, 1]
    queries = projected[:, :, 2]
    k_self = projected[:, :, 3]
    my_user = hist_index // heads
    my_length = lax.dynamic_slice_in_dim(lengths, my_user, 1)
    q_row = 2 * per_hist * sub
    packed_a = lax.all_to_all(
        pack_for_heads(picked_slot, halves[0], queries, users_here, heads),
        "hist", split_axis=0, concat_axis=0, tiled=True,
    )
    history_mine = attend(my_length, packed_a, packed_a, q_row, sub, tile_len, 0, score_scale)
    packed_b = lax.all_to_all(
        pack_for_heads(picked_slot, halves[1], None, users_here, heads),
        "hist", split_axis=0, concat_axis=0, tiled=True,
    )
    history_mine = history_mine + attend(my_length, packed_b, packed_a, q_row, sub, tile_len, sub, score_scale)
    history_back = lax.all_to_all(
        history_mine.reshape(hist_count, cand_rows, head_dim), "hist", split_axis=0, concat_axis=0, tiled=True
    )
    row_limit = (live_counts - hist_index * cand_rows).astype(jnp.int32)
    return finish(
        history_back, projected.reshape(users_here, cand_rows, 4 * width), cand_x, w_out, self_bias,
        lengths.astype(jnp.int32), row_limit, heads, score_scale,
    )


def solution(mesh):
    return jax.shard_map(
        local,
        mesh=mesh,
        in_specs=(
            P("req", "hist", None),
            P(("req", "hist"), None, None),
            P(),
            P(),
            P(),
            P(),
            P(),
            P(),
            P(),
        ),
        out_specs=P("req", "hist", None),
        check_vma=False,
    )
```

```python
import functools
import math

import jax
import jax.numpy as jnp
from jax import lax
from jax.experimental import pallas as pl
from jax.experimental.pallas import tpu as pltpu
from jax.sharding import PartitionSpec as P


def layer_norm(values):
    mean_value = jnp.mean(values, axis=-1, keepdims=True)
    centred = values - mean_value
    spread = jnp.mean(centred * centred, axis=-1, keepdims=True)
    return centred * lax.rsqrt(spread + 1e-05)


def silu_tanh(values):
    return values * (0.5 + 0.5 * jnp.tanh(0.5 * values))


def req_a2a_kernel(send_ref, recv_ref, send_sem, recv_sem, local_sem, *, axis, other_axis):
    n = send_ref.shape[0]
    me = lax.axis_index(axis)
    other = lax.axis_index(other_axis)
    barrier = pltpu.get_barrier_semaphore()
    for k in range(1, n):
        peer = lax.rem(me + k, n)
        pl.semaphore_signal(
            barrier, inc=1, device_id={axis: peer, other_axis: other}, device_id_type=pl.DeviceIdType.MESH
        )
    pl.semaphore_wait(barrier, n - 1)
    copies = []
    for k in range(1, n):
        peer = lax.rem(me + k, n)
        copy = pltpu.make_async_remote_copy(
            src_ref=send_ref.at[peer],
            dst_ref=recv_ref.at[me],
            send_sem=send_sem.at[k],
            recv_sem=recv_sem.at[k],
            device_id={axis: peer, other_axis: other},
            device_id_type=pl.DeviceIdType.MESH,
        )
        copy.start()
        copies.append(copy)
    own = pltpu.make_async_copy(send_ref.at[me], recv_ref.at[me], local_sem)
    own.start()
    own.wait()
    for copy in copies:
        copy.wait_send()
    for k in range(1, n):
        src = lax.rem(me + n - k, n)
        pltpu.make_async_remote_copy(
            src_ref=send_ref.at[src],
            dst_ref=recv_ref.at[src],
            send_sem=send_sem.at[k],
            recv_sem=recv_sem.at[k],
            device_id={axis: src, other_axis: other},
            device_id_type=pl.DeviceIdType.MESH,
        ).wait_recv()


def req_a2a(x, collective_id):
    n = x.shape[0]
    return pl.pallas_call(
        functools.partial(req_a2a_kernel, axis="req", other_axis="hist"),
        out_shape=jax.ShapeDtypeStruct(x.shape, x.dtype),
        in_specs=[pl.BlockSpec(memory_space=pl.ANY)],
        out_specs=pl.BlockSpec(memory_space=pl.ANY),
        scratch_shapes=[
            pltpu.SemaphoreType.DMA((n,)),
            pltpu.SemaphoreType.DMA((n,)),
            pltpu.SemaphoreType.DMA(()),
        ],
        compiler_params=pltpu.CompilerParams(collective_id=collective_id, has_side_effects=True),
    )(x)


def attend_kernel(len_ref, kv_ref, qsrc_ref, *rest, n_tiles, sub, tile_len, offset, q_row, score_scale, chunk):
    if len(rest) == 3:
        init_ref, o_ref, q_ref = rest
    else:
        init_ref = None
        o_ref, q_ref = rest
    length = len_ref[0]
    n_cls, _, head_dim = kv_ref.shape
    span = n_tiles * sub
    block = q_ref.shape[0] // n_cls
    half_scale = 0.5 * score_scale
    for b in range(n_cls):
        q_ref[pl.ds(b * block, block), :] = qsrc_ref[b, pl.ds(q_row, block), :]
    if init_ref is None:
        o_ref[...] = jnp.zeros_like(o_ref)
    else:
        o_ref[...] = init_ref[...]

    def one_class(c, carry):
        key_index = lax.broadcasted_iota(jnp.int32, (1, span), 1)
        position = (c + n_cls * (key_index // sub)) * tile_len + offset + key_index % sub
        live = position < length

        def add_class(masked):
            keys = kv_ref[c, pl.ds(0, span), :]
            values = kv_ref[c, pl.ds(span, span), :]
            for ci in range(q_ref.shape[0] // chunk):
                rows = pl.ds(ci * chunk, chunk)
                scores = lax.dot_general(
                    q_ref[rows, :], keys, (((1,), (1,)), ((), ())), preferred_element_type=jnp.float32
                )
                half = scores * half_scale
                weights = half + half * jnp.tanh(half)
                if masked:
                    weights = jnp.where(live, weights, 0.0)
                o_ref[rows, :] += jnp.dot(weights.astype(jnp.bfloat16), values, preferred_element_type=jnp.float32)

        last_key = (c + n_cls * (n_tiles - 1)) * tile_len + offset + sub
        whole = last_key <= length
        pl.when(whole)(lambda: add_class(False))
        pl.when(jnp.logical_and(jnp.logical_not(whole), c * tile_len + offset < length))(lambda: add_class(True))
        return carry

    lax.fori_loop(0, n_cls, one_class, 0)


def attend(length, kv_packed, q_packed, q_row, n_tiles, sub, tile_len, offset, score_scale, init=None):
    n_cls, _, head_dim = q_packed.shape
    rows = n_cls * (q_packed.shape[1] - q_row)
    chunk = 2048
    kernel = functools.partial(
        attend_kernel,
        n_tiles=n_tiles,
        sub=sub,
        tile_len=tile_len,
        offset=offset,
        q_row=q_row,
        score_scale=score_scale,
        chunk=chunk,
    )
    return pl.pallas_call(
        kernel,
        out_shape=jax.ShapeDtypeStruct((rows, head_dim), jnp.float32),
        in_specs=[pl.BlockSpec(memory_space=pltpu.SMEM)]
        + [pl.BlockSpec(memory_space=pltpu.VMEM)] * (2 if init is None else 3),
        out_specs=pl.BlockSpec(memory_space=pltpu.VMEM),
        scratch_shapes=[pltpu.VMEM((rows, head_dim), jnp.bfloat16)],
    )(length, kv_packed, q_packed, *([] if init is None else [init]))


def pack_kernel(picked_ref, tiles_hbm, *rest, heads, users, per_hist, with_q):
    if with_q:
        q_ref, out_ref, staged, in_sem = rest
    else:
        out_ref, staged, in_sem = rest
    width = tiles_hbm.shape[2] // 2
    head_dim = width // heads
    sub = tiles_hbm.shape[1]
    span = per_hist * sub
    n_in = users * per_hist
    reads = []
    for i in range(n_in):
        read = pltpu.make_async_copy(tiles_hbm.at[picked_ref[i]], staged.at[i], in_sem.at[i])
        read.start()
        reads.append(read)
    if with_q:
        cand_rows = q_ref.shape[1]
        for u in range(users):
            for e in range(heads):
                out_ref[u * heads + e, pl.ds(2 * span, cand_rows), :] = q_ref[u, :, pl.ds(e * head_dim, head_dim)]
    for i in range(n_in):
        u, t = divmod(i, per_hist)
        reads[i].wait()
        for piece in range(2 * heads):
            e, kv = divmod(piece, 2)
            out_ref[u * heads + e, pl.ds(kv * span + t * sub, sub), :] = staged[
                i, :, pl.ds(piece * head_dim, head_dim)
            ]


def pack_for_heads(picked_slot, tiles, queries, users, heads):
    n_in = picked_slot.shape[0]
    per_hist = n_in // users
    sub, wide = tiles.shape[1], tiles.shape[2]
    head_dim = wide // (2 * heads)
    rows = 2 * per_hist * sub + (0 if queries is None else queries.shape[1])
    operands = [picked_slot, tiles] + ([] if queries is None else [queries])
    return pl.pallas_call(
        functools.partial(pack_kernel, heads=heads, users=users, per_hist=per_hist, with_q=queries is not None),
        out_shape=jax.ShapeDtypeStruct((users * heads, rows, head_dim), tiles.dtype),
        in_specs=[pl.BlockSpec(memory_space=pltpu.SMEM), pl.BlockSpec(memory_space=pl.ANY)]
        + ([] if queries is None else [pl.BlockSpec(memory_space=pltpu.VMEM)]),
        out_specs=pl.BlockSpec(memory_space=pltpu.VMEM),
        scratch_shapes=[
            pltpu.VMEM((n_in, sub, wide), tiles.dtype),
            pltpu.SemaphoreType.DMA((n_in,)),
        ],
    )(*operands)


def finish_kernel(
    bias_ref, len_ref, limit_ref, hist_ref, proj_ref, x_ref, w_ref, out_ref, att_ref, *, heads, score_scale
):
    users, rows, width = x_ref.shape
    head_dim = width // heads
    for u in range(users):
        divisor = (len_ref[u] + 1).astype(jnp.float32)
        for e in range(heads):
            value = proj_ref[u, :, pl.ds(width + e * head_dim, head_dim)].astype(jnp.float32)
            query = proj_ref[u, :, pl.ds(2 * width + e * head_dim, head_dim)].astype(jnp.float32)
            key = proj_ref[u, :, pl.ds(3 * width + e * head_dim, head_dim)].astype(jnp.float32)
            self_score = jnp.sum(query * key, axis=-1, keepdims=True) * score_scale + bias_ref[e]
            own = self_score * (0.5 + 0.5 * jnp.tanh(0.5 * self_score)) * value
            att_ref[:, pl.ds(e * head_dim, head_dim)] = (hist_ref[u * heads + e] + own) / divisor
        attended = att_ref[...]
        centred = attended - jnp.mean(attended, axis=-1, keepdims=True)
        spread = jnp.mean(centred * centred, axis=-1, keepdims=True)
        gate = proj_ref[u, :, pl.ds(0, width)].astype(jnp.float32)
        gated = (centred * lax.rsqrt(spread + 1e-05) * gate).astype(jnp.bfloat16)
        result = x_ref[u].astype(jnp.float32) + jnp.dot(gated, w_ref[...], preferred_element_type=jnp.float32)
        row = lax.broadcasted_iota(jnp.int32, (rows, 1), 0)
        out_ref[u] = jnp.where(row < limit_ref[u], result, 0.0).astype(out_ref.dtype)


def finish(history_back, projected, cand_x, w_out, self_bias, lengths, row_limit, heads, score_scale):
    users, rows, width = cand_x.shape
    smem = pl.BlockSpec(memory_space=pltpu.SMEM)
    vmem = pl.BlockSpec(memory_space=pltpu.VMEM)
    return pl.pallas_call(
        functools.partial(finish_kernel, heads=heads, score_scale=score_scale),
        out_shape=jax.ShapeDtypeStruct(cand_x.shape, cand_x.dtype),
        in_specs=[smem, smem, smem, vmem, vmem, vmem, vmem],
        out_specs=vmem,
        scratch_shapes=[pltpu.VMEM((rows, width), jnp.float32)],
    )(self_bias, lengths, row_limit, history_back, projected, cand_x, w_out)


def local(cand_x, kv_cache, w_uvqk, w_out, self_bias, user_rank, hist_len, cand_count, tile_slot):
    users_here, cand_rows, width = cand_x.shape
    heads = self_bias.shape[0]
    head_dim = width // heads
    score_scale = 1.0 / math.sqrt(head_dim)
    slots_own, tile_len, _ = kv_cache.shape
    user_total, tiles_max = tile_slot.shape
    req_count = lax.axis_size("req")
    hist_count = lax.axis_size("hist")
    req_index = lax.axis_index("req")
    hist_index = lax.axis_index("hist")
    per_hist = tiles_max // hist_count
    capacity = slots_own // req_count + 1
    first_slot = req_index * users_here
    user_ids = lax.dynamic_slice_in_dim(user_rank, first_slot, users_here)
    match_user = user_ids[:, None] == jnp.arange(user_total)[None, :]
    lengths = jnp.sum(jnp.where(match_user, hist_len[None, :], 0), axis=1)
    live_counts = jnp.sum(jnp.where(match_user, cand_count[None, :], 0), axis=1)
    column = lax.dynamic_index_in_dim(
        tile_slot.reshape(user_total, per_hist, hist_count), hist_index, axis=2, keepdims=False
    )
    codes = column.reshape(-1)
    owners = codes // slots_own
    local_slot = codes % slots_own
    dests = jnp.repeat(jnp.arange(user_total) // users_here, per_hist)
    entry_ids = jnp.arange(codes.shape[0])
    same_pair = (
        (owners[:, None] == owners[None, :])
        & (dests[:, None] == dests[None, :])
        & (entry_ids[:, None] > entry_ids[None, :])
    )
    places = jnp.sum(jnp.where(same_pair, 1, 0), axis=1)
    picked = (
        (owners[None, None, :] == req_index)
        & (dests[None, None, :] == jnp.arange(req_count)[:, None, None])
        & (places[None, None, :] == jnp.arange(capacity)[None, :, None])
    )
    source_slot = jnp.sum(jnp.where(picked, local_slot[None, None, :], 0), axis=2).reshape(-1)
    first_entry = first_slot * per_hist
    my_owner = lax.dynamic_slice_in_dim(owners, first_entry, users_here * per_hist)
    my_place = lax.dynamic_slice_in_dim(places, first_entry, users_here * per_hist)
    picked_slot = (my_owner * capacity + my_place).astype(jnp.int32)
    first_len = tile_len - tile_len // 4
    bounds = [(0, first_len), (first_len, tile_len)]
    halves = []
    for half, (lo, hi) in enumerate(bounds):
        kv_half = lax.slice_in_dim(kv_cache, lo, hi, axis=1)
        outgoing = kv_half.at[source_slot].get(mode="promise_in_bounds")
        outgoing = outgoing.reshape(req_count, capacity, hi - lo, 2 * width)
        if half == 0:
            incoming = lax.all_to_all(outgoing, "req", split_axis=0, concat_axis=0, tiled=True)
        else:
            incoming = req_a2a(outgoing, 0)
        halves.append(incoming.reshape(req_count * capacity, hi - lo, 2 * width))
    normed = layer_norm(cand_x.astype(jnp.float32)).astype(jnp.bfloat16)
    mixed_in = jnp.dot(normed.reshape(-1, width), w_uvqk, preferred_element_type=jnp.float32)
    projected = jax.nn.silu(mixed_in).astype(jnp.bfloat16).reshape(users_here, cand_rows, 4, width)
    u_gate = projected[:, :, 0]
    v_self = projected[:, :, 1]
    queries = projected[:, :, 2]
    k_self = projected[:, :, 3]
    my_user = hist_index // heads
    my_length = lax.dynamic_slice_in_dim(lengths, my_user, 1)
    q_row = 2 * per_hist * first_len
    packed_a = lax.all_to_all(
        pack_for_heads(picked_slot, halves[0], queries, users_here, heads),
        "hist", split_axis=0, concat_axis=0, tiled=True,
    )
    history_mine = attend(my_length, packed_a, packed_a, q_row, per_hist, first_len, tile_len, 0, score_scale)
    packed_b = lax.all_to_all(
        pack_for_heads(picked_slot, halves[1], None, users_here, heads),
        "hist", split_axis=0, concat_axis=0, tiled=True,
    )
    history_mine = attend(
        my_length, packed_b, packed_a, q_row, per_hist, tile_len - first_len, tile_len, first_len, score_scale,
        init=history_mine,
    )
    history_back = lax.all_to_all(
        history_mine.reshape(hist_count, cand_rows, head_dim), "hist", split_axis=0, concat_axis=0, tiled=True
    )
    row_limit = (live_counts - hist_index * cand_rows).astype(jnp.int32)
    return finish(
        history_back, projected.reshape(users_here, cand_rows, 4 * width), cand_x, w_out, self_bias,
        lengths.astype(jnp.int32), row_limit, heads, score_scale,
    )


def solution(mesh):
    return jax.shard_map(
        local,
        mesh=mesh,
        in_specs=(
            P("req", "hist", None),
            P(("req", "hist"), None, None),
            P(),
            P(),
            P(),
            P(),
            P(),
            P(),
            P(),
        ),
        out_specs=P("req", "hist", None),
        check_vma=False,
    )
```

```python
import functools
import math

import jax
import jax.numpy as jnp
from jax import lax
from jax.experimental import pallas as pl
from jax.experimental.pallas import tpu as pltpu
from jax.sharding import PartitionSpec as P


def layer_norm(values):
    mean_value = jnp.mean(values, axis=-1, keepdims=True)
    centred = values - mean_value
    spread = jnp.mean(centred * centred, axis=-1, keepdims=True)
    return centred * lax.rsqrt(spread + 1e-05)


def silu_tanh(values):
    return values * (0.5 + 0.5 * jnp.tanh(0.5 * values))


def req_a2a_kernel(send_ref, recv_ref, send_sem, recv_sem, local_sem, *, axis, other_axis):
    n = send_ref.shape[0]
    me = lax.axis_index(axis)
    other = lax.axis_index(other_axis)
    barrier = pltpu.get_barrier_semaphore()
    for k in range(1, n):
        peer = lax.rem(me + k, n)
        pl.semaphore_signal(
            barrier, inc=1, device_id={axis: peer, other_axis: other}, device_id_type=pl.DeviceIdType.MESH
        )
    pl.semaphore_wait(barrier, n - 1)
    copies = []
    for k in range(1, n):
        peer = lax.rem(me + k, n)
        copy = pltpu.make_async_remote_copy(
            src_ref=send_ref.at[peer],
            dst_ref=recv_ref.at[me],
            send_sem=send_sem.at[k],
            recv_sem=recv_sem.at[k],
            device_id={axis: peer, other_axis: other},
            device_id_type=pl.DeviceIdType.MESH,
        )
        copy.start()
        copies.append(copy)
    own = pltpu.make_async_copy(send_ref.at[me], recv_ref.at[me], local_sem)
    own.start()
    own.wait()
    for copy in copies:
        copy.wait_send()
    for k in range(1, n):
        src = lax.rem(me + n - k, n)
        pltpu.make_async_remote_copy(
            src_ref=send_ref.at[src],
            dst_ref=recv_ref.at[src],
            send_sem=send_sem.at[k],
            recv_sem=recv_sem.at[k],
            device_id={axis: src, other_axis: other},
            device_id_type=pl.DeviceIdType.MESH,
        ).wait_recv()


def req_a2a(x, collective_id):
    n = x.shape[0]
    return pl.pallas_call(
        functools.partial(req_a2a_kernel, axis="req", other_axis="hist"),
        out_shape=jax.ShapeDtypeStruct(x.shape, x.dtype),
        in_specs=[pl.BlockSpec(memory_space=pl.ANY)],
        out_specs=pl.BlockSpec(memory_space=pl.ANY),
        scratch_shapes=[
            pltpu.SemaphoreType.DMA((n,)),
            pltpu.SemaphoreType.DMA((n,)),
            pltpu.SemaphoreType.DMA(()),
        ],
        compiler_params=pltpu.CompilerParams(collective_id=collective_id, has_side_effects=True),
    )(x)


def attend_kernel(len_ref, kv_ref, qsrc_ref, *rest, n_tiles, sub, tile_len, offset, q_row, score_scale, chunk):
    if len(rest) == 3:
        init_ref, o_ref, q_ref = rest
    else:
        init_ref = None
        o_ref, q_ref = rest
    length = len_ref[0]
    n_cls, _, head_dim = kv_ref.shape
    span = n_tiles * sub
    block = q_ref.shape[0] // n_cls
    half_scale = 0.5 * score_scale
    for b in range(n_cls):
        q_ref[pl.ds(b * block, block), :] = qsrc_ref[b, pl.ds(q_row, block), :]
    if init_ref is None:
        o_ref[...] = jnp.zeros_like(o_ref)
    else:
        o_ref[...] = init_ref[...]

    def one_class(c, carry):
        key_index = lax.broadcasted_iota(jnp.int32, (1, span), 1)
        position = (c + n_cls * (key_index // sub)) * tile_len + offset + key_index % sub
        live = position < length

        def add_class(masked):
            keys = kv_ref[c, pl.ds(0, span), :]
            values = kv_ref[c, pl.ds(span, span), :]
            for ci in range(q_ref.shape[0] // chunk):
                rows = pl.ds(ci * chunk, chunk)
                scores = lax.dot_general(
                    q_ref[rows, :], keys, (((1,), (1,)), ((), ())), preferred_element_type=jnp.float32
                )
                half = scores * half_scale
                weights = half + half * jnp.tanh(half)
                if masked:
                    weights = jnp.where(live, weights, 0.0)
                o_ref[rows, :] += jnp.dot(weights.astype(jnp.bfloat16), values, preferred_element_type=jnp.float32)

        last_key = (c + n_cls * (n_tiles - 1)) * tile_len + offset + sub
        whole = last_key <= length
        pl.when(whole)(lambda: add_class(False))
        pl.when(jnp.logical_and(jnp.logical_not(whole), c * tile_len + offset < length))(lambda: add_class(True))
        return carry

    lax.fori_loop(0, n_cls, one_class, 0)


def attend(length, kv_packed, q_packed, q_row, n_tiles, sub, tile_len, offset, score_scale, init=None):
    n_cls, _, head_dim = q_packed.shape
    rows = n_cls * (q_packed.shape[1] - q_row)
    chunk = 2048
    kernel = functools.partial(
        attend_kernel,
        n_tiles=n_tiles,
        sub=sub,
        tile_len=tile_len,
        offset=offset,
        q_row=q_row,
        score_scale=score_scale,
        chunk=chunk,
    )
    return pl.pallas_call(
        kernel,
        out_shape=jax.ShapeDtypeStruct((rows, head_dim), jnp.float32),
        in_specs=[pl.BlockSpec(memory_space=pltpu.SMEM)]
        + [pl.BlockSpec(memory_space=pltpu.VMEM)] * (2 if init is None else 3),
        out_specs=pl.BlockSpec(memory_space=pltpu.VMEM),
        scratch_shapes=[pltpu.VMEM((rows, head_dim), jnp.bfloat16)],
    )(length, kv_packed, q_packed, *([] if init is None else [init]))


def pack_kernel(picked_ref, tiles_hbm, *rest, heads, users, per_hist, with_q):
    if with_q:
        q_ref, out_ref, staged, in_sem = rest
    else:
        out_ref, staged, in_sem = rest
    width = tiles_hbm.shape[2] // 2
    head_dim = width // heads
    sub = tiles_hbm.shape[1]
    span = per_hist * sub
    n_in = users * per_hist
    reads = []
    for i in range(n_in):
        read = pltpu.make_async_copy(tiles_hbm.at[picked_ref[i]], staged.at[i], in_sem.at[i])
        read.start()
        reads.append(read)
    if with_q:
        cand_rows = q_ref.shape[1]
        for u in range(users):
            for e in range(heads):
                out_ref[u * heads + e, pl.ds(2 * span, cand_rows), :] = q_ref[u, :, pl.ds(e * head_dim, head_dim)]
    for i in range(n_in):
        u, t = divmod(i, per_hist)
        reads[i].wait()
        for piece in range(2 * heads):
            e, kv = divmod(piece, 2)
            out_ref[u * heads + e, pl.ds(kv * span + t * sub, sub), :] = staged[
                i, :, pl.ds(piece * head_dim, head_dim)
            ]


def pack_for_heads(picked_slot, tiles, queries, users, heads):
    n_in = picked_slot.shape[0]
    per_hist = n_in // users
    sub, wide = tiles.shape[1], tiles.shape[2]
    head_dim = wide // (2 * heads)
    rows = 2 * per_hist * sub + (0 if queries is None else queries.shape[1])
    operands = [picked_slot, tiles] + ([] if queries is None else [queries])
    return pl.pallas_call(
        functools.partial(pack_kernel, heads=heads, users=users, per_hist=per_hist, with_q=queries is not None),
        out_shape=jax.ShapeDtypeStruct((users * heads, rows, head_dim), tiles.dtype),
        in_specs=[pl.BlockSpec(memory_space=pltpu.SMEM), pl.BlockSpec(memory_space=pl.ANY)]
        + ([] if queries is None else [pl.BlockSpec(memory_space=pltpu.VMEM)]),
        out_specs=pl.BlockSpec(memory_space=pltpu.VMEM),
        scratch_shapes=[
            pltpu.VMEM((n_in, sub, wide), tiles.dtype),
            pltpu.SemaphoreType.DMA((n_in,)),
        ],
    )(*operands)


def finish_kernel(
    bias_ref, len_ref, limit_ref, hist_ref, proj_ref, x_ref, w_ref, out_ref, att_ref, *, heads, score_scale
):
    users, rows, width = x_ref.shape
    head_dim = width // heads
    for u in range(users):
        divisor = (len_ref[u] + 1).astype(jnp.float32)
        for e in range(heads):
            value = proj_ref[u, :, pl.ds(width + e * head_dim, head_dim)].astype(jnp.float32)
            query = proj_ref[u, :, pl.ds(2 * width + e * head_dim, head_dim)].astype(jnp.float32)
            key = proj_ref[u, :, pl.ds(3 * width + e * head_dim, head_dim)].astype(jnp.float32)
            self_score = jnp.sum(query * key, axis=-1, keepdims=True) * score_scale + bias_ref[e]
            own = self_score * (0.5 + 0.5 * jnp.tanh(0.5 * self_score)) * value
            history = hist_ref[u * heads + e].astype(jnp.float32)
            att_ref[:, pl.ds(e * head_dim, head_dim)] = (history + own) / divisor
        attended = att_ref[...]
        centred = attended - jnp.mean(attended, axis=-1, keepdims=True)
        spread = jnp.mean(centred * centred, axis=-1, keepdims=True)
        gate = proj_ref[u, :, pl.ds(0, width)].astype(jnp.float32)
        gated = (centred * lax.rsqrt(spread + 1e-05) * gate).astype(jnp.bfloat16)
        result = x_ref[u].astype(jnp.float32) + jnp.dot(gated, w_ref[...], preferred_element_type=jnp.float32)
        row = lax.broadcasted_iota(jnp.int32, (rows, 1), 0)
        out_ref[u] = jnp.where(row < limit_ref[u], result, 0.0).astype(out_ref.dtype)


def finish(history_back, projected, cand_x, w_out, self_bias, lengths, row_limit, heads, score_scale):
    users, rows, width = cand_x.shape
    smem = pl.BlockSpec(memory_space=pltpu.SMEM)
    vmem = pl.BlockSpec(memory_space=pltpu.VMEM)
    return pl.pallas_call(
        functools.partial(finish_kernel, heads=heads, score_scale=score_scale),
        out_shape=jax.ShapeDtypeStruct(cand_x.shape, cand_x.dtype),
        in_specs=[smem, smem, smem, vmem, vmem, vmem, vmem],
        out_specs=vmem,
        scratch_shapes=[pltpu.VMEM((rows, width), jnp.float32)],
    )(self_bias, lengths, row_limit, history_back, projected, cand_x, w_out)


def local(cand_x, kv_cache, w_uvqk, w_out, self_bias, user_rank, hist_len, cand_count, tile_slot):
    users_here, cand_rows, width = cand_x.shape
    heads = self_bias.shape[0]
    head_dim = width // heads
    score_scale = 1.0 / math.sqrt(head_dim)
    slots_own, tile_len, _ = kv_cache.shape
    user_total, tiles_max = tile_slot.shape
    req_count = lax.axis_size("req")
    hist_count = lax.axis_size("hist")
    req_index = lax.axis_index("req")
    hist_index = lax.axis_index("hist")
    per_hist = tiles_max // hist_count
    capacity = slots_own // req_count + 1
    first_slot = req_index * users_here
    user_ids = lax.dynamic_slice_in_dim(user_rank, first_slot, users_here)
    match_user = user_ids[:, None] == jnp.arange(user_total)[None, :]
    lengths = jnp.sum(jnp.where(match_user, hist_len[None, :], 0), axis=1)
    live_counts = jnp.sum(jnp.where(match_user, cand_count[None, :], 0), axis=1)
    column = lax.dynamic_index_in_dim(
        tile_slot.reshape(user_total, per_hist, hist_count), hist_index, axis=2, keepdims=False
    )
    codes = column.reshape(-1)
    owners = codes // slots_own
    local_slot = codes % slots_own
    dests = jnp.repeat(jnp.arange(user_total) // users_here, per_hist)
    entry_ids = jnp.arange(codes.shape[0])
    same_pair = (
        (owners[:, None] == owners[None, :])
        & (dests[:, None] == dests[None, :])
        & (entry_ids[:, None] > entry_ids[None, :])
    )
    places = jnp.sum(jnp.where(same_pair, 1, 0), axis=1)
    picked = (
        (owners[None, None, :] == req_index)
        & (dests[None, None, :] == jnp.arange(req_count)[:, None, None])
        & (places[None, None, :] == jnp.arange(capacity)[None, :, None])
    )
    source_slot = jnp.sum(jnp.where(picked, local_slot[None, None, :], 0), axis=2).reshape(-1)
    first_entry = first_slot * per_hist
    my_owner = lax.dynamic_slice_in_dim(owners, first_entry, users_here * per_hist)
    my_place = lax.dynamic_slice_in_dim(places, first_entry, users_here * per_hist)
    picked_slot = (my_owner * capacity + my_place).astype(jnp.int32)
    sub = tile_len // 2
    halves = []
    for half in range(2):
        kv_half = lax.slice_in_dim(kv_cache, half * sub, (half + 1) * sub, axis=1)
        outgoing = kv_half.at[source_slot].get(mode="promise_in_bounds")
        outgoing = outgoing.reshape(req_count, capacity, sub, 2 * width)
        if half == 0:
            incoming = lax.all_to_all(outgoing, "req", split_axis=0, concat_axis=0, tiled=True)
        else:
            incoming = req_a2a(outgoing, 0)
        halves.append(incoming.reshape(req_count * capacity, sub, 2 * width))
    normed = layer_norm(cand_x.astype(jnp.float32)).astype(jnp.bfloat16)
    mixed_in = jnp.dot(normed.reshape(-1, width), w_uvqk, preferred_element_type=jnp.float32)
    projected = jax.nn.silu(mixed_in).astype(jnp.bfloat16).reshape(users_here, cand_rows, 4, width)
    u_gate = projected[:, :, 0]
    v_self = projected[:, :, 1]
    queries = projected[:, :, 2]
    k_self = projected[:, :, 3]
    my_user = hist_index // heads
    my_length = lax.dynamic_slice_in_dim(lengths, my_user, 1)
    q_row = 2 * per_hist * sub
    packed_a = lax.all_to_all(
        pack_for_heads(picked_slot, halves[0], queries, users_here, heads),
        "hist", split_axis=0, concat_axis=0, tiled=True,
    )
    history_mine = attend(my_length, packed_a, packed_a, q_row, per_hist, sub, tile_len, 0, score_scale)
    packed_b = lax.all_to_all(
        pack_for_heads(picked_slot, halves[1], None, users_here, heads),
        "hist", split_axis=0, concat_axis=0, tiled=True,
    )
    history_mine = attend(
        my_length, packed_b, packed_a, q_row, per_hist, sub, tile_len, sub, score_scale, init=history_mine
    ).astype(jnp.bfloat16)
    history_back = lax.all_to_all(
        history_mine.reshape(hist_count, cand_rows, head_dim), "hist", split_axis=0, concat_axis=0, tiled=True
    )
    row_limit = (live_counts - hist_index * cand_rows).astype(jnp.int32)
    return finish(
        history_back, projected.reshape(users_here, cand_rows, 4 * width), cand_x, w_out, self_bias,
        lengths.astype(jnp.int32), row_limit, heads, score_scale,
    )


def solution(mesh):
    return jax.shard_map(
        local,
        mesh=mesh,
        in_specs=(
            P("req", "hist", None),
            P(("req", "hist"), None, None),
            P(),
            P(),
            P(),
            P(),
            P(),
            P(),
            P(),
        ),
        out_specs=P("req", "hist", None),
        check_vma=False,
    )
```

```python
import functools
import math

import jax
import jax.numpy as jnp
from jax import lax
from jax.experimental import pallas as pl
from jax.experimental.pallas import tpu as pltpu
from jax.sharding import PartitionSpec as P


def layer_norm(values):
    mean_value = jnp.mean(values, axis=-1, keepdims=True)
    centred = values - mean_value
    spread = jnp.mean(centred * centred, axis=-1, keepdims=True)
    return centred * lax.rsqrt(spread + 1e-05)


def silu_tanh(values):
    return values * (0.5 + 0.5 * jnp.tanh(0.5 * values))


def req_a2a_kernel(send_ref, recv_ref, send_sem, recv_sem, local_sem, *, axis, other_axis):
    n = send_ref.shape[0]
    me = lax.axis_index(axis)
    other = lax.axis_index(other_axis)
    barrier = pltpu.get_barrier_semaphore()
    for k in range(1, n):
        peer = lax.rem(me + k, n)
        pl.semaphore_signal(
            barrier, inc=1, device_id={axis: peer, other_axis: other}, device_id_type=pl.DeviceIdType.MESH
        )
    pl.semaphore_wait(barrier, n - 1)
    copies = []
    for k in range(1, n):
        peer = lax.rem(me + k, n)
        copy = pltpu.make_async_remote_copy(
            src_ref=send_ref.at[peer],
            dst_ref=recv_ref.at[me],
            send_sem=send_sem.at[k],
            recv_sem=recv_sem.at[k],
            device_id={axis: peer, other_axis: other},
            device_id_type=pl.DeviceIdType.MESH,
        )
        copy.start()
        copies.append(copy)
    own = pltpu.make_async_copy(send_ref.at[me], recv_ref.at[me], local_sem)
    own.start()
    own.wait()
    for copy in copies:
        copy.wait_send()
    for k in range(1, n):
        src = lax.rem(me + n - k, n)
        pltpu.make_async_remote_copy(
            src_ref=send_ref.at[src],
            dst_ref=recv_ref.at[src],
            send_sem=send_sem.at[k],
            recv_sem=recv_sem.at[k],
            device_id={axis: src, other_axis: other},
            device_id_type=pl.DeviceIdType.MESH,
        ).wait_recv()


def req_a2a(x, collective_id):
    n = x.shape[0]
    return pl.pallas_call(
        functools.partial(req_a2a_kernel, axis="req", other_axis="hist"),
        out_shape=jax.ShapeDtypeStruct(x.shape, x.dtype),
        in_specs=[pl.BlockSpec(memory_space=pl.ANY)],
        out_specs=pl.BlockSpec(memory_space=pl.ANY),
        scratch_shapes=[
            pltpu.SemaphoreType.DMA((n,)),
            pltpu.SemaphoreType.DMA((n,)),
            pltpu.SemaphoreType.DMA(()),
        ],
        compiler_params=pltpu.CompilerParams(collective_id=collective_id, has_side_effects=True),
    )(x)


def attend_kernel(len_ref, kv_ref, qsrc_ref, *rest, n_tiles, sub, tile_len, offset, q_row, score_scale, chunk):
    if len(rest) == 3:
        init_ref, o_ref, q_ref = rest
    else:
        init_ref = None
        o_ref, q_ref = rest
    length = len_ref[0]
    n_cls, _, head_dim = kv_ref.shape
    span = n_tiles * sub
    block = q_ref.shape[0] // n_cls
    half_scale = 0.5 * score_scale
    for b in range(n_cls):
        q_ref[pl.ds(b * block, block), :] = qsrc_ref[b, pl.ds(q_row, block), :]
    if init_ref is None:
        o_ref[...] = jnp.zeros_like(o_ref)
    else:
        o_ref[...] = init_ref[...]

    def one_class(c, carry):
        key_index = lax.broadcasted_iota(jnp.int32, (1, span), 1)
        position = (c + n_cls * (key_index // sub)) * tile_len + offset + key_index % sub
        live = position < length

        def add_class(masked):
            keys = kv_ref[c, pl.ds(0, span), :]
            values = kv_ref[c, pl.ds(span, span), :]
            for ci in range(q_ref.shape[0] // chunk):
                rows = pl.ds(ci * chunk, chunk)
                scores = lax.dot_general(
                    q_ref[rows, :], keys, (((1,), (1,)), ((), ())), preferred_element_type=jnp.float32
                )
                half = scores * half_scale
                weights = half + half * jnp.tanh(half)
                if masked:
                    weights = jnp.where(live, weights, 0.0)
                o_ref[rows, :] += jnp.dot(weights.astype(jnp.bfloat16), values, preferred_element_type=jnp.float32)

        last_key = (c + n_cls * (n_tiles - 1)) * tile_len + offset + sub
        whole = last_key <= length
        pl.when(whole)(lambda: add_class(False))
        pl.when(jnp.logical_and(jnp.logical_not(whole), c * tile_len + offset < length))(lambda: add_class(True))
        return carry

    lax.fori_loop(0, n_cls, one_class, 0)


def attend(length, kv_packed, q_packed, q_row, n_tiles, sub, tile_len, offset, score_scale, init=None):
    n_cls, _, head_dim = q_packed.shape
    rows = n_cls * (q_packed.shape[1] - q_row)
    chunk = 2048
    kernel = functools.partial(
        attend_kernel,
        n_tiles=n_tiles,
        sub=sub,
        tile_len=tile_len,
        offset=offset,
        q_row=q_row,
        score_scale=score_scale,
        chunk=chunk,
    )
    return pl.pallas_call(
        kernel,
        out_shape=jax.ShapeDtypeStruct((rows, head_dim), jnp.float32),
        in_specs=[pl.BlockSpec(memory_space=pltpu.SMEM)]
        + [pl.BlockSpec(memory_space=pltpu.VMEM)] * (2 if init is None else 3),
        out_specs=pl.BlockSpec(memory_space=pltpu.VMEM),
        scratch_shapes=[pltpu.VMEM((rows, head_dim), jnp.bfloat16)],
    )(length, kv_packed, q_packed, *([] if init is None else [init]))


def pack_kernel(picked_ref, tiles_hbm, *rest, heads, users, per_hist, with_q):
    if with_q:
        q_ref, out_ref, staged, in_sem = rest
    else:
        out_ref, staged, in_sem = rest
    width = tiles_hbm.shape[2] // 2
    head_dim = width // heads
    sub = tiles_hbm.shape[1]
    span = per_hist * sub
    n_in = users * per_hist
    reads = []
    for i in range(n_in):
        read = pltpu.make_async_copy(tiles_hbm.at[picked_ref[i]], staged.at[i], in_sem.at[i])
        read.start()
        reads.append(read)
    if with_q:
        cand_rows = q_ref.shape[1]
        for u in range(users):
            for e in range(heads):
                out_ref[u * heads + e, pl.ds(2 * span, cand_rows), :] = q_ref[u, :, pl.ds(e * head_dim, head_dim)]
    for i in range(n_in):
        u, t = divmod(i, per_hist)
        reads[i].wait()
        for piece in range(2 * heads):
            e, kv = divmod(piece, 2)
            out_ref[u * heads + e, pl.ds(kv * span + t * sub, sub), :] = staged[
                i, :, pl.ds(piece * head_dim, head_dim)
            ]


def pack_for_heads(picked_slot, tiles, queries, users, heads):
    n_in = picked_slot.shape[0]
    per_hist = n_in // users
    sub, wide = tiles.shape[1], tiles.shape[2]
    head_dim = wide // (2 * heads)
    rows = 2 * per_hist * sub + (0 if queries is None else queries.shape[1])
    operands = [picked_slot, tiles] + ([] if queries is None else [queries])
    return pl.pallas_call(
        functools.partial(pack_kernel, heads=heads, users=users, per_hist=per_hist, with_q=queries is not None),
        out_shape=jax.ShapeDtypeStruct((users * heads, rows, head_dim), tiles.dtype),
        in_specs=[pl.BlockSpec(memory_space=pltpu.SMEM), pl.BlockSpec(memory_space=pl.ANY)]
        + ([] if queries is None else [pl.BlockSpec(memory_space=pltpu.VMEM)]),
        out_specs=pl.BlockSpec(memory_space=pltpu.VMEM),
        scratch_shapes=[
            pltpu.VMEM((n_in, sub, wide), tiles.dtype),
            pltpu.SemaphoreType.DMA((n_in,)),
        ],
    )(*operands)


def finish_kernel(
    bias_ref, len_ref, limit_ref, hist_ref, proj_ref, x_ref, w_ref, out_ref, att_ref, *, heads, score_scale
):
    users, rows, width = x_ref.shape
    head_dim = width // heads
    for u in range(users):
        divisor = (len_ref[u] + 1).astype(jnp.float32)
        for e in range(heads):
            value = proj_ref[u, :, pl.ds(width + e * head_dim, head_dim)].astype(jnp.float32)
            query = proj_ref[u, :, pl.ds(2 * width + e * head_dim, head_dim)].astype(jnp.float32)
            key = proj_ref[u, :, pl.ds(3 * width + e * head_dim, head_dim)].astype(jnp.float32)
            self_score = jnp.sum(query * key, axis=-1, keepdims=True) * score_scale + bias_ref[e]
            own = self_score * (0.5 + 0.5 * jnp.tanh(0.5 * self_score)) * value
            history = hist_ref[u * heads + e].astype(jnp.float32)
            att_ref[:, pl.ds(e * head_dim, head_dim)] = (history + own) / divisor
        attended = att_ref[...]
        centred = attended - jnp.mean(attended, axis=-1, keepdims=True)
        spread = jnp.mean(centred * centred, axis=-1, keepdims=True)
        gate = proj_ref[u, :, pl.ds(0, width)].astype(jnp.float32)
        gated = (centred * lax.rsqrt(spread + 1e-05) * gate).astype(jnp.bfloat16)
        result = x_ref[u].astype(jnp.float32) + jnp.dot(gated, w_ref[...], preferred_element_type=jnp.float32)
        row = lax.broadcasted_iota(jnp.int32, (rows, 1), 0)
        out_ref[u] = jnp.where(row < limit_ref[u], result, 0.0).astype(out_ref.dtype)


def finish(history_back, projected, cand_x, w_out, self_bias, lengths, row_limit, heads, score_scale):
    users, rows, width = cand_x.shape
    smem = pl.BlockSpec(memory_space=pltpu.SMEM)
    vmem = pl.BlockSpec(memory_space=pltpu.VMEM)
    return pl.pallas_call(
        functools.partial(finish_kernel, heads=heads, score_scale=score_scale),
        out_shape=jax.ShapeDtypeStruct(cand_x.shape, cand_x.dtype),
        in_specs=[smem, smem, smem, vmem, vmem, vmem, vmem],
        out_specs=vmem,
        scratch_shapes=[pltpu.VMEM((rows, width), jnp.float32)],
    )(self_bias, lengths, row_limit, history_back, projected, cand_x, w_out)


def local(cand_x, kv_cache, w_uvqk, w_out, self_bias, user_rank, hist_len, cand_count, tile_slot):
    users_here, cand_rows, width = cand_x.shape
    heads = self_bias.shape[0]
    head_dim = width // heads
    score_scale = 1.0 / math.sqrt(head_dim)
    slots_own, tile_len, _ = kv_cache.shape
    user_total, tiles_max = tile_slot.shape
    req_count = lax.axis_size("req")
    hist_count = lax.axis_size("hist")
    req_index = lax.axis_index("req")
    hist_index = lax.axis_index("hist")
    per_hist = tiles_max // hist_count
    capacity = slots_own // req_count + 1
    first_slot = req_index * users_here
    user_ids = lax.dynamic_slice_in_dim(user_rank, first_slot, users_here)
    match_user = user_ids[:, None] == jnp.arange(user_total)[None, :]
    lengths = jnp.sum(jnp.where(match_user, hist_len[None, :], 0), axis=1)
    live_counts = jnp.sum(jnp.where(match_user, cand_count[None, :], 0), axis=1)
    column = lax.dynamic_index_in_dim(
        tile_slot.reshape(user_total, per_hist, hist_count), hist_index, axis=2, keepdims=False
    )
    codes = column.reshape(-1)
    owners = codes // slots_own
    local_slot = codes % slots_own
    dests = jnp.repeat(jnp.arange(user_total) // users_here, per_hist)
    entry_ids = jnp.arange(codes.shape[0])
    same_pair = (
        (owners[:, None] == owners[None, :])
        & (dests[:, None] == dests[None, :])
        & (entry_ids[:, None] > entry_ids[None, :])
    )
    places = jnp.sum(jnp.where(same_pair, 1, 0), axis=1)
    picked = (
        (owners[None, None, :] == req_index)
        & (dests[None, None, :] == jnp.arange(req_count)[:, None, None])
        & (places[None, None, :] == jnp.arange(capacity)[None, :, None])
    )
    source_slot = jnp.sum(jnp.where(picked, local_slot[None, None, :], 0), axis=2).reshape(-1)
    first_entry = first_slot * per_hist
    my_owner = lax.dynamic_slice_in_dim(owners, first_entry, users_here * per_hist)
    my_place = lax.dynamic_slice_in_dim(places, first_entry, users_here * per_hist)
    picked_slot = (my_owner * capacity + my_place).astype(jnp.int32)
    sub = tile_len // 2
    sending = []
    for half in range(2):
        kv_half = lax.slice_in_dim(kv_cache, half * sub, (half + 1) * sub, axis=1)
        outgoing = kv_half.at[source_slot].get(mode="promise_in_bounds")
        sending.append(outgoing.reshape(req_count, capacity, sub, 2 * width))
    first_in = lax.all_to_all(sending[0], "req", split_axis=0, concat_axis=0, tiled=True)
    normed = layer_norm(cand_x.astype(jnp.float32)).astype(jnp.bfloat16)
    mixed_in = jnp.dot(normed.reshape(-1, width), w_uvqk, preferred_element_type=jnp.float32)
    projected = jax.nn.silu(mixed_in).astype(jnp.bfloat16).reshape(users_here, cand_rows, 4, width)
    projected, second_out = lax.optimization_barrier((projected, sending[1]))
    second_in = req_a2a(second_out, 0)
    halves = [
        first_in.reshape(req_count * capacity, sub, 2 * width),
        second_in.reshape(req_count * capacity, sub, 2 * width),
    ]
    u_gate = projected[:, :, 0]
    v_self = projected[:, :, 1]
    queries = projected[:, :, 2]
    k_self = projected[:, :, 3]
    my_user = hist_index // heads
    my_length = lax.dynamic_slice_in_dim(lengths, my_user, 1)
    q_row = 2 * per_hist * sub
    packed_a = lax.all_to_all(
        pack_for_heads(picked_slot, halves[0], queries, users_here, heads),
        "hist", split_axis=0, concat_axis=0, tiled=True,
    )
    history_mine = attend(my_length, packed_a, packed_a, q_row, per_hist, sub, tile_len, 0, score_scale)
    packed_b = lax.all_to_all(
        pack_for_heads(picked_slot, halves[1], None, users_here, heads),
        "hist", split_axis=0, concat_axis=0, tiled=True,
    )
    history_mine = attend(
        my_length, packed_b, packed_a, q_row, per_hist, sub, tile_len, sub, score_scale, init=history_mine
    ).astype(jnp.bfloat16)
    history_back = lax.all_to_all(
        history_mine.reshape(hist_count, cand_rows, head_dim), "hist", split_axis=0, concat_axis=0, tiled=True
    )
    row_limit = (live_counts - hist_index * cand_rows).astype(jnp.int32)
    return finish(
        history_back, projected.reshape(users_here, cand_rows, 4 * width), cand_x, w_out, self_bias,
        lengths.astype(jnp.int32), row_limit, heads, score_scale,
    )


def solution(mesh):
    return jax.shard_map(
        local,
        mesh=mesh,
        in_specs=(
            P("req", "hist", None),
            P(("req", "hist"), None, None),
            P(),
            P(),
            P(),
            P(),
            P(),
            P(),
            P(),
        ),
        out_specs=P("req", "hist", None),
        check_vma=False,
    )
```

```python
import functools
import math

import jax
import jax.numpy as jnp
from jax import lax
from jax.experimental import pallas as pl
from jax.experimental.pallas import tpu as pltpu
from jax.sharding import PartitionSpec as P


def layer_norm(values):
    mean_value = jnp.mean(values, axis=-1, keepdims=True)
    centred = values - mean_value
    spread = jnp.mean(centred * centred, axis=-1, keepdims=True)
    return centred * lax.rsqrt(spread + 1e-05)


def silu_tanh(values):
    return values * (0.5 + 0.5 * jnp.tanh(0.5 * values))


def req_a2a_kernel(send_ref, recv_ref, send_sem, recv_sem, local_sem, *, axis, other_axis):
    n = send_ref.shape[0]
    me = lax.axis_index(axis)
    other = lax.axis_index(other_axis)
    barrier = pltpu.get_barrier_semaphore()
    for k in range(1, n):
        peer = lax.rem(me + k, n)
        pl.semaphore_signal(
            barrier, inc=1, device_id={axis: peer, other_axis: other}, device_id_type=pl.DeviceIdType.MESH
        )
    pl.semaphore_wait(barrier, n - 1)
    copies = []
    for k in range(1, n):
        peer = lax.rem(me + k, n)
        copy = pltpu.make_async_remote_copy(
            src_ref=send_ref.at[peer],
            dst_ref=recv_ref.at[me],
            send_sem=send_sem.at[k],
            recv_sem=recv_sem.at[k],
            device_id={axis: peer, other_axis: other},
            device_id_type=pl.DeviceIdType.MESH,
        )
        copy.start()
        copies.append(copy)
    own = pltpu.make_async_copy(send_ref.at[me], recv_ref.at[me], local_sem)
    own.start()
    own.wait()
    for copy in copies:
        copy.wait_send()
    for k in range(1, n):
        src = lax.rem(me + n - k, n)
        pltpu.make_async_remote_copy(
            src_ref=send_ref.at[src],
            dst_ref=recv_ref.at[src],
            send_sem=send_sem.at[k],
            recv_sem=recv_sem.at[k],
            device_id={axis: src, other_axis: other},
            device_id_type=pl.DeviceIdType.MESH,
        ).wait_recv()


def req_a2a(x, collective_id):
    n = x.shape[0]
    return pl.pallas_call(
        functools.partial(req_a2a_kernel, axis="req", other_axis="hist"),
        out_shape=jax.ShapeDtypeStruct(x.shape, x.dtype),
        in_specs=[pl.BlockSpec(memory_space=pl.ANY)],
        out_specs=pl.BlockSpec(memory_space=pl.ANY),
        scratch_shapes=[
            pltpu.SemaphoreType.DMA((n,)),
            pltpu.SemaphoreType.DMA((n,)),
            pltpu.SemaphoreType.DMA(()),
        ],
        compiler_params=pltpu.CompilerParams(collective_id=collective_id, has_side_effects=True),
    )(x)


def attend_kernel(len_ref, kv_ref, qsrc_ref, *rest, n_tiles, sub, tile_len, offset, q_row, score_scale, chunk):
    if len(rest) == 4:
        init_ref, out_ref, q_ref, o_ref = rest
    else:
        init_ref = out_ref = None
        o_ref, q_ref = rest
    length = len_ref[0]
    n_cls, _, head_dim = kv_ref.shape
    span = n_tiles * sub
    block = q_ref.shape[0] // n_cls
    half_scale = 0.5 * score_scale
    for b in range(n_cls):
        q_ref[pl.ds(b * block, block), :] = qsrc_ref[b, pl.ds(q_row, block), :]
    if init_ref is None:
        o_ref[...] = jnp.zeros_like(o_ref)
    else:
        o_ref[...] = init_ref[...]

    def one_class(c, carry):
        key_index = lax.broadcasted_iota(jnp.int32, (1, span), 1)
        position = (c + n_cls * (key_index // sub)) * tile_len + offset + key_index % sub
        live = position < length

        def add_class(masked):
            keys = kv_ref[c, pl.ds(0, span), :]
            values = kv_ref[c, pl.ds(span, span), :]
            for ci in range(q_ref.shape[0] // chunk):
                rows = pl.ds(ci * chunk, chunk)
                scores = lax.dot_general(
                    q_ref[rows, :], keys, (((1,), (1,)), ((), ())), preferred_element_type=jnp.float32
                )
                half = scores * half_scale
                weights = half + half * jnp.tanh(half)
                if masked:
                    weights = jnp.where(live, weights, 0.0)
                o_ref[rows, :] += jnp.dot(weights.astype(jnp.bfloat16), values, preferred_element_type=jnp.float32)

        last_key = (c + n_cls * (n_tiles - 1)) * tile_len + offset + sub
        whole = last_key <= length
        pl.when(whole)(lambda: add_class(False))
        pl.when(jnp.logical_and(jnp.logical_not(whole), c * tile_len + offset < length))(lambda: add_class(True))
        return carry

    lax.fori_loop(0, n_cls, one_class, 0)
    if out_ref is not None:
        out_ref[...] = o_ref[...].astype(out_ref.dtype)


def attend(length, kv_packed, q_packed, q_row, n_tiles, sub, tile_len, offset, score_scale, init=None):
    n_cls, _, head_dim = q_packed.shape
    rows = n_cls * (q_packed.shape[1] - q_row)
    chunk = 2048
    kernel = functools.partial(
        attend_kernel,
        n_tiles=n_tiles,
        sub=sub,
        tile_len=tile_len,
        offset=offset,
        q_row=q_row,
        score_scale=score_scale,
        chunk=chunk,
    )
    return pl.pallas_call(
        kernel,
        out_shape=jax.ShapeDtypeStruct((rows, head_dim), jnp.float32 if init is None else jnp.bfloat16),
        in_specs=[pl.BlockSpec(memory_space=pltpu.SMEM)]
        + [pl.BlockSpec(memory_space=pltpu.VMEM)] * (2 if init is None else 3),
        out_specs=pl.BlockSpec(memory_space=pltpu.VMEM),
        scratch_shapes=[pltpu.VMEM((rows, head_dim), jnp.bfloat16)]
        + ([] if init is None else [pltpu.VMEM((rows, head_dim), jnp.float32)]),
    )(length, kv_packed, q_packed, *([] if init is None else [init]))


def pack_kernel(picked_ref, tiles_hbm, *rest, heads, users, per_hist, with_q):
    if with_q:
        q_ref, out_ref, staged, in_sem = rest
    else:
        out_ref, staged, in_sem = rest
    width = tiles_hbm.shape[2] // 2
    head_dim = width // heads
    sub = tiles_hbm.shape[1]
    span = per_hist * sub
    n_in = users * per_hist
    reads = []
    for i in range(n_in):
        read = pltpu.make_async_copy(tiles_hbm.at[picked_ref[i]], staged.at[i], in_sem.at[i])
        read.start()
        reads.append(read)
    if with_q:
        cand_rows = q_ref.shape[1]
        for u in range(users):
            for e in range(heads):
                out_ref[u * heads + e, pl.ds(2 * span, cand_rows), :] = q_ref[u, :, pl.ds(e * head_dim, head_dim)]
    for i in range(n_in):
        u, t = divmod(i, per_hist)
        reads[i].wait()
        for piece in range(2 * heads):
            e, kv = divmod(piece, 2)
            out_ref[u * heads + e, pl.ds(kv * span + t * sub, sub), :] = staged[
                i, :, pl.ds(piece * head_dim, head_dim)
            ]


def pack_for_heads(picked_slot, tiles, queries, users, heads):
    n_in = picked_slot.shape[0]
    per_hist = n_in // users
    sub, wide = tiles.shape[1], tiles.shape[2]
    head_dim = wide // (2 * heads)
    rows = 2 * per_hist * sub + (0 if queries is None else queries.shape[1])
    operands = [picked_slot, tiles] + ([] if queries is None else [queries])
    return pl.pallas_call(
        functools.partial(pack_kernel, heads=heads, users=users, per_hist=per_hist, with_q=queries is not None),
        out_shape=jax.ShapeDtypeStruct((users * heads, rows, head_dim), tiles.dtype),
        in_specs=[pl.BlockSpec(memory_space=pltpu.SMEM), pl.BlockSpec(memory_space=pl.ANY)]
        + ([] if queries is None else [pl.BlockSpec(memory_space=pltpu.VMEM)]),
        out_specs=pl.BlockSpec(memory_space=pltpu.VMEM),
        scratch_shapes=[
            pltpu.VMEM((n_in, sub, wide), tiles.dtype),
            pltpu.SemaphoreType.DMA((n_in,)),
        ],
    )(*operands)


def finish_kernel(
    bias_ref, len_ref, limit_ref, hist_ref, proj_ref, x_ref, w_ref, out_ref, att_ref, *, heads, score_scale
):
    users, rows, width = x_ref.shape
    head_dim = width // heads
    for u in range(users):
        divisor = (len_ref[u] + 1).astype(jnp.float32)
        for e in range(heads):
            value = proj_ref[u, :, pl.ds(width + e * head_dim, head_dim)].astype(jnp.float32)
            query = proj_ref[u, :, pl.ds(2 * width + e * head_dim, head_dim)].astype(jnp.float32)
            key = proj_ref[u, :, pl.ds(3 * width + e * head_dim, head_dim)].astype(jnp.float32)
            self_score = jnp.sum(query * key, axis=-1, keepdims=True) * score_scale + bias_ref[e]
            own = self_score * (0.5 + 0.5 * jnp.tanh(0.5 * self_score)) * value
            history = hist_ref[u * heads + e].astype(jnp.float32)
            att_ref[:, pl.ds(e * head_dim, head_dim)] = (history + own) / divisor
        attended = att_ref[...]
        centred = attended - jnp.mean(attended, axis=-1, keepdims=True)
        spread = jnp.mean(centred * centred, axis=-1, keepdims=True)
        gate = proj_ref[u, :, pl.ds(0, width)].astype(jnp.float32)
        gated = (centred * lax.rsqrt(spread + 1e-05) * gate).astype(jnp.bfloat16)
        result = x_ref[u].astype(jnp.float32) + jnp.dot(gated, w_ref[...], preferred_element_type=jnp.float32)
        row = lax.broadcasted_iota(jnp.int32, (rows, 1), 0)
        out_ref[u] = jnp.where(row < limit_ref[u], result, 0.0).astype(out_ref.dtype)


def finish(history_back, projected, cand_x, w_out, self_bias, lengths, row_limit, heads, score_scale):
    users, rows, width = cand_x.shape
    smem = pl.BlockSpec(memory_space=pltpu.SMEM)
    vmem = pl.BlockSpec(memory_space=pltpu.VMEM)
    return pl.pallas_call(
        functools.partial(finish_kernel, heads=heads, score_scale=score_scale),
        out_shape=jax.ShapeDtypeStruct(cand_x.shape, cand_x.dtype),
        in_specs=[smem, smem, smem, vmem, vmem, vmem, vmem],
        out_specs=vmem,
        scratch_shapes=[pltpu.VMEM((rows, width), jnp.float32)],
    )(self_bias, lengths, row_limit, history_back, projected, cand_x, w_out)


def local(cand_x, kv_cache, w_uvqk, w_out, self_bias, user_rank, hist_len, cand_count, tile_slot):
    users_here, cand_rows, width = cand_x.shape
    heads = self_bias.shape[0]
    head_dim = width // heads
    score_scale = 1.0 / math.sqrt(head_dim)
    slots_own, tile_len, _ = kv_cache.shape
    user_total, tiles_max = tile_slot.shape
    req_count = lax.axis_size("req")
    hist_count = lax.axis_size("hist")
    req_index = lax.axis_index("req")
    hist_index = lax.axis_index("hist")
    per_hist = tiles_max // hist_count
    capacity = slots_own // req_count + 1
    first_slot = req_index * users_here
    user_ids = lax.dynamic_slice_in_dim(user_rank, first_slot, users_here)
    match_user = user_ids[:, None] == jnp.arange(user_total)[None, :]
    lengths = jnp.sum(jnp.where(match_user, hist_len[None, :], 0), axis=1)
    live_counts = jnp.sum(jnp.where(match_user, cand_count[None, :], 0), axis=1)
    column = lax.dynamic_index_in_dim(
        tile_slot.reshape(user_total, per_hist, hist_count), hist_index, axis=2, keepdims=False
    )
    codes = column.reshape(-1)
    owners = codes // slots_own
    local_slot = codes % slots_own
    dests = jnp.repeat(jnp.arange(user_total) // users_here, per_hist)
    entry_ids = jnp.arange(codes.shape[0])
    same_pair = (
        (owners[:, None] == owners[None, :])
        & (dests[:, None] == dests[None, :])
        & (entry_ids[:, None] > entry_ids[None, :])
    )
    places = jnp.sum(jnp.where(same_pair, 1, 0), axis=1)
    picked = (
        (owners[None, None, :] == req_index)
        & (dests[None, None, :] == jnp.arange(req_count)[:, None, None])
        & (places[None, None, :] == jnp.arange(capacity)[None, :, None])
    )
    source_slot = jnp.sum(jnp.where(picked, local_slot[None, None, :], 0), axis=2).reshape(-1)
    first_entry = first_slot * per_hist
    my_owner = lax.dynamic_slice_in_dim(owners, first_entry, users_here * per_hist)
    my_place = lax.dynamic_slice_in_dim(places, first_entry, users_here * per_hist)
    picked_slot = (my_owner * capacity + my_place).astype(jnp.int32)
    sub = tile_len // 2
    sending = []
    for half in range(2):
        kv_half = lax.slice_in_dim(kv_cache, half * sub, (half + 1) * sub, axis=1)
        outgoing = kv_half.at[source_slot].get(mode="promise_in_bounds")
        sending.append(outgoing.reshape(req_count, capacity, sub, 2 * width))
    first_in = lax.all_to_all(sending[0], "req", split_axis=0, concat_axis=0, tiled=True)
    normed = layer_norm(cand_x.astype(jnp.float32)).astype(jnp.bfloat16)
    mixed_in = jnp.dot(normed.reshape(-1, width), w_uvqk, preferred_element_type=jnp.float32)
    projected = jax.nn.silu(mixed_in).astype(jnp.bfloat16).reshape(users_here, cand_rows, 4 * width)
    projected, second_out = lax.optimization_barrier((projected, sending[1]))
    second_in = req_a2a(second_out, 0)
    halves = [
        first_in.reshape(req_count * capacity, sub, 2 * width),
        second_in.reshape(req_count * capacity, sub, 2 * width),
    ]
    queries = projected[:, :, 2 * width : 3 * width]
    my_user = hist_index // heads
    my_length = lax.dynamic_slice_in_dim(lengths, my_user, 1)
    q_row = 2 * per_hist * sub
    packed_a = lax.all_to_all(
        pack_for_heads(picked_slot, halves[0], queries, users_here, heads),
        "hist", split_axis=0, concat_axis=0, tiled=True,
    )
    history_mine = attend(my_length, packed_a, packed_a, q_row, per_hist, sub, tile_len, 0, score_scale)
    packed_b = lax.all_to_all(
        pack_for_heads(picked_slot, halves[1], None, users_here, heads),
        "hist", split_axis=0, concat_axis=0, tiled=True,
    )
    history_mine = attend(
        my_length, packed_b, packed_a, q_row, per_hist, sub, tile_len, sub, score_scale, init=history_mine
    )
    history_back = lax.all_to_all(
        history_mine.reshape(hist_count, cand_rows, head_dim), "hist", split_axis=0, concat_axis=0, tiled=True
    )
    row_limit = (live_counts - hist_index * cand_rows).astype(jnp.int32)
    return finish(
        history_back, projected, cand_x, w_out, self_bias,
        lengths.astype(jnp.int32), row_limit, heads, score_scale,
    )


def solution(mesh):
    return jax.shard_map(
        local,
        mesh=mesh,
        in_specs=(
            P("req", "hist", None),
            P(("req", "hist"), None, None),
            P(),
            P(),
            P(),
            P(),
            P(),
            P(),
            P(),
        ),
        out_specs=P("req", "hist", None),
        check_vma=False,
    )
```

```python
import functools
import math

import jax
import jax.numpy as jnp
from jax import lax
from jax.experimental import pallas as pl
from jax.experimental.pallas import tpu as pltpu
from jax.sharding import PartitionSpec as P


def layer_norm(values):
    mean_value = jnp.mean(values, axis=-1, keepdims=True)
    centred = values - mean_value
    spread = jnp.mean(centred * centred, axis=-1, keepdims=True)
    return centred * lax.rsqrt(spread + 1e-05)


def silu_tanh(values):
    return values * (0.5 + 0.5 * jnp.tanh(0.5 * values))


def req_a2a_kernel(send_ref, recv_ref, send_sem, recv_sem, local_sem, *, axis, other_axis):
    n = send_ref.shape[0]
    me = lax.axis_index(axis)
    other = lax.axis_index(other_axis)
    barrier = pltpu.get_barrier_semaphore()
    for k in range(1, n):
        peer = lax.rem(me + k, n)
        pl.semaphore_signal(
            barrier, inc=1, device_id={axis: peer, other_axis: other}, device_id_type=pl.DeviceIdType.MESH
        )
    pl.semaphore_wait(barrier, n - 1)
    copies = []
    for k in range(1, n):
        peer = lax.rem(me + k, n)
        copy = pltpu.make_async_remote_copy(
            src_ref=send_ref.at[peer],
            dst_ref=recv_ref.at[me],
            send_sem=send_sem.at[k],
            recv_sem=recv_sem.at[k],
            device_id={axis: peer, other_axis: other},
            device_id_type=pl.DeviceIdType.MESH,
        )
        copy.start()
        copies.append(copy)
    own = pltpu.make_async_copy(send_ref.at[me], recv_ref.at[me], local_sem)
    own.start()
    own.wait()
    for copy in copies:
        copy.wait_send()
    for k in range(1, n):
        src = lax.rem(me + n - k, n)
        pltpu.make_async_remote_copy(
            src_ref=send_ref.at[src],
            dst_ref=recv_ref.at[src],
            send_sem=send_sem.at[k],
            recv_sem=recv_sem.at[k],
            device_id={axis: src, other_axis: other},
            device_id_type=pl.DeviceIdType.MESH,
        ).wait_recv()


def req_a2a(x, collective_id):
    n = x.shape[0]
    return pl.pallas_call(
        functools.partial(req_a2a_kernel, axis="req", other_axis="hist"),
        out_shape=jax.ShapeDtypeStruct(x.shape, x.dtype),
        in_specs=[pl.BlockSpec(memory_space=pl.ANY)],
        out_specs=pl.BlockSpec(memory_space=pl.ANY),
        scratch_shapes=[
            pltpu.SemaphoreType.DMA((n,)),
            pltpu.SemaphoreType.DMA((n,)),
            pltpu.SemaphoreType.DMA(()),
        ],
        compiler_params=pltpu.CompilerParams(collective_id=collective_id, has_side_effects=True),
    )(x)


def attend_kernel(len_ref, kv_ref, qsrc_ref, *rest, n_tiles, sub, tile_len, offset, q_row, score_scale, chunk):
    if len(rest) == 3:
        init_ref, o_ref, q_ref = rest
    else:
        init_ref = None
        o_ref, q_ref = rest
    length = len_ref[0]
    n_cls, _, head_dim = kv_ref.shape
    span = n_tiles * sub
    block = q_ref.shape[0] // n_cls
    half_scale = 0.5 * score_scale
    for b in range(n_cls):
        q_ref[pl.ds(b * block, block), :] = qsrc_ref[b, pl.ds(q_row, block), :]
    if init_ref is None:
        o_ref[...] = jnp.zeros_like(o_ref)
    else:
        o_ref[...] = init_ref[...]

    def one_class(c, carry):
        key_index = lax.broadcasted_iota(jnp.int32, (1, span), 1)
        position = (c + n_cls * (key_index // sub)) * tile_len + offset + key_index % sub
        live = position < length

        def add_class(masked):
            keys = kv_ref[c, pl.ds(0, span), :]
            values = kv_ref[c, pl.ds(span, span), :]
            for ci in range(q_ref.shape[0] // chunk):
                rows = pl.ds(ci * chunk, chunk)
                scores = lax.dot_general(
                    q_ref[rows, :], keys, (((1,), (1,)), ((), ())), preferred_element_type=jnp.float32
                )
                half = scores * half_scale
                weights = half + half * jnp.tanh(half)
                if masked:
                    weights = jnp.where(live, weights, 0.0)
                o_ref[rows, :] += jnp.dot(weights.astype(jnp.bfloat16), values, preferred_element_type=jnp.float32)

        last_key = (c + n_cls * (n_tiles - 1)) * tile_len + offset + sub
        whole = last_key <= length
        pl.when(whole)(lambda: add_class(False))
        pl.when(jnp.logical_and(jnp.logical_not(whole), c * tile_len + offset < length))(lambda: add_class(True))
        return carry

    lax.fori_loop(0, n_cls, one_class, 0)


def attend(length, kv_packed, q_packed, q_row, n_tiles, sub, tile_len, offset, score_scale, init=None):
    n_cls, _, head_dim = q_packed.shape
    rows = n_cls * (q_packed.shape[1] - q_row)
    chunk = 2048
    kernel = functools.partial(
        attend_kernel,
        n_tiles=n_tiles,
        sub=sub,
        tile_len=tile_len,
        offset=offset,
        q_row=q_row,
        score_scale=score_scale,
        chunk=chunk,
    )
    return pl.pallas_call(
        kernel,
        out_shape=jax.ShapeDtypeStruct((rows, head_dim), jnp.float32),
        in_specs=[pl.BlockSpec(memory_space=pltpu.SMEM)]
        + [pl.BlockSpec(memory_space=pltpu.VMEM)] * (2 if init is None else 3),
        out_specs=pl.BlockSpec(memory_space=pltpu.VMEM),
        scratch_shapes=[pltpu.VMEM((rows, head_dim), jnp.bfloat16)],
    )(length, kv_packed, q_packed, *([] if init is None else [init]))


def pack_kernel(picked_ref, tiles_hbm, *rest, heads, users, per_hist, with_q):
    if with_q:
        q_ref, out_ref, staged, in_sem = rest
    else:
        out_ref, staged, in_sem = rest
    width = tiles_hbm.shape[2] // 2
    head_dim = width // heads
    sub = tiles_hbm.shape[1]
    span = per_hist * sub
    n_in = users * per_hist
    reads = []
    for i in range(n_in):
        read = pltpu.make_async_copy(tiles_hbm.at[picked_ref[i]], staged.at[i], in_sem.at[i])
        read.start()
        reads.append(read)
    if with_q:
        cand_rows = q_ref.shape[1]
        for u in range(users):
            for e in range(heads):
                out_ref[u * heads + e, pl.ds(2 * span, cand_rows), :] = q_ref[u, :, pl.ds(e * head_dim, head_dim)]
    for i in range(n_in):
        u, t = divmod(i, per_hist)
        reads[i].wait()
        for piece in range(2 * heads):
            e, kv = divmod(piece, 2)
            out_ref[u * heads + e, pl.ds(kv * span + t * sub, sub), :] = staged[
                i, :, pl.ds(piece * head_dim, head_dim)
            ]


def pack_for_heads(picked_slot, tiles, queries, users, heads):
    n_in = picked_slot.shape[0]
    per_hist = n_in // users
    sub, wide = tiles.shape[1], tiles.shape[2]
    head_dim = wide // (2 * heads)
    rows = 2 * per_hist * sub + (0 if queries is None else queries.shape[1])
    operands = [picked_slot, tiles] + ([] if queries is None else [queries])
    return pl.pallas_call(
        functools.partial(pack_kernel, heads=heads, users=users, per_hist=per_hist, with_q=queries is not None),
        out_shape=jax.ShapeDtypeStruct((users * heads, rows, head_dim), tiles.dtype),
        in_specs=[pl.BlockSpec(memory_space=pltpu.SMEM), pl.BlockSpec(memory_space=pl.ANY)]
        + ([] if queries is None else [pl.BlockSpec(memory_space=pltpu.VMEM)]),
        out_specs=pl.BlockSpec(memory_space=pltpu.VMEM),
        scratch_shapes=[
            pltpu.VMEM((n_in, sub, wide), tiles.dtype),
            pltpu.SemaphoreType.DMA((n_in,)),
        ],
    )(*operands)


def finish_kernel(
    bias_ref, len_ref, limit_ref, hist_ref, proj_ref, x_ref, w_ref, out_ref, att_ref, *, heads, score_scale
):
    users, rows, width = x_ref.shape
    head_dim = width // heads
    for u in range(users):
        divisor = (len_ref[u] + 1).astype(jnp.float32)
        for e in range(heads):
            value = proj_ref[u, :, pl.ds(width + e * head_dim, head_dim)].astype(jnp.float32)
            query = proj_ref[u, :, pl.ds(2 * width + e * head_dim, head_dim)].astype(jnp.float32)
            key = proj_ref[u, :, pl.ds(3 * width + e * head_dim, head_dim)].astype(jnp.float32)
            self_score = jnp.sum(query * key, axis=-1, keepdims=True) * score_scale + bias_ref[e]
            own = self_score * (0.5 + 0.5 * jnp.tanh(0.5 * self_score)) * value
            history = hist_ref[u * heads + e].astype(jnp.float32)
            att_ref[:, pl.ds(e * head_dim, head_dim)] = (history + own) / divisor
        attended = att_ref[...]
        centred = attended - jnp.mean(attended, axis=-1, keepdims=True)
        spread = jnp.mean(centred * centred, axis=-1, keepdims=True)
        gate = proj_ref[u, :, pl.ds(0, width)].astype(jnp.float32)
        gated = (centred * lax.rsqrt(spread + 1e-05) * gate).astype(jnp.bfloat16)
        result = x_ref[u].astype(jnp.float32) + jnp.dot(gated, w_ref[...], preferred_element_type=jnp.float32)
        row = lax.broadcasted_iota(jnp.int32, (rows, 1), 0)
        out_ref[u] = jnp.where(row < limit_ref[u], result, 0.0).astype(out_ref.dtype)


def finish(history_back, projected, cand_x, w_out, self_bias, lengths, row_limit, heads, score_scale):
    users, rows, width = cand_x.shape
    smem = pl.BlockSpec(memory_space=pltpu.SMEM)
    vmem = pl.BlockSpec(memory_space=pltpu.VMEM)
    return pl.pallas_call(
        functools.partial(finish_kernel, heads=heads, score_scale=score_scale),
        out_shape=jax.ShapeDtypeStruct(cand_x.shape, cand_x.dtype),
        in_specs=[smem, smem, smem, vmem, vmem, vmem, vmem],
        out_specs=vmem,
        scratch_shapes=[pltpu.VMEM((rows, width), jnp.float32)],
    )(self_bias, lengths, row_limit, history_back, projected, cand_x, w_out)


def local(cand_x, kv_cache, w_uvqk, w_out, self_bias, user_rank, hist_len, cand_count, tile_slot):
    users_here, cand_rows, width = cand_x.shape
    heads = self_bias.shape[0]
    head_dim = width // heads
    score_scale = 1.0 / math.sqrt(head_dim)
    slots_own, tile_len, _ = kv_cache.shape
    user_total, tiles_max = tile_slot.shape
    req_count = lax.axis_size("req")
    hist_count = lax.axis_size("hist")
    req_index = lax.axis_index("req")
    hist_index = lax.axis_index("hist")
    per_hist = tiles_max // hist_count
    capacity = slots_own // req_count + 1
    first_slot = req_index * users_here
    user_ids = lax.dynamic_slice_in_dim(user_rank, first_slot, users_here)
    match_user = user_ids[:, None] == jnp.arange(user_total)[None, :]
    lengths = jnp.sum(jnp.where(match_user, hist_len[None, :], 0), axis=1)
    live_counts = jnp.sum(jnp.where(match_user, cand_count[None, :], 0), axis=1)
    column = lax.dynamic_index_in_dim(
        tile_slot.reshape(user_total, per_hist, hist_count), hist_index, axis=2, keepdims=False
    )
    codes = column.reshape(-1)
    owners = codes // slots_own
    local_slot = codes % slots_own
    dests = jnp.repeat(jnp.arange(user_total) // users_here, per_hist)
    entry_ids = jnp.arange(codes.shape[0])
    same_pair = (
        (owners[:, None] == owners[None, :])
        & (dests[:, None] == dests[None, :])
        & (entry_ids[:, None] > entry_ids[None, :])
    )
    places = jnp.sum(jnp.where(same_pair, 1, 0), axis=1)
    picked = (
        (owners[None, None, :] == req_index)
        & (dests[None, None, :] == jnp.arange(req_count)[:, None, None])
        & (places[None, None, :] == jnp.arange(capacity)[None, :, None])
    )
    source_slot = jnp.sum(jnp.where(picked, local_slot[None, None, :], 0), axis=2).reshape(-1)
    first_entry = first_slot * per_hist
    my_owner = lax.dynamic_slice_in_dim(owners, first_entry, users_here * per_hist)
    my_place = lax.dynamic_slice_in_dim(places, first_entry, users_here * per_hist)
    picked_slot = (my_owner * capacity + my_place).astype(jnp.int32)
    sub = tile_len // 2
    sending = []
    for half in range(2):
        kv_halves = kv_cache.reshape(slots_own, tile_len // sub, sub, 2 * width)
        outgoing = kv_halves.at[source_slot, half].get(mode="promise_in_bounds")
        sending.append(outgoing.reshape(req_count, capacity, sub, 2 * width))
    first_in = lax.all_to_all(sending[0], "req", split_axis=0, concat_axis=0, tiled=True)
    normed = layer_norm(cand_x.astype(jnp.float32)).astype(jnp.bfloat16)
    mixed_in = jnp.dot(normed.reshape(-1, width), w_uvqk, preferred_element_type=jnp.float32)
    projected = jax.nn.silu(mixed_in).astype(jnp.bfloat16).reshape(users_here, cand_rows, 4, width)
    projected, second_out = lax.optimization_barrier((projected, sending[1]))
    second_in = req_a2a(second_out, 0)
    halves = [
        first_in.reshape(req_count * capacity, sub, 2 * width),
        second_in.reshape(req_count * capacity, sub, 2 * width),
    ]
    u_gate = projected[:, :, 0]
    v_self = projected[:, :, 1]
    queries = projected[:, :, 2]
    k_self = projected[:, :, 3]
    my_user = hist_index // heads
    my_length = lax.dynamic_slice_in_dim(lengths, my_user, 1)
    q_row = 2 * per_hist * sub
    packed_a = lax.all_to_all(
        pack_for_heads(picked_slot, halves[0], queries, users_here, heads),
        "hist", split_axis=0, concat_axis=0, tiled=True,
    )
    history_mine = attend(my_length, packed_a, packed_a, q_row, per_hist, sub, tile_len, 0, score_scale)
    packed_b = lax.all_to_all(
        pack_for_heads(picked_slot, halves[1], None, users_here, heads),
        "hist", split_axis=0, concat_axis=0, tiled=True,
    )
    history_mine = attend(
        my_length, packed_b, packed_a, q_row, per_hist, sub, tile_len, sub, score_scale, init=history_mine
    ).astype(jnp.bfloat16)
    history_back = lax.all_to_all(
        history_mine.reshape(hist_count, cand_rows, head_dim), "hist", split_axis=0, concat_axis=0, tiled=True
    )
    row_limit = (live_counts - hist_index * cand_rows).astype(jnp.int32)
    return finish(
        history_back, projected.reshape(users_here, cand_rows, 4 * width), cand_x, w_out, self_bias,
        lengths.astype(jnp.int32), row_limit, heads, score_scale,
    )


def solution(mesh):
    return jax.shard_map(
        local,
        mesh=mesh,
        in_specs=(
            P("req", "hist", None),
            P(("req", "hist"), None, None),
            P(),
            P(),
            P(),
            P(),
            P(),
            P(),
            P(),
        ),
        out_specs=P("req", "hist", None),
        check_vma=False,
    )
```

```python
import functools
import math

import jax
import jax.numpy as jnp
from jax import lax
from jax.experimental import pallas as pl
from jax.experimental.pallas import tpu as pltpu
from jax.sharding import PartitionSpec as P


def layer_norm(values):
    mean_value = jnp.mean(values, axis=-1, keepdims=True)
    centred = values - mean_value
    spread = jnp.mean(centred * centred, axis=-1, keepdims=True)
    return centred * lax.rsqrt(spread + 1e-05)


def silu_tanh(values):
    return values * (0.5 + 0.5 * jnp.tanh(0.5 * values))


def req_a2a_kernel(send_ref, recv_ref, send_sem, recv_sem, local_sem, *, axis, other_axis):
    n = send_ref.shape[0]
    me = lax.axis_index(axis)
    other = lax.axis_index(other_axis)
    barrier = pltpu.get_barrier_semaphore()
    for k in range(1, n):
        peer = lax.rem(me + k, n)
        pl.semaphore_signal(
            barrier, inc=1, device_id={axis: peer, other_axis: other}, device_id_type=pl.DeviceIdType.MESH
        )
    pl.semaphore_wait(barrier, n - 1)
    copies = []
    for k in range(1, n):
        peer = lax.rem(me + k, n)
        copy = pltpu.make_async_remote_copy(
            src_ref=send_ref.at[peer],
            dst_ref=recv_ref.at[me],
            send_sem=send_sem.at[k],
            recv_sem=recv_sem.at[k],
            device_id={axis: peer, other_axis: other},
            device_id_type=pl.DeviceIdType.MESH,
        )
        copy.start()
        copies.append(copy)
    own = pltpu.make_async_copy(send_ref.at[me], recv_ref.at[me], local_sem)
    own.start()
    own.wait()
    for copy in copies:
        copy.wait_send()
    for k in range(1, n):
        src = lax.rem(me + n - k, n)
        pltpu.make_async_remote_copy(
            src_ref=send_ref.at[src],
            dst_ref=recv_ref.at[src],
            send_sem=send_sem.at[k],
            recv_sem=recv_sem.at[k],
            device_id={axis: src, other_axis: other},
            device_id_type=pl.DeviceIdType.MESH,
        ).wait_recv()


def req_a2a(x, collective_id):
    n = x.shape[0]
    return pl.pallas_call(
        functools.partial(req_a2a_kernel, axis="req", other_axis="hist"),
        out_shape=jax.ShapeDtypeStruct(x.shape, x.dtype),
        in_specs=[pl.BlockSpec(memory_space=pl.ANY)],
        out_specs=pl.BlockSpec(memory_space=pl.ANY),
        scratch_shapes=[
            pltpu.SemaphoreType.DMA((n,)),
            pltpu.SemaphoreType.DMA((n,)),
            pltpu.SemaphoreType.DMA(()),
        ],
        compiler_params=pltpu.CompilerParams(collective_id=collective_id, has_side_effects=True),
    )(x)


def attend_kernel(len_ref, kv_ref, qsrc_ref, *rest, n_tiles, sub, tile_len, offset, q_row, score_scale, chunk):
    if len(rest) == 3:
        init_ref, o_ref, q_ref = rest
    else:
        init_ref = None
        o_ref, q_ref = rest
    length = len_ref[0]
    n_cls, _, head_dim = kv_ref.shape
    span = n_tiles * sub
    block = q_ref.shape[0] // n_cls
    half_scale = 0.5 * score_scale
    for b in range(n_cls):
        q_ref[pl.ds(b * block, block), :] = qsrc_ref[b]
    if init_ref is None:
        o_ref[...] = jnp.zeros_like(o_ref)
    else:
        o_ref[...] = init_ref[...]

    def one_class(c, carry):
        key_index = lax.broadcasted_iota(jnp.int32, (1, span), 1)
        position = (c + n_cls * (key_index // sub)) * tile_len + offset + key_index % sub
        live = position < length

        def add_class(masked):
            keys = kv_ref[c, pl.ds(0, span), :]
            values = kv_ref[c, pl.ds(span, span), :]
            for ci in range(q_ref.shape[0] // chunk):
                rows = pl.ds(ci * chunk, chunk)
                scores = lax.dot_general(
                    q_ref[rows, :], keys, (((1,), (1,)), ((), ())), preferred_element_type=jnp.float32
                )
                half = scores * half_scale
                weights = half + half * jnp.tanh(half)
                if masked:
                    weights = jnp.where(live, weights, 0.0)
                o_ref[rows, :] += jnp.dot(weights.astype(jnp.bfloat16), values, preferred_element_type=jnp.float32)

        last_key = (c + n_cls * (n_tiles - 1)) * tile_len + offset + sub
        whole = last_key <= length
        pl.when(whole)(lambda: add_class(False))
        pl.when(jnp.logical_and(jnp.logical_not(whole), c * tile_len + offset < length))(lambda: add_class(True))
        return carry

    lax.fori_loop(0, n_cls, one_class, 0)


def attend(length, kv_packed, q_packed, q_row, n_tiles, sub, tile_len, offset, score_scale, init=None):
    n_cls, _, head_dim = q_packed.shape
    rows = n_cls * (q_packed.shape[1] - q_row)
    chunk = 2048
    kernel = functools.partial(
        attend_kernel,
        n_tiles=n_tiles,
        sub=sub,
        tile_len=tile_len,
        offset=offset,
        q_row=q_row,
        score_scale=score_scale,
        chunk=chunk,
    )
    return pl.pallas_call(
        kernel,
        grid=(1,),
        out_shape=jax.ShapeDtypeStruct((rows, head_dim), jnp.float32),
        in_specs=[
            pl.BlockSpec(memory_space=pltpu.SMEM),
            pl.BlockSpec(memory_space=pltpu.VMEM),
            pl.BlockSpec((n_cls, rows // n_cls, head_dim), lambda i: (0, q_row // (rows // n_cls), 0)),
        ]
        + ([] if init is None else [pl.BlockSpec(memory_space=pltpu.VMEM)]),
        out_specs=pl.BlockSpec(memory_space=pltpu.VMEM),
        scratch_shapes=[pltpu.VMEM((rows, head_dim), jnp.bfloat16)],
    )(length, kv_packed, q_packed, *([] if init is None else [init]))


def pack_kernel(picked_ref, tiles_hbm, *rest, heads, users, per_hist, with_q):
    if with_q:
        q_ref, out_ref, staged, in_sem = rest
    else:
        out_ref, staged, in_sem = rest
    width = tiles_hbm.shape[2] // 2
    head_dim = width // heads
    sub = tiles_hbm.shape[1]
    span = per_hist * sub
    n_in = users * per_hist
    reads = []
    for i in range(n_in):
        read = pltpu.make_async_copy(tiles_hbm.at[picked_ref[i]], staged.at[i], in_sem.at[i])
        read.start()
        reads.append(read)
    if with_q:
        cand_rows = q_ref.shape[1]
        for u in range(users):
            for e in range(heads):
                out_ref[u * heads + e, pl.ds(2 * span, cand_rows), :] = q_ref[u, :, pl.ds(e * head_dim, head_dim)]
    for i in range(n_in):
        u, t = divmod(i, per_hist)
        reads[i].wait()
        for piece in range(2 * heads):
            e, kv = divmod(piece, 2)
            out_ref[u * heads + e, pl.ds(kv * span + t * sub, sub), :] = staged[
                i, :, pl.ds(piece * head_dim, head_dim)
            ]


def pack_for_heads(picked_slot, tiles, queries, users, heads):
    n_in = picked_slot.shape[0]
    per_hist = n_in // users
    sub, wide = tiles.shape[1], tiles.shape[2]
    head_dim = wide // (2 * heads)
    rows = 2 * per_hist * sub + (0 if queries is None else queries.shape[1])
    operands = [picked_slot, tiles] + ([] if queries is None else [queries])
    return pl.pallas_call(
        functools.partial(pack_kernel, heads=heads, users=users, per_hist=per_hist, with_q=queries is not None),
        out_shape=jax.ShapeDtypeStruct((users * heads, rows, head_dim), tiles.dtype),
        in_specs=[pl.BlockSpec(memory_space=pltpu.SMEM), pl.BlockSpec(memory_space=pl.ANY)]
        + ([] if queries is None else [pl.BlockSpec(memory_space=pltpu.VMEM)]),
        out_specs=pl.BlockSpec(memory_space=pltpu.VMEM),
        scratch_shapes=[
            pltpu.VMEM((n_in, sub, wide), tiles.dtype),
            pltpu.SemaphoreType.DMA((n_in,)),
        ],
    )(*operands)


def finish_kernel(
    bias_ref, len_ref, limit_ref, hist_ref, proj_ref, x_ref, w_ref, out_ref, att_ref, *, heads, score_scale
):
    users, rows, width = x_ref.shape
    head_dim = width // heads
    for u in range(users):
        divisor = (len_ref[u] + 1).astype(jnp.float32)
        for e in range(heads):
            value = proj_ref[u, :, pl.ds(width + e * head_dim, head_dim)].astype(jnp.float32)
            query = proj_ref[u, :, pl.ds(2 * width + e * head_dim, head_dim)].astype(jnp.float32)
            key = proj_ref[u, :, pl.ds(3 * width + e * head_dim, head_dim)].astype(jnp.float32)
            self_score = jnp.sum(query * key, axis=-1, keepdims=True) * score_scale + bias_ref[e]
            own = self_score * (0.5 + 0.5 * jnp.tanh(0.5 * self_score)) * value
            history = hist_ref[u * heads + e].astype(jnp.float32)
            att_ref[:, pl.ds(e * head_dim, head_dim)] = (history + own) / divisor
        attended = att_ref[...]
        centred = attended - jnp.mean(attended, axis=-1, keepdims=True)
        spread = jnp.mean(centred * centred, axis=-1, keepdims=True)
        gate = proj_ref[u, :, pl.ds(0, width)].astype(jnp.float32)
        gated = (centred * lax.rsqrt(spread + 1e-05) * gate).astype(jnp.bfloat16)
        result = x_ref[u].astype(jnp.float32) + jnp.dot(gated, w_ref[...], preferred_element_type=jnp.float32)
        row = lax.broadcasted_iota(jnp.int32, (rows, 1), 0)
        out_ref[u] = jnp.where(row < limit_ref[u], result, 0.0).astype(out_ref.dtype)


def finish(history_back, projected, cand_x, w_out, self_bias, lengths, row_limit, heads, score_scale):
    users, rows, width = cand_x.shape
    smem = pl.BlockSpec(memory_space=pltpu.SMEM)
    vmem = pl.BlockSpec(memory_space=pltpu.VMEM)
    return pl.pallas_call(
        functools.partial(finish_kernel, heads=heads, score_scale=score_scale),
        out_shape=jax.ShapeDtypeStruct(cand_x.shape, cand_x.dtype),
        in_specs=[smem, smem, smem, vmem, vmem, vmem, vmem],
        out_specs=vmem,
        scratch_shapes=[pltpu.VMEM((rows, width), jnp.float32)],
    )(self_bias, lengths, row_limit, history_back, projected, cand_x, w_out)


def local(cand_x, kv_cache, w_uvqk, w_out, self_bias, user_rank, hist_len, cand_count, tile_slot):
    users_here, cand_rows, width = cand_x.shape
    heads = self_bias.shape[0]
    head_dim = width // heads
    score_scale = 1.0 / math.sqrt(head_dim)
    slots_own, tile_len, _ = kv_cache.shape
    user_total, tiles_max = tile_slot.shape
    req_count = lax.axis_size("req")
    hist_count = lax.axis_size("hist")
    req_index = lax.axis_index("req")
    hist_index = lax.axis_index("hist")
    per_hist = tiles_max // hist_count
    capacity = slots_own // req_count + 1
    first_slot = req_index * users_here
    user_ids = lax.dynamic_slice_in_dim(user_rank, first_slot, users_here)
    match_user = user_ids[:, None] == jnp.arange(user_total)[None, :]
    lengths = jnp.sum(jnp.where(match_user, hist_len[None, :], 0), axis=1)
    live_counts = jnp.sum(jnp.where(match_user, cand_count[None, :], 0), axis=1)
    column = lax.dynamic_index_in_dim(
        tile_slot.reshape(user_total, per_hist, hist_count), hist_index, axis=2, keepdims=False
    )
    codes = column.reshape(-1)
    owners = codes // slots_own
    local_slot = codes % slots_own
    dests = jnp.repeat(jnp.arange(user_total) // users_here, per_hist)
    entry_ids = jnp.arange(codes.shape[0])
    same_pair = (
        (owners[:, None] == owners[None, :])
        & (dests[:, None] == dests[None, :])
        & (entry_ids[:, None] > entry_ids[None, :])
    )
    places = jnp.sum(jnp.where(same_pair, 1, 0), axis=1)
    picked = (
        (owners[None, None, :] == req_index)
        & (dests[None, None, :] == jnp.arange(req_count)[:, None, None])
        & (places[None, None, :] == jnp.arange(capacity)[None, :, None])
    )
    source_slot = jnp.sum(jnp.where(picked, local_slot[None, None, :], 0), axis=2).reshape(-1)
    first_entry = first_slot * per_hist
    my_owner = lax.dynamic_slice_in_dim(owners, first_entry, users_here * per_hist)
    my_place = lax.dynamic_slice_in_dim(places, first_entry, users_here * per_hist)
    picked_slot = (my_owner * capacity + my_place).astype(jnp.int32)
    sub = tile_len // 2
    sending = []
    for half in range(2):
        kv_half = lax.slice_in_dim(kv_cache, half * sub, (half + 1) * sub, axis=1)
        outgoing = kv_half.at[source_slot].get(mode="promise_in_bounds")
        sending.append(outgoing.reshape(req_count, capacity, sub, 2 * width))
    first_in = lax.all_to_all(sending[0], "req", split_axis=0, concat_axis=0, tiled=True)
    normed = layer_norm(cand_x.astype(jnp.float32)).astype(jnp.bfloat16)
    mixed_in = jnp.dot(normed.reshape(-1, width), w_uvqk, preferred_element_type=jnp.float32)
    projected = jax.nn.silu(mixed_in).astype(jnp.bfloat16).reshape(users_here, cand_rows, 4, width)
    projected, second_out = lax.optimization_barrier((projected, sending[1]))
    second_in = req_a2a(second_out, 0)
    halves = [
        first_in.reshape(req_count * capacity, sub, 2 * width),
        second_in.reshape(req_count * capacity, sub, 2 * width),
    ]
    u_gate = projected[:, :, 0]
    v_self = projected[:, :, 1]
    queries = projected[:, :, 2]
    k_self = projected[:, :, 3]
    my_user = hist_index // heads
    my_length = lax.dynamic_slice_in_dim(lengths, my_user, 1)
    q_row = 2 * per_hist * sub
    packed_a = lax.all_to_all(
        pack_for_heads(picked_slot, halves[0], queries, users_here, heads),
        "hist", split_axis=0, concat_axis=0, tiled=True,
    )
    history_mine = attend(my_length, packed_a, packed_a, q_row, per_hist, sub, tile_len, 0, score_scale)
    packed_b = lax.all_to_all(
        pack_for_heads(picked_slot, halves[1], None, users_here, heads),
        "hist", split_axis=0, concat_axis=0, tiled=True,
    )
    history_mine = attend(
        my_length, packed_b, packed_a, q_row, per_hist, sub, tile_len, sub, score_scale, init=history_mine
    ).astype(jnp.bfloat16)
    history_back = lax.all_to_all(
        history_mine.reshape(hist_count, cand_rows, head_dim), "hist", split_axis=0, concat_axis=0, tiled=True
    )
    row_limit = (live_counts - hist_index * cand_rows).astype(jnp.int32)
    return finish(
        history_back, projected.reshape(users_here, cand_rows, 4 * width), cand_x, w_out, self_bias,
        lengths.astype(jnp.int32), row_limit, heads, score_scale,
    )


def solution(mesh):
    return jax.shard_map(
        local,
        mesh=mesh,
        in_specs=(
            P("req", "hist", None),
            P(("req", "hist"), None, None),
            P(),
            P(),
            P(),
            P(),
            P(),
            P(),
            P(),
        ),
        out_specs=P("req", "hist", None),
        check_vma=False,
    )
```

```python
import functools
import math

import jax
import jax.numpy as jnp
from jax import lax
from jax.experimental import pallas as pl
from jax.experimental.pallas import tpu as pltpu
from jax.sharding import PartitionSpec as P


def layer_norm(values):
    mean_value = jnp.mean(values, axis=-1, keepdims=True)
    centred = values - mean_value
    spread = jnp.mean(centred * centred, axis=-1, keepdims=True)
    return centred * lax.rsqrt(spread + 1e-05)


def silu_tanh(values):
    return values * (0.5 + 0.5 * jnp.tanh(0.5 * values))


def req_a2a_kernel(send_ref, recv_ref, send_sem, recv_sem, local_sem, *, axis, other_axis):
    n = send_ref.shape[0]
    me = lax.axis_index(axis)
    other = lax.axis_index(other_axis)
    barrier = pltpu.get_barrier_semaphore()
    for k in range(1, n):
        peer = lax.rem(me + k, n)
        pl.semaphore_signal(
            barrier, inc=1, device_id={axis: peer, other_axis: other}, device_id_type=pl.DeviceIdType.MESH
        )
    pl.semaphore_wait(barrier, n - 1)
    copies = []
    for k in range(1, n):
        peer = lax.rem(me + k, n)
        copy = pltpu.make_async_remote_copy(
            src_ref=send_ref.at[peer],
            dst_ref=recv_ref.at[me],
            send_sem=send_sem.at[k],
            recv_sem=recv_sem.at[k],
            device_id={axis: peer, other_axis: other},
            device_id_type=pl.DeviceIdType.MESH,
        )
        copy.start()
        copies.append(copy)
    own = pltpu.make_async_copy(send_ref.at[me], recv_ref.at[me], local_sem)
    own.start()
    own.wait()
    for copy in copies:
        copy.wait_send()
    for k in range(1, n):
        src = lax.rem(me + n - k, n)
        pltpu.make_async_remote_copy(
            src_ref=send_ref.at[src],
            dst_ref=recv_ref.at[src],
            send_sem=send_sem.at[k],
            recv_sem=recv_sem.at[k],
            device_id={axis: src, other_axis: other},
            device_id_type=pl.DeviceIdType.MESH,
        ).wait_recv()


def req_a2a(x, collective_id):
    n = x.shape[0]
    return pl.pallas_call(
        functools.partial(req_a2a_kernel, axis="req", other_axis="hist"),
        out_shape=jax.ShapeDtypeStruct(x.shape, x.dtype),
        in_specs=[pl.BlockSpec(memory_space=pl.ANY)],
        out_specs=pl.BlockSpec(memory_space=pl.ANY),
        scratch_shapes=[
            pltpu.SemaphoreType.DMA((n,)),
            pltpu.SemaphoreType.DMA((n,)),
            pltpu.SemaphoreType.DMA(()),
        ],
        compiler_params=pltpu.CompilerParams(collective_id=collective_id, has_side_effects=True),
    )(x)


def attend_kernel(len_ref, kv_ref, qsrc_ref, *rest, n_tiles, sub, tile_len, offset, q_row, score_scale, chunk):
    if len(rest) == 3:
        init_ref, o_ref, q_ref = rest
    else:
        init_ref = None
        o_ref, q_ref = rest
    length = len_ref[0]
    n_cls, _, head_dim = kv_ref.shape
    span = n_tiles * sub
    block = q_ref.shape[0] // n_cls
    half_scale = 0.5 * score_scale
    for b in range(n_cls):
        q_ref[pl.ds(b * block, block), :] = qsrc_ref[b, pl.ds(q_row, block), :]
    if init_ref is None:
        o_ref[...] = jnp.zeros_like(o_ref)
    else:
        o_ref[...] = init_ref[...]

    def one_class(c, carry):
        key_index = lax.broadcasted_iota(jnp.int32, (1, span), 1)
        position = (c + n_cls * (key_index // sub)) * tile_len + offset + key_index % sub
        live = position < length

        def add_class(masked):
            keys = kv_ref[c, pl.ds(0, span), :]
            values = kv_ref[c, pl.ds(span, span), :]
            for ci in range(q_ref.shape[0] // chunk):
                rows = pl.ds(ci * chunk, chunk)
                scores = lax.dot_general(
                    q_ref[rows, :], keys, (((1,), (1,)), ((), ())), preferred_element_type=jnp.float32
                )
                half = scores * half_scale
                weights = half + half * jnp.tanh(half)
                if masked:
                    weights = jnp.where(live, weights, 0.0)
                o_ref[rows, :] += jnp.dot(weights.astype(jnp.bfloat16), values, preferred_element_type=jnp.float32)

        last_key = (c + n_cls * (n_tiles - 1)) * tile_len + offset + sub
        whole = last_key <= length
        pl.when(whole)(lambda: add_class(False))
        pl.when(jnp.logical_and(jnp.logical_not(whole), c * tile_len + offset < length))(lambda: add_class(True))
        return carry

    lax.fori_loop(0, n_cls, one_class, 0)


def attend(length, kv_packed, q_packed, q_row, n_tiles, sub, tile_len, offset, score_scale, init=None):
    n_cls, _, head_dim = q_packed.shape
    rows = n_cls * (q_packed.shape[1] - q_row)
    chunk = 2048
    kernel = functools.partial(
        attend_kernel,
        n_tiles=n_tiles,
        sub=sub,
        tile_len=tile_len,
        offset=offset,
        q_row=q_row,
        score_scale=score_scale,
        chunk=chunk,
    )
    return pl.pallas_call(
        kernel,
        out_shape=jax.ShapeDtypeStruct((rows, head_dim), jnp.float32),
        in_specs=[pl.BlockSpec(memory_space=pltpu.SMEM)]
        + [pl.BlockSpec(memory_space=pltpu.VMEM)] * (2 if init is None else 3),
        out_specs=pl.BlockSpec(memory_space=pltpu.VMEM),
        scratch_shapes=[pltpu.VMEM((rows, head_dim), jnp.bfloat16)],
    )(length, kv_packed, q_packed, *([] if init is None else [init]))


def pack_kernel(picked_ref, tiles_hbm, *rest, heads, users, per_hist, with_q):
    if with_q:
        q_ref, out_ref, staged, in_sem = rest
    else:
        out_ref, staged, in_sem = rest
    width = tiles_hbm.shape[2] // 2
    head_dim = width // heads
    sub = tiles_hbm.shape[1]
    span = per_hist * sub
    n_in = users * per_hist
    reads = []
    for i in range(n_in):
        read = pltpu.make_async_copy(tiles_hbm.at[picked_ref[i]], staged.at[i], in_sem.at[i])
        read.start()
        reads.append(read)
    if with_q:
        cand_rows = q_ref.shape[1]
        for u in range(users):
            for e in range(heads):
                out_ref[u * heads + e, pl.ds(2 * span, cand_rows), :] = q_ref[u, :, pl.ds(e * head_dim, head_dim)]
    for i in range(n_in):
        u, t = divmod(i, per_hist)
        reads[i].wait()
        for piece in range(2 * heads):
            e, kv = divmod(piece, 2)
            out_ref[u * heads + e, pl.ds(kv * span + t * sub, sub), :] = staged[
                i, :, pl.ds(piece * head_dim, head_dim)
            ]


def pack_for_heads(picked_slot, tiles, queries, users, heads):
    n_in = picked_slot.shape[0]
    per_hist = n_in // users
    sub, wide = tiles.shape[1], tiles.shape[2]
    head_dim = wide // (2 * heads)
    rows = 2 * per_hist * sub + (0 if queries is None else queries.shape[1])
    operands = [picked_slot, tiles] + ([] if queries is None else [queries])
    return pl.pallas_call(
        functools.partial(pack_kernel, heads=heads, users=users, per_hist=per_hist, with_q=queries is not None),
        out_shape=jax.ShapeDtypeStruct((users * heads, rows, head_dim), tiles.dtype),
        in_specs=[pl.BlockSpec(memory_space=pltpu.SMEM), pl.BlockSpec(memory_space=pl.ANY)]
        + ([] if queries is None else [pl.BlockSpec(memory_space=pltpu.VMEM)]),
        out_specs=pl.BlockSpec(memory_space=pltpu.VMEM),
        scratch_shapes=[
            pltpu.VMEM((n_in, sub, wide), tiles.dtype),
            pltpu.SemaphoreType.DMA((n_in,)),
        ],
    )(*operands)


def finish_kernel(
    bias_ref, len_ref, limit_ref, hist_ref, proj_ref, x_ref, w_ref, out_ref, att_ref, *, heads, score_scale
):
    _, rows, width = x_ref.shape
    head_dim = width // heads
    u = pl.program_id(0)
    divisor = (len_ref[u] + 1).astype(jnp.float32)
    for e in range(heads):
        value = proj_ref[0, :, pl.ds(width + e * head_dim, head_dim)].astype(jnp.float32)
        query = proj_ref[0, :, pl.ds(2 * width + e * head_dim, head_dim)].astype(jnp.float32)
        key = proj_ref[0, :, pl.ds(3 * width + e * head_dim, head_dim)].astype(jnp.float32)
        self_score = jnp.sum(query * key, axis=-1, keepdims=True) * score_scale + bias_ref[e]
        own = self_score * (0.5 + 0.5 * jnp.tanh(0.5 * self_score)) * value
        history = hist_ref[e].astype(jnp.float32)
        att_ref[:, pl.ds(e * head_dim, head_dim)] = (history + own) / divisor
    attended = att_ref[...]
    centred = attended - jnp.mean(attended, axis=-1, keepdims=True)
    spread = jnp.mean(centred * centred, axis=-1, keepdims=True)
    gate = proj_ref[0, :, pl.ds(0, width)].astype(jnp.float32)
    gated = (centred * lax.rsqrt(spread + 1e-05) * gate).astype(jnp.bfloat16)
    result = x_ref[0].astype(jnp.float32) + jnp.dot(gated, w_ref[...], preferred_element_type=jnp.float32)
    row = lax.broadcasted_iota(jnp.int32, (rows, 1), 0)
    out_ref[0] = jnp.where(row < limit_ref[u], result, 0.0).astype(out_ref.dtype)


def finish(history_back, projected, cand_x, w_out, self_bias, lengths, row_limit, heads, score_scale):
    users, rows, width = cand_x.shape
    head_dim = width // heads
    smem = pl.BlockSpec(memory_space=pltpu.SMEM)
    return pl.pallas_call(
        functools.partial(finish_kernel, heads=heads, score_scale=score_scale),
        grid=(users,),
        out_shape=jax.ShapeDtypeStruct(cand_x.shape, cand_x.dtype),
        in_specs=[
            smem,
            smem,
            smem,
            pl.BlockSpec((heads, rows, head_dim), lambda u: (u, 0, 0)),
            pl.BlockSpec((1, rows, projected.shape[2]), lambda u: (u, 0, 0)),
            pl.BlockSpec((1, rows, width), lambda u: (u, 0, 0)),
            pl.BlockSpec((width, width), lambda u: (0, 0)),
        ],
        out_specs=pl.BlockSpec((1, rows, width), lambda u: (u, 0, 0)),
        scratch_shapes=[pltpu.VMEM((rows, width), jnp.float32)],
    )(self_bias, lengths, row_limit, history_back, projected, cand_x, w_out)


def local(cand_x, kv_cache, w_uvqk, w_out, self_bias, user_rank, hist_len, cand_count, tile_slot):
    users_here, cand_rows, width = cand_x.shape
    heads = self_bias.shape[0]
    head_dim = width // heads
    score_scale = 1.0 / math.sqrt(head_dim)
    slots_own, tile_len, _ = kv_cache.shape
    user_total, tiles_max = tile_slot.shape
    req_count = lax.axis_size("req")
    hist_count = lax.axis_size("hist")
    req_index = lax.axis_index("req")
    hist_index = lax.axis_index("hist")
    per_hist = tiles_max // hist_count
    capacity = slots_own // req_count + 1
    first_slot = req_index * users_here
    user_ids = lax.dynamic_slice_in_dim(user_rank, first_slot, users_here)
    match_user = user_ids[:, None] == jnp.arange(user_total)[None, :]
    lengths = jnp.sum(jnp.where(match_user, hist_len[None, :], 0), axis=1)
    live_counts = jnp.sum(jnp.where(match_user, cand_count[None, :], 0), axis=1)
    column = lax.dynamic_index_in_dim(
        tile_slot.reshape(user_total, per_hist, hist_count), hist_index, axis=2, keepdims=False
    )
    codes = column.reshape(-1)
    owners = codes // slots_own
    local_slot = codes % slots_own
    dests = jnp.repeat(jnp.arange(user_total) // users_here, per_hist)
    entry_ids = jnp.arange(codes.shape[0])
    same_pair = (
        (owners[:, None] == owners[None, :])
        & (dests[:, None] == dests[None, :])
        & (entry_ids[:, None] > entry_ids[None, :])
    )
    places = jnp.sum(jnp.where(same_pair, 1, 0), axis=1)
    picked = (
        (owners[None, None, :] == req_index)
        & (dests[None, None, :] == jnp.arange(req_count)[:, None, None])
        & (places[None, None, :] == jnp.arange(capacity)[None, :, None])
    )
    source_slot = jnp.sum(jnp.where(picked, local_slot[None, None, :], 0), axis=2).reshape(-1)
    first_entry = first_slot * per_hist
    my_owner = lax.dynamic_slice_in_dim(owners, first_entry, users_here * per_hist)
    my_place = lax.dynamic_slice_in_dim(places, first_entry, users_here * per_hist)
    picked_slot = (my_owner * capacity + my_place).astype(jnp.int32)
    sub = tile_len // 2
    sending = []
    for half in range(2):
        kv_half = lax.slice_in_dim(kv_cache, half * sub, (half + 1) * sub, axis=1)
        outgoing = kv_half.at[source_slot].get(mode="promise_in_bounds")
        sending.append(outgoing.reshape(req_count, capacity, sub, 2 * width))
    first_in = lax.all_to_all(sending[0], "req", split_axis=0, concat_axis=0, tiled=True)
    normed = layer_norm(cand_x.astype(jnp.float32)).astype(jnp.bfloat16)
    mixed_in = jnp.dot(normed.reshape(-1, width), w_uvqk, preferred_element_type=jnp.float32)
    projected = jax.nn.silu(mixed_in).astype(jnp.bfloat16).reshape(users_here, cand_rows, 4, width)
    projected, second_out = lax.optimization_barrier((projected, sending[1]))
    second_in = req_a2a(second_out, 0)
    halves = [
        first_in.reshape(req_count * capacity, sub, 2 * width),
        second_in.reshape(req_count * capacity, sub, 2 * width),
    ]
    u_gate = projected[:, :, 0]
    v_self = projected[:, :, 1]
    queries = projected[:, :, 2]
    k_self = projected[:, :, 3]
    my_user = hist_index // heads
    my_length = lax.dynamic_slice_in_dim(lengths, my_user, 1)
    q_row = 2 * per_hist * sub
    packed_a = lax.all_to_all(
        pack_for_heads(picked_slot, halves[0], queries, users_here, heads),
        "hist", split_axis=0, concat_axis=0, tiled=True,
    )
    history_mine = attend(my_length, packed_a, packed_a, q_row, per_hist, sub, tile_len, 0, score_scale)
    packed_b = lax.all_to_all(
        pack_for_heads(picked_slot, halves[1], None, users_here, heads),
        "hist", split_axis=0, concat_axis=0, tiled=True,
    )
    history_mine = attend(
        my_length, packed_b, packed_a, q_row, per_hist, sub, tile_len, sub, score_scale, init=history_mine
    ).astype(jnp.bfloat16)
    history_back = lax.all_to_all(
        history_mine.reshape(hist_count, cand_rows, head_dim), "hist", split_axis=0, concat_axis=0, tiled=True
    )
    row_limit = (live_counts - hist_index * cand_rows).astype(jnp.int32)
    return finish(
        history_back, projected.reshape(users_here, cand_rows, 4 * width), cand_x, w_out, self_bias,
        lengths.astype(jnp.int32), row_limit, heads, score_scale,
    )


def solution(mesh):
    return jax.shard_map(
        local,
        mesh=mesh,
        in_specs=(
            P("req", "hist", None),
            P(("req", "hist"), None, None),
            P(),
            P(),
            P(),
            P(),
            P(),
            P(),
            P(),
        ),
        out_specs=P("req", "hist", None),
        check_vma=False,
    )
```

```python
import functools
import math

import jax
import jax.numpy as jnp
from jax import lax
from jax.experimental import pallas as pl
from jax.experimental.pallas import tpu as pltpu
from jax.sharding import PartitionSpec as P


def layer_norm(values):
    mean_value = jnp.mean(values, axis=-1, keepdims=True)
    centred = values - mean_value
    spread = jnp.mean(centred * centred, axis=-1, keepdims=True)
    return centred * lax.rsqrt(spread + 1e-05)


def silu_tanh(values):
    return values * (0.5 + 0.5 * jnp.tanh(0.5 * values))


def req_a2a_kernel(send_ref, recv_ref, send_sem, recv_sem, local_sem, *, axis, other_axis):
    n = send_ref.shape[0]
    me = lax.axis_index(axis)
    other = lax.axis_index(other_axis)
    barrier = pltpu.get_barrier_semaphore()
    for k in range(1, n):
        peer = lax.rem(me + k, n)
        pl.semaphore_signal(
            barrier, inc=1, device_id={axis: peer, other_axis: other}, device_id_type=pl.DeviceIdType.MESH
        )
    pl.semaphore_wait(barrier, n - 1)
    copies = []
    for k in range(1, n):
        peer = lax.rem(me + k, n)
        copy = pltpu.make_async_remote_copy(
            src_ref=send_ref.at[peer],
            dst_ref=recv_ref.at[me],
            send_sem=send_sem.at[k],
            recv_sem=recv_sem.at[k],
            device_id={axis: peer, other_axis: other},
            device_id_type=pl.DeviceIdType.MESH,
        )
        copy.start()
        copies.append(copy)
    own = pltpu.make_async_copy(send_ref.at[me], recv_ref.at[me], local_sem)
    own.start()
    own.wait()
    for copy in copies:
        copy.wait_send()
    for k in range(1, n):
        src = lax.rem(me + n - k, n)
        pltpu.make_async_remote_copy(
            src_ref=send_ref.at[src],
            dst_ref=recv_ref.at[src],
            send_sem=send_sem.at[k],
            recv_sem=recv_sem.at[k],
            device_id={axis: src, other_axis: other},
            device_id_type=pl.DeviceIdType.MESH,
        ).wait_recv()


def req_a2a(x, collective_id):
    n = x.shape[0]
    return pl.pallas_call(
        functools.partial(req_a2a_kernel, axis="req", other_axis="hist"),
        out_shape=jax.ShapeDtypeStruct(x.shape, x.dtype),
        in_specs=[pl.BlockSpec(memory_space=pl.ANY)],
        out_specs=pl.BlockSpec(memory_space=pl.ANY),
        scratch_shapes=[
            pltpu.SemaphoreType.DMA((n,)),
            pltpu.SemaphoreType.DMA((n,)),
            pltpu.SemaphoreType.DMA(()),
        ],
        compiler_params=pltpu.CompilerParams(collective_id=collective_id, has_side_effects=True),
    )(x)


def attend_kernel(len_ref, kv_ref, qsrc_ref, *rest, n_tiles, sub, tile_len, offset, q_row, score_scale, chunk):
    if len(rest) == 3:
        init_ref, o_ref, q_ref = rest
    else:
        init_ref = None
        o_ref, q_ref = rest
    length = len_ref[0]
    n_cls, _, head_dim = kv_ref.shape
    span = n_tiles * sub
    block = q_ref.shape[0] // n_cls
    half_scale = 0.5 * score_scale
    for b in range(n_cls):
        q_ref[pl.ds(b * block, block), :] = qsrc_ref[b, pl.ds(q_row, block), :]
    if init_ref is None:
        o_ref[...] = jnp.zeros_like(o_ref)
    else:
        o_ref[...] = init_ref[...]

    def one_class(c, carry):
        key_index = lax.broadcasted_iota(jnp.int32, (1, span), 1)
        position = (c + n_cls * (key_index // sub)) * tile_len + offset + key_index % sub
        live = position < length

        def add_class(masked):
            keys = kv_ref[c, pl.ds(0, span), :]
            values = kv_ref[c, pl.ds(span, span), :]
            for ci in range(q_ref.shape[0] // chunk):
                rows = pl.ds(ci * chunk, chunk)
                scores = lax.dot_general(
                    q_ref[rows, :], keys, (((1,), (1,)), ((), ())), preferred_element_type=jnp.float32
                )
                half = scores * half_scale
                weights = half + half * jnp.tanh(half)
                if masked:
                    weights = jnp.where(live, weights, 0.0)
                o_ref[rows, :] += jnp.dot(weights.astype(jnp.bfloat16), values, preferred_element_type=jnp.float32)

        last_key = (c + n_cls * (n_tiles - 1)) * tile_len + offset + sub
        whole = last_key <= length
        pl.when(whole)(lambda: add_class(False))
        pl.when(jnp.logical_and(jnp.logical_not(whole), c * tile_len + offset < length))(lambda: add_class(True))
        return carry

    lax.fori_loop(0, n_cls, one_class, 0)


def attend(length, kv_packed, q_packed, q_row, n_tiles, sub, tile_len, offset, score_scale, init=None):
    n_cls, _, head_dim = q_packed.shape
    rows = n_cls * (q_packed.shape[1] - q_row)
    chunk = 2048
    kernel = functools.partial(
        attend_kernel,
        n_tiles=n_tiles,
        sub=sub,
        tile_len=tile_len,
        offset=offset,
        q_row=q_row,
        score_scale=score_scale,
        chunk=chunk,
    )
    return pl.pallas_call(
        kernel,
        out_shape=jax.ShapeDtypeStruct((rows, head_dim), jnp.float32),
        in_specs=[pl.BlockSpec(memory_space=pltpu.SMEM)]
        + [pl.BlockSpec(memory_space=pltpu.VMEM)] * (2 if init is None else 3),
        out_specs=pl.BlockSpec(memory_space=pltpu.VMEM),
        scratch_shapes=[pltpu.VMEM((rows, head_dim), jnp.bfloat16)],
    )(length, kv_packed, q_packed, *([] if init is None else [init]))


def pack_kernel(picked_ref, tiles_hbm, *rest, heads, users, per_hist, with_q):
    if with_q:
        q_ref, out_ref, staged, in_sem = rest
    else:
        out_ref, staged, in_sem = rest
    width = tiles_hbm.shape[2] // 2
    head_dim = width // heads
    sub = tiles_hbm.shape[1]
    span = per_hist * sub
    n_in = users * per_hist
    reads = []
    for i in range(n_in):
        read = pltpu.make_async_copy(tiles_hbm.at[picked_ref[i]], staged.at[i], in_sem.at[i])
        read.start()
        reads.append(read)
    if with_q:
        cand_rows = q_ref.shape[1]
        for u in range(users):
            for e in range(heads):
                out_ref[u * heads + e, pl.ds(2 * span, cand_rows), :] = q_ref[u, :, pl.ds(e * head_dim, head_dim)]
    for i in range(n_in):
        u, t = divmod(i, per_hist)
        reads[i].wait()
        for piece in range(2 * heads):
            e, kv = divmod(piece, 2)
            out_ref[u * heads + e, pl.ds(kv * span + t * sub, sub), :] = staged[
                i, :, pl.ds(piece * head_dim, head_dim)
            ]


def pack_for_heads(picked_slot, tiles, queries, users, heads):
    n_in = picked_slot.shape[0]
    per_hist = n_in // users
    sub, wide = tiles.shape[1], tiles.shape[2]
    head_dim = wide // (2 * heads)
    rows = 2 * per_hist * sub + (0 if queries is None else queries.shape[1])
    operands = [picked_slot, tiles] + ([] if queries is None else [queries])
    return pl.pallas_call(
        functools.partial(pack_kernel, heads=heads, users=users, per_hist=per_hist, with_q=queries is not None),
        out_shape=jax.ShapeDtypeStruct((users * heads, rows, head_dim), tiles.dtype),
        in_specs=[pl.BlockSpec(memory_space=pltpu.SMEM), pl.BlockSpec(memory_space=pl.ANY)]
        + ([] if queries is None else [pl.BlockSpec(memory_space=pltpu.VMEM)]),
        out_specs=pl.BlockSpec(memory_space=pltpu.VMEM),
        scratch_shapes=[
            pltpu.VMEM((n_in, sub, wide), tiles.dtype),
            pltpu.SemaphoreType.DMA((n_in,)),
        ],
    )(*operands)


def finish_kernel(
    bias_ref, len_ref, limit_ref, hist_ref, proj_ref, x_ref, w_ref, out_ref, att_ref, *, heads, score_scale
):
    users, rows, width = x_ref.shape
    head_dim = width // heads
    for u in range(users):
        divisor = (len_ref[u] + 1).astype(jnp.float32)
        for e in range(heads):
            value = proj_ref[u, :, pl.ds(width + e * head_dim, head_dim)].astype(jnp.float32)
            query = proj_ref[u, :, pl.ds(2 * width + e * head_dim, head_dim)].astype(jnp.float32)
            key = proj_ref[u, :, pl.ds(3 * width + e * head_dim, head_dim)].astype(jnp.float32)
            self_score = jnp.sum(query * key, axis=-1, keepdims=True) * score_scale + bias_ref[e]
            own = self_score * (0.5 + 0.5 * jnp.tanh(0.5 * self_score)) * value
            history = hist_ref[u * heads + e].astype(jnp.float32)
            att_ref[:, pl.ds(e * head_dim, head_dim)] = (history + own) / divisor
        attended = att_ref[...]
        centred = attended - jnp.mean(attended, axis=-1, keepdims=True)
        spread = jnp.mean(centred * centred, axis=-1, keepdims=True)
        gate = proj_ref[u, :, pl.ds(0, width)].astype(jnp.float32)
        gated = (centred * lax.rsqrt(spread + 1e-05) * gate).astype(jnp.bfloat16)
        result = x_ref[u].astype(jnp.float32) + jnp.dot(gated, w_ref[...], preferred_element_type=jnp.float32)
        row = lax.broadcasted_iota(jnp.int32, (rows, 1), 0)
        out_ref[u] = jnp.where(row < limit_ref[u], result, 0.0).astype(out_ref.dtype)


def finish(history_back, projected, cand_x, w_out, self_bias, lengths, row_limit, heads, score_scale):
    users, rows, width = cand_x.shape
    smem = pl.BlockSpec(memory_space=pltpu.SMEM)
    vmem = pl.BlockSpec(memory_space=pltpu.VMEM)
    return pl.pallas_call(
        functools.partial(finish_kernel, heads=heads, score_scale=score_scale),
        out_shape=jax.ShapeDtypeStruct(cand_x.shape, cand_x.dtype),
        in_specs=[smem, smem, smem, vmem, vmem, vmem, vmem],
        out_specs=vmem,
        scratch_shapes=[pltpu.VMEM((rows, width), jnp.float32)],
    )(self_bias, lengths, row_limit, history_back, projected, cand_x, w_out)


def local(cand_x, kv_cache, w_uvqk, w_out, self_bias, user_rank, hist_len, cand_count, tile_slot):
    users_here, cand_rows, width = cand_x.shape
    heads = self_bias.shape[0]
    head_dim = width // heads
    score_scale = 1.0 / math.sqrt(head_dim)
    slots_own, tile_len, _ = kv_cache.shape
    user_total, tiles_max = tile_slot.shape
    req_count = lax.axis_size("req")
    hist_count = lax.axis_size("hist")
    req_index = lax.axis_index("req")
    hist_index = lax.axis_index("hist")
    per_hist = tiles_max // hist_count
    capacity = slots_own // req_count + 1
    first_slot = req_index * users_here
    user_ids = lax.dynamic_slice_in_dim(user_rank, first_slot, users_here)
    match_user = user_ids[:, None] == jnp.arange(user_total)[None, :]
    lengths = jnp.sum(jnp.where(match_user, hist_len[None, :], 0), axis=1)
    live_counts = jnp.sum(jnp.where(match_user, cand_count[None, :], 0), axis=1)
    column = lax.dynamic_index_in_dim(
        tile_slot.reshape(user_total, per_hist, hist_count), hist_index, axis=2, keepdims=False
    )
    codes = column.reshape(-1)
    owners = codes // slots_own
    local_slot = codes % slots_own
    dests = jnp.repeat(jnp.arange(user_total) // users_here, per_hist)
    entry_ids = jnp.arange(codes.shape[0])
    same_pair = (
        (owners[:, None] == owners[None, :])
        & (dests[:, None] == dests[None, :])
        & (entry_ids[:, None] > entry_ids[None, :])
    )
    places = jnp.sum(jnp.where(same_pair, 1, 0), axis=1)
    picked = (
        (owners[None, None, :] == req_index)
        & (dests[None, None, :] == jnp.arange(req_count)[:, None, None])
        & (places[None, None, :] == jnp.arange(capacity)[None, :, None])
    )
    source_slot = jnp.sum(jnp.where(picked, local_slot[None, None, :], 0), axis=2).reshape(-1)
    first_entry = first_slot * per_hist
    my_owner = lax.dynamic_slice_in_dim(owners, first_entry, users_here * per_hist)
    my_place = lax.dynamic_slice_in_dim(places, first_entry, users_here * per_hist)
    picked_slot = (my_owner * capacity + my_place).astype(jnp.int32)
    first_len = tile_len * 5 // 8
    bounds = [(0, first_len), (first_len, tile_len)]
    sending = []
    for lo, hi in bounds:
        kv_half = lax.slice_in_dim(kv_cache, lo, hi, axis=1)
        outgoing = kv_half.at[source_slot].get(mode="promise_in_bounds")
        sending.append(outgoing.reshape(req_count, capacity, hi - lo, 2 * width))
    first_in = lax.all_to_all(sending[0], "req", split_axis=0, concat_axis=0, tiled=True)
    normed = layer_norm(cand_x.astype(jnp.float32)).astype(jnp.bfloat16)
    mixed_in = jnp.dot(normed.reshape(-1, width), w_uvqk, preferred_element_type=jnp.float32)
    projected = jax.nn.silu(mixed_in).astype(jnp.bfloat16).reshape(users_here, cand_rows, 4, width)
    projected, second_out = lax.optimization_barrier((projected, sending[1]))
    second_in = req_a2a(second_out, 0)
    halves = [
        first_in.reshape(req_count * capacity, first_len, 2 * width),
        second_in.reshape(req_count * capacity, tile_len - first_len, 2 * width),
    ]
    u_gate = projected[:, :, 0]
    v_self = projected[:, :, 1]
    queries = projected[:, :, 2]
    k_self = projected[:, :, 3]
    my_user = hist_index // heads
    my_length = lax.dynamic_slice_in_dim(lengths, my_user, 1)
    q_row = 2 * per_hist * first_len
    packed_a = lax.all_to_all(
        pack_for_heads(picked_slot, halves[0], queries, users_here, heads),
        "hist", split_axis=0, concat_axis=0, tiled=True,
    )
    history_mine = attend(my_length, packed_a, packed_a, q_row, per_hist, first_len, tile_len, 0, score_scale)
    packed_b = lax.all_to_all(
        pack_for_heads(picked_slot, halves[1], None, users_here, heads),
        "hist", split_axis=0, concat_axis=0, tiled=True,
    )
    history_mine = attend(
        my_length, packed_b, packed_a, q_row, per_hist, tile_len - first_len, tile_len, first_len, score_scale,
        init=history_mine,
    ).astype(jnp.bfloat16)
    history_back = lax.all_to_all(
        history_mine.reshape(hist_count, cand_rows, head_dim), "hist", split_axis=0, concat_axis=0, tiled=True
    )
    row_limit = (live_counts - hist_index * cand_rows).astype(jnp.int32)
    return finish(
        history_back, projected.reshape(users_here, cand_rows, 4 * width), cand_x, w_out, self_bias,
        lengths.astype(jnp.int32), row_limit, heads, score_scale,
    )


def solution(mesh):
    return jax.shard_map(
        local,
        mesh=mesh,
        in_specs=(
            P("req", "hist", None),
            P(("req", "hist"), None, None),
            P(),
            P(),
            P(),
            P(),
            P(),
            P(),
            P(),
        ),
        out_specs=P("req", "hist", None),
        check_vma=False,
    )
```

```python
import functools
import math

import jax
import jax.numpy as jnp
from jax import lax
from jax.experimental import pallas as pl
from jax.experimental.pallas import tpu as pltpu
from jax.sharding import PartitionSpec as P


def layer_norm(values):
    mean_value = jnp.mean(values, axis=-1, keepdims=True)
    centred = values - mean_value
    spread = jnp.mean(centred * centred, axis=-1, keepdims=True)
    return centred * lax.rsqrt(spread + 1e-05)


def silu_tanh(values):
    return values * (0.5 + 0.5 * jnp.tanh(0.5 * values))


def req_a2a_kernel(send_ref, recv_ref, send_sem, recv_sem, local_sem, *, axis, other_axis):
    n = send_ref.shape[0]
    me = lax.axis_index(axis)
    other = lax.axis_index(other_axis)
    barrier = pltpu.get_barrier_semaphore()
    for k in range(1, n):
        peer = lax.rem(me + k, n)
        pl.semaphore_signal(
            barrier, inc=1, device_id={axis: peer, other_axis: other}, device_id_type=pl.DeviceIdType.MESH
        )
    pl.semaphore_wait(barrier, n - 1)
    copies = []
    for k in range(1, n):
        peer = lax.rem(me + k, n)
        copy = pltpu.make_async_remote_copy(
            src_ref=send_ref.at[peer],
            dst_ref=recv_ref.at[me],
            send_sem=send_sem.at[k],
            recv_sem=recv_sem.at[k],
            device_id={axis: peer, other_axis: other},
            device_id_type=pl.DeviceIdType.MESH,
        )
        copy.start()
        copies.append(copy)
    own = pltpu.make_async_copy(send_ref.at[me], recv_ref.at[me], local_sem)
    own.start()
    own.wait()
    for copy in copies:
        copy.wait_send()
    for k in range(1, n):
        src = lax.rem(me + n - k, n)
        pltpu.make_async_remote_copy(
            src_ref=send_ref.at[src],
            dst_ref=recv_ref.at[src],
            send_sem=send_sem.at[k],
            recv_sem=recv_sem.at[k],
            device_id={axis: src, other_axis: other},
            device_id_type=pl.DeviceIdType.MESH,
        ).wait_recv()


def req_a2a(x, collective_id):
    n = x.shape[0]
    return pl.pallas_call(
        functools.partial(req_a2a_kernel, axis="req", other_axis="hist"),
        out_shape=jax.ShapeDtypeStruct(x.shape, x.dtype),
        in_specs=[pl.BlockSpec(memory_space=pl.ANY)],
        out_specs=pl.BlockSpec(memory_space=pl.ANY),
        scratch_shapes=[
            pltpu.SemaphoreType.DMA((n,)),
            pltpu.SemaphoreType.DMA((n,)),
            pltpu.SemaphoreType.DMA(()),
        ],
        compiler_params=pltpu.CompilerParams(collective_id=collective_id, has_side_effects=True),
    )(x)


def attend_kernel(len_ref, kv_ref, qsrc_ref, *rest, n_tiles, sub, tile_len, offset, q_row, score_scale, chunk):
    if len(rest) == 3:
        init_ref, o_ref, q_ref = rest
    else:
        init_ref = None
        o_ref, q_ref = rest
    length = len_ref[0]
    n_cls, _, head_dim = kv_ref.shape
    span = n_tiles * sub
    block = q_ref.shape[0] // n_cls
    half_scale = 0.5 * score_scale
    for b in range(n_cls):
        q_ref[pl.ds(b * block, block), :] = qsrc_ref[b, pl.ds(q_row, block), :]
    if init_ref is None:
        o_ref[...] = jnp.zeros_like(o_ref)
    else:
        o_ref[...] = init_ref[...]

    group = 1 if span % 128 == 0 else 2

    def one_class(g, carry):
        c = g * group
        key_index = lax.broadcasted_iota(jnp.int32, (1, group * span), 1)
        cls = c + key_index // span
        within = key_index % span
        position = (cls + n_cls * (within // sub)) * tile_len + offset + within % sub
        live = position < length

        def add_class(masked):
            keys = jnp.concatenate([kv_ref[c + j, pl.ds(0, span), :] for j in range(group)], axis=0)
            values = jnp.concatenate([kv_ref[c + j, pl.ds(span, span), :] for j in range(group)], axis=0)
            for ci in range(q_ref.shape[0] // chunk):
                rows = pl.ds(ci * chunk, chunk)
                scores = lax.dot_general(
                    q_ref[rows, :], keys, (((1,), (1,)), ((), ())), preferred_element_type=jnp.float32
                )
                half = scores * half_scale
                weights = half + half * jnp.tanh(half)
                if masked:
                    weights = jnp.where(live, weights, 0.0)
                o_ref[rows, :] += jnp.dot(weights.astype(jnp.bfloat16), values, preferred_element_type=jnp.float32)

        last_key = (c + group - 1 + n_cls * (n_tiles - 1)) * tile_len + offset + sub
        whole = last_key <= length
        pl.when(whole)(lambda: add_class(False))
        pl.when(jnp.logical_and(jnp.logical_not(whole), c * tile_len + offset < length))(lambda: add_class(True))
        return carry

    lax.fori_loop(0, n_cls // group, one_class, 0)


def attend(length, kv_packed, q_packed, q_row, n_tiles, sub, tile_len, offset, score_scale, init=None):
    n_cls, _, head_dim = q_packed.shape
    rows = n_cls * (q_packed.shape[1] - q_row)
    chunk = 2048
    kernel = functools.partial(
        attend_kernel,
        n_tiles=n_tiles,
        sub=sub,
        tile_len=tile_len,
        offset=offset,
        q_row=q_row,
        score_scale=score_scale,
        chunk=chunk,
    )
    return pl.pallas_call(
        kernel,
        out_shape=jax.ShapeDtypeStruct((rows, head_dim), jnp.float32),
        in_specs=[pl.BlockSpec(memory_space=pltpu.SMEM)]
        + [pl.BlockSpec(memory_space=pltpu.VMEM)] * (2 if init is None else 3),
        out_specs=pl.BlockSpec(memory_space=pltpu.VMEM),
        scratch_shapes=[pltpu.VMEM((rows, head_dim), jnp.bfloat16)],
    )(length, kv_packed, q_packed, *([] if init is None else [init]))


def pack_kernel(picked_ref, tiles_hbm, *rest, heads, users, per_hist, with_q):
    if with_q:
        q_ref, out_ref, staged, in_sem = rest
    else:
        out_ref, staged, in_sem = rest
    width = tiles_hbm.shape[2] // 2
    head_dim = width // heads
    sub = tiles_hbm.shape[1]
    span = per_hist * sub
    n_in = users * per_hist
    reads = []
    for i in range(n_in):
        read = pltpu.make_async_copy(tiles_hbm.at[picked_ref[i]], staged.at[i], in_sem.at[i])
        read.start()
        reads.append(read)
    if with_q:
        cand_rows = q_ref.shape[1]
        for u in range(users):
            for e in range(heads):
                out_ref[u * heads + e, pl.ds(2 * span, cand_rows), :] = q_ref[u, :, pl.ds(e * head_dim, head_dim)]
    for i in range(n_in):
        u, t = divmod(i, per_hist)
        reads[i].wait()
        for piece in range(2 * heads):
            e, kv = divmod(piece, 2)
            out_ref[u * heads + e, pl.ds(kv * span + t * sub, sub), :] = staged[
                i, :, pl.ds(piece * head_dim, head_dim)
            ]


def pack_for_heads(picked_slot, tiles, queries, users, heads):
    n_in = picked_slot.shape[0]
    per_hist = n_in // users
    sub, wide = tiles.shape[1], tiles.shape[2]
    head_dim = wide // (2 * heads)
    rows = 2 * per_hist * sub + (0 if queries is None else queries.shape[1])
    operands = [picked_slot, tiles] + ([] if queries is None else [queries])
    return pl.pallas_call(
        functools.partial(pack_kernel, heads=heads, users=users, per_hist=per_hist, with_q=queries is not None),
        out_shape=jax.ShapeDtypeStruct((users * heads, rows, head_dim), tiles.dtype),
        in_specs=[pl.BlockSpec(memory_space=pltpu.SMEM), pl.BlockSpec(memory_space=pl.ANY)]
        + ([] if queries is None else [pl.BlockSpec(memory_space=pltpu.VMEM)]),
        out_specs=pl.BlockSpec(memory_space=pltpu.VMEM),
        scratch_shapes=[
            pltpu.VMEM((n_in, sub, wide), tiles.dtype),
            pltpu.SemaphoreType.DMA((n_in,)),
        ],
    )(*operands)


def finish_kernel(
    bias_ref, len_ref, limit_ref, hist_ref, proj_ref, x_ref, w_ref, out_ref, att_ref, *, heads, score_scale
):
    users, rows, width = x_ref.shape
    head_dim = width // heads
    for u in range(users):
        divisor = (len_ref[u] + 1).astype(jnp.float32)
        for e in range(heads):
            value = proj_ref[u, :, pl.ds(width + e * head_dim, head_dim)].astype(jnp.float32)
            query = proj_ref[u, :, pl.ds(2 * width + e * head_dim, head_dim)].astype(jnp.float32)
            key = proj_ref[u, :, pl.ds(3 * width + e * head_dim, head_dim)].astype(jnp.float32)
            self_score = jnp.sum(query * key, axis=-1, keepdims=True) * score_scale + bias_ref[e]
            own = self_score * (0.5 + 0.5 * jnp.tanh(0.5 * self_score)) * value
            history = hist_ref[u * heads + e].astype(jnp.float32)
            att_ref[:, pl.ds(e * head_dim, head_dim)] = (history + own) / divisor
        attended = att_ref[...]
        centred = attended - jnp.mean(attended, axis=-1, keepdims=True)
        spread = jnp.mean(centred * centred, axis=-1, keepdims=True)
        gate = proj_ref[u, :, pl.ds(0, width)].astype(jnp.float32)
        gated = (centred * lax.rsqrt(spread + 1e-05) * gate).astype(jnp.bfloat16)
        result = x_ref[u].astype(jnp.float32) + jnp.dot(gated, w_ref[...], preferred_element_type=jnp.float32)
        row = lax.broadcasted_iota(jnp.int32, (rows, 1), 0)
        out_ref[u] = jnp.where(row < limit_ref[u], result, 0.0).astype(out_ref.dtype)


def finish(history_back, projected, cand_x, w_out, self_bias, lengths, row_limit, heads, score_scale):
    users, rows, width = cand_x.shape
    smem = pl.BlockSpec(memory_space=pltpu.SMEM)
    vmem = pl.BlockSpec(memory_space=pltpu.VMEM)
    return pl.pallas_call(
        functools.partial(finish_kernel, heads=heads, score_scale=score_scale),
        out_shape=jax.ShapeDtypeStruct(cand_x.shape, cand_x.dtype),
        in_specs=[smem, smem, smem, vmem, vmem, vmem, vmem],
        out_specs=vmem,
        scratch_shapes=[pltpu.VMEM((rows, width), jnp.float32)],
    )(self_bias, lengths, row_limit, history_back, projected, cand_x, w_out)


def local(cand_x, kv_cache, w_uvqk, w_out, self_bias, user_rank, hist_len, cand_count, tile_slot):
    users_here, cand_rows, width = cand_x.shape
    heads = self_bias.shape[0]
    head_dim = width // heads
    score_scale = 1.0 / math.sqrt(head_dim)
    slots_own, tile_len, _ = kv_cache.shape
    user_total, tiles_max = tile_slot.shape
    req_count = lax.axis_size("req")
    hist_count = lax.axis_size("hist")
    req_index = lax.axis_index("req")
    hist_index = lax.axis_index("hist")
    per_hist = tiles_max // hist_count
    capacity = slots_own // req_count + 1
    first_slot = req_index * users_here
    user_ids = lax.dynamic_slice_in_dim(user_rank, first_slot, users_here)
    match_user = user_ids[:, None] == jnp.arange(user_total)[None, :]
    lengths = jnp.sum(jnp.where(match_user, hist_len[None, :], 0), axis=1)
    live_counts = jnp.sum(jnp.where(match_user, cand_count[None, :], 0), axis=1)
    column = lax.dynamic_index_in_dim(
        tile_slot.reshape(user_total, per_hist, hist_count), hist_index, axis=2, keepdims=False
    )
    codes = column.reshape(-1)
    owners = codes // slots_own
    local_slot = codes % slots_own
    dests = jnp.repeat(jnp.arange(user_total) // users_here, per_hist)
    entry_ids = jnp.arange(codes.shape[0])
    same_pair = (
        (owners[:, None] == owners[None, :])
        & (dests[:, None] == dests[None, :])
        & (entry_ids[:, None] > entry_ids[None, :])
    )
    places = jnp.sum(jnp.where(same_pair, 1, 0), axis=1)
    picked = (
        (owners[None, None, :] == req_index)
        & (dests[None, None, :] == jnp.arange(req_count)[:, None, None])
        & (places[None, None, :] == jnp.arange(capacity)[None, :, None])
    )
    source_slot = jnp.sum(jnp.where(picked, local_slot[None, None, :], 0), axis=2).reshape(-1)
    first_entry = first_slot * per_hist
    my_owner = lax.dynamic_slice_in_dim(owners, first_entry, users_here * per_hist)
    my_place = lax.dynamic_slice_in_dim(places, first_entry, users_here * per_hist)
    picked_slot = (my_owner * capacity + my_place).astype(jnp.int32)
    first_len = tile_len * 5 // 8
    bounds = [(0, first_len), (first_len, tile_len)]
    sending = []
    for lo, hi in bounds:
        kv_half = lax.slice_in_dim(kv_cache, lo, hi, axis=1)
        outgoing = kv_half.at[source_slot].get(mode="promise_in_bounds")
        sending.append(outgoing.reshape(req_count, capacity, hi - lo, 2 * width))
    first_in = lax.all_to_all(sending[0], "req", split_axis=0, concat_axis=0, tiled=True)
    normed = layer_norm(cand_x.astype(jnp.float32)).astype(jnp.bfloat16)
    mixed_in = jnp.dot(normed.reshape(-1, width), w_uvqk, preferred_element_type=jnp.float32)
    projected = jax.nn.silu(mixed_in).astype(jnp.bfloat16).reshape(users_here, cand_rows, 4, width)
    projected, second_out = lax.optimization_barrier((projected, sending[1]))
    second_in = req_a2a(second_out, 0)
    halves = [
        first_in.reshape(req_count * capacity, first_len, 2 * width),
        second_in.reshape(req_count * capacity, tile_len - first_len, 2 * width),
    ]
    u_gate = projected[:, :, 0]
    v_self = projected[:, :, 1]
    queries = projected[:, :, 2]
    k_self = projected[:, :, 3]
    my_user = hist_index // heads
    my_length = lax.dynamic_slice_in_dim(lengths, my_user, 1)
    q_row = 2 * per_hist * first_len
    packed_a = lax.all_to_all(
        pack_for_heads(picked_slot, halves[0], queries, users_here, heads),
        "hist", split_axis=0, concat_axis=0, tiled=True,
    )
    history_mine = attend(my_length, packed_a, packed_a, q_row, per_hist, first_len, tile_len, 0, score_scale)
    packed_b = lax.all_to_all(
        pack_for_heads(picked_slot, halves[1], None, users_here, heads),
        "hist", split_axis=0, concat_axis=0, tiled=True,
    )
    history_mine = attend(
        my_length, packed_b, packed_a, q_row, per_hist, tile_len - first_len, tile_len, first_len, score_scale,
        init=history_mine,
    ).astype(jnp.bfloat16)
    history_back = lax.all_to_all(
        history_mine.reshape(hist_count, cand_rows, head_dim), "hist", split_axis=0, concat_axis=0, tiled=True
    )
    row_limit = (live_counts - hist_index * cand_rows).astype(jnp.int32)
    return finish(
        history_back, projected.reshape(users_here, cand_rows, 4 * width), cand_x, w_out, self_bias,
        lengths.astype(jnp.int32), row_limit, heads, score_scale,
    )


def solution(mesh):
    return jax.shard_map(
        local,
        mesh=mesh,
        in_specs=(
            P("req", "hist", None),
            P(("req", "hist"), None, None),
            P(),
            P(),
            P(),
            P(),
            P(),
            P(),
            P(),
        ),
        out_specs=P("req", "hist", None),
        check_vma=False,
    )
```

```python
import functools
import math

import jax
import jax.numpy as jnp
from jax import lax
from jax.experimental import pallas as pl
from jax.experimental.pallas import tpu as pltpu
from jax.sharding import PartitionSpec as P


def layer_norm(values):
    mean_value = jnp.mean(values, axis=-1, keepdims=True)
    centred = values - mean_value
    spread = jnp.mean(centred * centred, axis=-1, keepdims=True)
    return centred * lax.rsqrt(spread + 1e-05)


def silu_tanh(values):
    return values * (0.5 + 0.5 * jnp.tanh(0.5 * values))


def req_a2a_kernel(send_ref, recv_ref, send_sem, recv_sem, local_sem, *, axis, other_axis):
    n = send_ref.shape[0]
    me = lax.axis_index(axis)
    other = lax.axis_index(other_axis)
    barrier = pltpu.get_barrier_semaphore()
    for k in range(1, n):
        peer = lax.rem(me + k, n)
        pl.semaphore_signal(
            barrier, inc=1, device_id={axis: peer, other_axis: other}, device_id_type=pl.DeviceIdType.MESH
        )
    pl.semaphore_wait(barrier, n - 1)
    copies = []
    for k in range(1, n):
        peer = lax.rem(me + k, n)
        copy = pltpu.make_async_remote_copy(
            src_ref=send_ref.at[peer],
            dst_ref=recv_ref.at[me],
            send_sem=send_sem.at[k],
            recv_sem=recv_sem.at[k],
            device_id={axis: peer, other_axis: other},
            device_id_type=pl.DeviceIdType.MESH,
        )
        copy.start()
        copies.append(copy)
    own = pltpu.make_async_copy(send_ref.at[me], recv_ref.at[me], local_sem)
    own.start()
    own.wait()
    for copy in copies:
        copy.wait_send()
    for k in range(1, n):
        src = lax.rem(me + n - k, n)
        pltpu.make_async_remote_copy(
            src_ref=send_ref.at[src],
            dst_ref=recv_ref.at[src],
            send_sem=send_sem.at[k],
            recv_sem=recv_sem.at[k],
            device_id={axis: src, other_axis: other},
            device_id_type=pl.DeviceIdType.MESH,
        ).wait_recv()


def req_a2a(x, collective_id):
    n = x.shape[0]
    return pl.pallas_call(
        functools.partial(req_a2a_kernel, axis="req", other_axis="hist"),
        out_shape=jax.ShapeDtypeStruct(x.shape, x.dtype),
        in_specs=[pl.BlockSpec(memory_space=pl.ANY)],
        out_specs=pl.BlockSpec(memory_space=pl.ANY),
        scratch_shapes=[
            pltpu.SemaphoreType.DMA((n,)),
            pltpu.SemaphoreType.DMA((n,)),
            pltpu.SemaphoreType.DMA(()),
        ],
        compiler_params=pltpu.CompilerParams(collective_id=collective_id, has_side_effects=True),
    )(x)


def attend_kernel(len_ref, kv_ref, qsrc_ref, *rest, n_tiles, sub, tile_len, offset, q_row, score_scale, chunk):
    if len(rest) == 4:
        init_ref, out_ref, q_ref, o_ref = rest
    else:
        init_ref = out_ref = None
        o_ref, q_ref = rest
    length = len_ref[0]
    n_cls, _, head_dim = kv_ref.shape
    span = n_tiles * sub
    block = q_ref.shape[0] // n_cls
    half_scale = 0.5 * score_scale
    for b in range(n_cls):
        q_ref[pl.ds(b * block, block), :] = qsrc_ref[b, pl.ds(q_row, block), :]
    if init_ref is None:
        o_ref[...] = jnp.zeros_like(o_ref)
    else:
        o_ref[...] = init_ref[...]

    group = 1 if span % 128 == 0 else 2

    def one_class(g, carry):
        c = g * group
        key_index = lax.broadcasted_iota(jnp.int32, (1, group * span), 1)
        cls = c + key_index // span
        within = key_index % span
        position = (cls + n_cls * (within // sub)) * tile_len + offset + within % sub
        live = position < length

        def add_class(masked):
            keys = jnp.concatenate([kv_ref[c + j, pl.ds(0, span), :] for j in range(group)], axis=0)
            values = jnp.concatenate([kv_ref[c + j, pl.ds(span, span), :] for j in range(group)], axis=0)
            for ci in range(q_ref.shape[0] // chunk):
                rows = pl.ds(ci * chunk, chunk)
                scores = lax.dot_general(
                    q_ref[rows, :], keys, (((1,), (1,)), ((), ())), preferred_element_type=jnp.float32
                )
                half = scores * half_scale
                weights = half + half * jnp.tanh(half)
                if masked:
                    weights = jnp.where(live, weights, 0.0)
                o_ref[rows, :] += jnp.dot(weights.astype(jnp.bfloat16), values, preferred_element_type=jnp.float32)

        last_key = (c + group - 1 + n_cls * (n_tiles - 1)) * tile_len + offset + sub
        whole = last_key <= length
        pl.when(whole)(lambda: add_class(False))
        pl.when(jnp.logical_and(jnp.logical_not(whole), c * tile_len + offset < length))(lambda: add_class(True))
        return carry

    lax.fori_loop(0, n_cls // group, one_class, 0)
    if out_ref is not None:
        out_ref[...] = o_ref[...].astype(out_ref.dtype)


def attend(length, kv_packed, q_packed, q_row, n_tiles, sub, tile_len, offset, score_scale, init=None):
    n_cls, _, head_dim = q_packed.shape
    rows = n_cls * (q_packed.shape[1] - q_row)
    chunk = 2048
    kernel = functools.partial(
        attend_kernel,
        n_tiles=n_tiles,
        sub=sub,
        tile_len=tile_len,
        offset=offset,
        q_row=q_row,
        score_scale=score_scale,
        chunk=chunk,
    )
    return pl.pallas_call(
        kernel,
        out_shape=jax.ShapeDtypeStruct((rows, head_dim), jnp.float32 if init is None else jnp.bfloat16),
        in_specs=[pl.BlockSpec(memory_space=pltpu.SMEM)]
        + [pl.BlockSpec(memory_space=pltpu.VMEM)] * (2 if init is None else 3),
        out_specs=pl.BlockSpec(memory_space=pltpu.VMEM),
        scratch_shapes=[pltpu.VMEM((rows, head_dim), jnp.bfloat16)]
        + ([] if init is None else [pltpu.VMEM((rows, head_dim), jnp.float32)]),
    )(length, kv_packed, q_packed, *([] if init is None else [init]))


def pack_kernel(picked_ref, tiles_hbm, *rest, heads, users, per_hist, with_q):
    if with_q:
        q_ref, out_ref, staged, in_sem = rest
    else:
        out_ref, staged, in_sem = rest
    width = tiles_hbm.shape[2] // 2
    head_dim = width // heads
    sub = tiles_hbm.shape[1]
    span = per_hist * sub
    n_in = users * per_hist
    reads = []
    for i in range(n_in):
        read = pltpu.make_async_copy(tiles_hbm.at[picked_ref[i]], staged.at[i], in_sem.at[i])
        read.start()
        reads.append(read)
    if with_q:
        cand_rows = q_ref.shape[1]
        for u in range(users):
            for e in range(heads):
                out_ref[u * heads + e, pl.ds(2 * span, cand_rows), :] = q_ref[u, :, pl.ds(e * head_dim, head_dim)]
    for i in range(n_in):
        u, t = divmod(i, per_hist)
        reads[i].wait()
        for piece in range(2 * heads):
            e, kv = divmod(piece, 2)
            out_ref[u * heads + e, pl.ds(kv * span + t * sub, sub), :] = staged[
                i, :, pl.ds(piece * head_dim, head_dim)
            ]


def pack_for_heads(picked_slot, tiles, queries, users, heads):
    n_in = picked_slot.shape[0]
    per_hist = n_in // users
    sub, wide = tiles.shape[1], tiles.shape[2]
    head_dim = wide // (2 * heads)
    rows = 2 * per_hist * sub + (0 if queries is None else queries.shape[1])
    operands = [picked_slot, tiles] + ([] if queries is None else [queries])
    return pl.pallas_call(
        functools.partial(pack_kernel, heads=heads, users=users, per_hist=per_hist, with_q=queries is not None),
        out_shape=jax.ShapeDtypeStruct((users * heads, rows, head_dim), tiles.dtype),
        in_specs=[pl.BlockSpec(memory_space=pltpu.SMEM), pl.BlockSpec(memory_space=pl.ANY)]
        + ([] if queries is None else [pl.BlockSpec(memory_space=pltpu.VMEM)]),
        out_specs=pl.BlockSpec(memory_space=pltpu.VMEM),
        scratch_shapes=[
            pltpu.VMEM((n_in, sub, wide), tiles.dtype),
            pltpu.SemaphoreType.DMA((n_in,)),
        ],
    )(*operands)


def finish_kernel(
    bias_ref, len_ref, limit_ref, hist_ref, proj_ref, x_ref, w_ref, out_ref, att_ref, *, heads, score_scale
):
    users, rows, width = x_ref.shape
    head_dim = width // heads
    for u in range(users):
        divisor = (len_ref[u] + 1).astype(jnp.float32)
        for e in range(heads):
            value = proj_ref[u, :, pl.ds(width + e * head_dim, head_dim)].astype(jnp.float32)
            query = proj_ref[u, :, pl.ds(2 * width + e * head_dim, head_dim)].astype(jnp.float32)
            key = proj_ref[u, :, pl.ds(3 * width + e * head_dim, head_dim)].astype(jnp.float32)
            self_score = jnp.sum(query * key, axis=-1, keepdims=True) * score_scale + bias_ref[e]
            own = self_score * (0.5 + 0.5 * jnp.tanh(0.5 * self_score)) * value
            history = hist_ref[u * heads + e].astype(jnp.float32)
            att_ref[:, pl.ds(e * head_dim, head_dim)] = (history + own) / divisor
        attended = att_ref[...]
        centred = attended - jnp.mean(attended, axis=-1, keepdims=True)
        spread = jnp.mean(centred * centred, axis=-1, keepdims=True)
        gate = proj_ref[u, :, pl.ds(0, width)].astype(jnp.float32)
        gated = (centred * lax.rsqrt(spread + 1e-05) * gate).astype(jnp.bfloat16)
        result = x_ref[u].astype(jnp.float32) + jnp.dot(gated, w_ref[...], preferred_element_type=jnp.float32)
        row = lax.broadcasted_iota(jnp.int32, (rows, 1), 0)
        out_ref[u] = jnp.where(row < limit_ref[u], result, 0.0).astype(out_ref.dtype)


def finish(history_back, projected, cand_x, w_out, self_bias, lengths, row_limit, heads, score_scale):
    users, rows, width = cand_x.shape
    smem = pl.BlockSpec(memory_space=pltpu.SMEM)
    vmem = pl.BlockSpec(memory_space=pltpu.VMEM)
    return pl.pallas_call(
        functools.partial(finish_kernel, heads=heads, score_scale=score_scale),
        out_shape=jax.ShapeDtypeStruct(cand_x.shape, cand_x.dtype),
        in_specs=[smem, smem, smem, vmem, vmem, vmem, vmem],
        out_specs=vmem,
        scratch_shapes=[pltpu.VMEM((rows, width), jnp.float32)],
    )(self_bias, lengths, row_limit, history_back, projected, cand_x, w_out)


def local(cand_x, kv_cache, w_uvqk, w_out, self_bias, user_rank, hist_len, cand_count, tile_slot):
    users_here, cand_rows, width = cand_x.shape
    heads = self_bias.shape[0]
    head_dim = width // heads
    score_scale = 1.0 / math.sqrt(head_dim)
    slots_own, tile_len, _ = kv_cache.shape
    user_total, tiles_max = tile_slot.shape
    req_count = lax.axis_size("req")
    hist_count = lax.axis_size("hist")
    req_index = lax.axis_index("req")
    hist_index = lax.axis_index("hist")
    per_hist = tiles_max // hist_count
    capacity = slots_own // req_count + 1
    first_slot = req_index * users_here
    user_ids = lax.dynamic_slice_in_dim(user_rank, first_slot, users_here)
    match_user = user_ids[:, None] == jnp.arange(user_total)[None, :]
    lengths = jnp.sum(jnp.where(match_user, hist_len[None, :], 0), axis=1)
    live_counts = jnp.sum(jnp.where(match_user, cand_count[None, :], 0), axis=1)
    column = lax.dynamic_index_in_dim(
        tile_slot.reshape(user_total, per_hist, hist_count), hist_index, axis=2, keepdims=False
    )
    codes = column.reshape(-1)
    owners = codes // slots_own
    local_slot = codes % slots_own
    dests = jnp.repeat(jnp.arange(user_total) // users_here, per_hist)
    entry_ids = jnp.arange(codes.shape[0])
    same_pair = (
        (owners[:, None] == owners[None, :])
        & (dests[:, None] == dests[None, :])
        & (entry_ids[:, None] > entry_ids[None, :])
    )
    places = jnp.sum(jnp.where(same_pair, 1, 0), axis=1)
    picked = (
        (owners[None, None, :] == req_index)
        & (dests[None, None, :] == jnp.arange(req_count)[:, None, None])
        & (places[None, None, :] == jnp.arange(capacity)[None, :, None])
    )
    source_slot = jnp.sum(jnp.where(picked, local_slot[None, None, :], 0), axis=2).reshape(-1)
    first_entry = first_slot * per_hist
    my_owner = lax.dynamic_slice_in_dim(owners, first_entry, users_here * per_hist)
    my_place = lax.dynamic_slice_in_dim(places, first_entry, users_here * per_hist)
    picked_slot = (my_owner * capacity + my_place).astype(jnp.int32)
    first_len = tile_len * 5 // 8
    bounds = [(0, first_len), (first_len, tile_len)]
    sending = []
    for lo, hi in bounds:
        kv_half = lax.slice_in_dim(kv_cache, lo, hi, axis=1)
        outgoing = kv_half.at[source_slot].get(mode="promise_in_bounds")
        sending.append(outgoing.reshape(req_count, capacity, hi - lo, 2 * width))
    first_in = lax.all_to_all(sending[0], "req", split_axis=0, concat_axis=0, tiled=True)
    normed = layer_norm(cand_x.astype(jnp.float32)).astype(jnp.bfloat16)
    mixed_in = jnp.dot(normed.reshape(-1, width), w_uvqk, preferred_element_type=jnp.float32)
    projected = jax.nn.silu(mixed_in).astype(jnp.bfloat16).reshape(users_here, cand_rows, 4, width)
    projected, second_out = lax.optimization_barrier((projected, sending[1]))
    second_in = req_a2a(second_out, 0)
    halves = [
        first_in.reshape(req_count * capacity, first_len, 2 * width),
        second_in.reshape(req_count * capacity, tile_len - first_len, 2 * width),
    ]
    u_gate = projected[:, :, 0]
    v_self = projected[:, :, 1]
    queries = projected[:, :, 2]
    k_self = projected[:, :, 3]
    my_user = hist_index // heads
    my_length = lax.dynamic_slice_in_dim(lengths, my_user, 1)
    q_row = 2 * per_hist * first_len
    packed_a = lax.all_to_all(
        pack_for_heads(picked_slot, halves[0], queries, users_here, heads),
        "hist", split_axis=0, concat_axis=0, tiled=True,
    )
    history_mine = attend(my_length, packed_a, packed_a, q_row, per_hist, first_len, tile_len, 0, score_scale)
    packed_b = lax.all_to_all(
        pack_for_heads(picked_slot, halves[1], None, users_here, heads),
        "hist", split_axis=0, concat_axis=0, tiled=True,
    )
    history_mine = attend(
        my_length, packed_b, packed_a, q_row, per_hist, tile_len - first_len, tile_len, first_len, score_scale,
        init=history_mine,
    )
    history_back = lax.all_to_all(
        history_mine.reshape(hist_count, cand_rows, head_dim), "hist", split_axis=0, concat_axis=0, tiled=True
    )
    row_limit = (live_counts - hist_index * cand_rows).astype(jnp.int32)
    return finish(
        history_back, projected.reshape(users_here, cand_rows, 4 * width), cand_x, w_out, self_bias,
        lengths.astype(jnp.int32), row_limit, heads, score_scale,
    )


def solution(mesh):
    return jax.shard_map(
        local,
        mesh=mesh,
        in_specs=(
            P("req", "hist", None),
            P(("req", "hist"), None, None),
            P(),
            P(),
            P(),
            P(),
            P(),
            P(),
            P(),
        ),
        out_specs=P("req", "hist", None),
        check_vma=False,
    )
```

```python
import functools
import math

import jax
import jax.numpy as jnp
from jax import lax
from jax.experimental import pallas as pl
from jax.experimental.pallas import tpu as pltpu
from jax.sharding import PartitionSpec as P


def layer_norm(values):
    mean_value = jnp.mean(values, axis=-1, keepdims=True)
    centred = values - mean_value
    spread = jnp.mean(centred * centred, axis=-1, keepdims=True)
    return centred * lax.rsqrt(spread + 1e-05)


def silu_tanh(values):
    return values * (0.5 + 0.5 * jnp.tanh(0.5 * values))


def req_a2a_kernel(send_ref, recv_ref, send_sem, recv_sem, local_sem, *, axis, other_axis):
    n = send_ref.shape[0]
    me = lax.axis_index(axis)
    other = lax.axis_index(other_axis)
    barrier = pltpu.get_barrier_semaphore()
    for k in range(1, n):
        peer = lax.rem(me + k, n)
        pl.semaphore_signal(
            barrier, inc=1, device_id={axis: peer, other_axis: other}, device_id_type=pl.DeviceIdType.MESH
        )
    pl.semaphore_wait(barrier, n - 1)
    copies = []
    for k in range(1, n):
        peer = lax.rem(me + k, n)
        copy = pltpu.make_async_remote_copy(
            src_ref=send_ref.at[peer],
            dst_ref=recv_ref.at[me],
            send_sem=send_sem.at[k],
            recv_sem=recv_sem.at[k],
            device_id={axis: peer, other_axis: other},
            device_id_type=pl.DeviceIdType.MESH,
        )
        copy.start()
        copies.append(copy)
    own = pltpu.make_async_copy(send_ref.at[me], recv_ref.at[me], local_sem)
    own.start()
    own.wait()
    for copy in copies:
        copy.wait_send()
    for k in range(1, n):
        src = lax.rem(me + n - k, n)
        pltpu.make_async_remote_copy(
            src_ref=send_ref.at[src],
            dst_ref=recv_ref.at[src],
            send_sem=send_sem.at[k],
            recv_sem=recv_sem.at[k],
            device_id={axis: src, other_axis: other},
            device_id_type=pl.DeviceIdType.MESH,
        ).wait_recv()


def req_a2a(x, collective_id):
    n = x.shape[0]
    return pl.pallas_call(
        functools.partial(req_a2a_kernel, axis="req", other_axis="hist"),
        out_shape=jax.ShapeDtypeStruct(x.shape, x.dtype),
        in_specs=[pl.BlockSpec(memory_space=pl.ANY)],
        out_specs=pl.BlockSpec(memory_space=pl.ANY),
        scratch_shapes=[
            pltpu.SemaphoreType.DMA((n,)),
            pltpu.SemaphoreType.DMA((n,)),
            pltpu.SemaphoreType.DMA(()),
        ],
        compiler_params=pltpu.CompilerParams(collective_id=collective_id, has_side_effects=True),
    )(x)


def attend_kernel(len_ref, kv_ref, qsrc_ref, *rest, n_tiles, sub, tile_len, offset, q_row, score_scale, chunk):
    if len(rest) == 4:
        init_ref, out_ref, q_ref, o_ref = rest
    else:
        init_ref = out_ref = None
        o_ref, q_ref = rest
    length = len_ref[0]
    n_cls, _, head_dim = kv_ref.shape
    span = n_tiles * sub
    block = q_ref.shape[0] // n_cls
    half_scale = 0.5 * score_scale
    for b in range(n_cls):
        q_ref[pl.ds(b * block, block), :] = qsrc_ref[b, pl.ds(q_row, block), :]
    if init_ref is None:
        o_ref[...] = jnp.zeros_like(o_ref)
    else:
        o_ref[...] = init_ref[...]

    group = 4 if 4 * span <= 1024 else (1 if span % 128 == 0 else 2)

    def one_class(g, carry):
        c = g * group
        key_index = lax.broadcasted_iota(jnp.int32, (1, group * span), 1)
        cls = c + key_index // span
        within = key_index % span
        position = (cls + n_cls * (within // sub)) * tile_len + offset + within % sub
        live = position < length

        def add_class(masked):
            keys = jnp.concatenate([kv_ref[c + j, pl.ds(0, span), :] for j in range(group)], axis=0)
            values = jnp.concatenate([kv_ref[c + j, pl.ds(span, span), :] for j in range(group)], axis=0)
            for ci in range(q_ref.shape[0] // chunk):
                rows = pl.ds(ci * chunk, chunk)
                scores = lax.dot_general(
                    q_ref[rows, :], keys, (((1,), (1,)), ((), ())), preferred_element_type=jnp.float32
                )
                half = scores * half_scale
                weights = half + half * jnp.tanh(half)
                if masked:
                    weights = jnp.where(live, weights, 0.0)
                o_ref[rows, :] += jnp.dot(weights.astype(jnp.bfloat16), values, preferred_element_type=jnp.float32)

        last_key = (c + group - 1 + n_cls * (n_tiles - 1)) * tile_len + offset + sub
        whole = last_key <= length
        pl.when(whole)(lambda: add_class(False))
        pl.when(jnp.logical_and(jnp.logical_not(whole), c * tile_len + offset < length))(lambda: add_class(True))
        return carry

    lax.fori_loop(0, n_cls // group, one_class, 0)
    if out_ref is not None:
        out_ref[...] = o_ref[...].astype(out_ref.dtype)


def attend(length, kv_packed, q_packed, q_row, n_tiles, sub, tile_len, offset, score_scale, init=None):
    n_cls, _, head_dim = q_packed.shape
    rows = n_cls * (q_packed.shape[1] - q_row)
    chunk = 2048
    kernel = functools.partial(
        attend_kernel,
        n_tiles=n_tiles,
        sub=sub,
        tile_len=tile_len,
        offset=offset,
        q_row=q_row,
        score_scale=score_scale,
        chunk=chunk,
    )
    return pl.pallas_call(
        kernel,
        out_shape=jax.ShapeDtypeStruct((rows, head_dim), jnp.float32 if init is None else jnp.bfloat16),
        in_specs=[pl.BlockSpec(memory_space=pltpu.SMEM)]
        + [pl.BlockSpec(memory_space=pltpu.VMEM)] * (2 if init is None else 3),
        out_specs=pl.BlockSpec(memory_space=pltpu.VMEM),
        scratch_shapes=[pltpu.VMEM((rows, head_dim), jnp.bfloat16)]
        + ([] if init is None else [pltpu.VMEM((rows, head_dim), jnp.float32)]),
    )(length, kv_packed, q_packed, *([] if init is None else [init]))


def pack_kernel(picked_ref, tiles_hbm, *rest, heads, users, per_hist, with_q):
    if with_q:
        q_ref, out_ref, staged, in_sem = rest
    else:
        out_ref, staged, in_sem = rest
    width = tiles_hbm.shape[2] // 2
    head_dim = width // heads
    sub = tiles_hbm.shape[1]
    span = per_hist * sub
    n_in = users * per_hist
    reads = []
    for i in range(n_in):
        read = pltpu.make_async_copy(tiles_hbm.at[picked_ref[i]], staged.at[i], in_sem.at[i])
        read.start()
        reads.append(read)
    if with_q:
        cand_rows = q_ref.shape[1]
        for u in range(users):
            for e in range(heads):
                out_ref[u * heads + e, pl.ds(2 * span, cand_rows), :] = q_ref[u, :, pl.ds(e * head_dim, head_dim)]
    for i in range(n_in):
        u, t = divmod(i, per_hist)
        reads[i].wait()
        for piece in range(2 * heads):
            e, kv = divmod(piece, 2)
            out_ref[u * heads + e, pl.ds(kv * span + t * sub, sub), :] = staged[
                i, :, pl.ds(piece * head_dim, head_dim)
            ]


def pack_for_heads(picked_slot, tiles, queries, users, heads):
    n_in = picked_slot.shape[0]
    per_hist = n_in // users
    sub, wide = tiles.shape[1], tiles.shape[2]
    head_dim = wide // (2 * heads)
    rows = 2 * per_hist * sub + (0 if queries is None else queries.shape[1])
    operands = [picked_slot, tiles] + ([] if queries is None else [queries])
    return pl.pallas_call(
        functools.partial(pack_kernel, heads=heads, users=users, per_hist=per_hist, with_q=queries is not None),
        out_shape=jax.ShapeDtypeStruct((users * heads, rows, head_dim), tiles.dtype),
        in_specs=[pl.BlockSpec(memory_space=pltpu.SMEM), pl.BlockSpec(memory_space=pl.ANY)]
        + ([] if queries is None else [pl.BlockSpec(memory_space=pltpu.VMEM)]),
        out_specs=pl.BlockSpec(memory_space=pltpu.VMEM),
        scratch_shapes=[
            pltpu.VMEM((n_in, sub, wide), tiles.dtype),
            pltpu.SemaphoreType.DMA((n_in,)),
        ],
    )(*operands)


def finish_kernel(
    bias_ref, len_ref, limit_ref, hist_ref, proj_ref, x_ref, w_ref, out_ref, att_ref, *, heads, score_scale
):
    users, rows, width = x_ref.shape
    head_dim = width // heads
    for u in range(users):
        divisor = (len_ref[u] + 1).astype(jnp.float32)
        for e in range(heads):
            value = proj_ref[u, :, pl.ds(width + e * head_dim, head_dim)].astype(jnp.float32)
            query = proj_ref[u, :, pl.ds(2 * width + e * head_dim, head_dim)].astype(jnp.float32)
            key = proj_ref[u, :, pl.ds(3 * width + e * head_dim, head_dim)].astype(jnp.float32)
            self_score = jnp.sum(query * key, axis=-1, keepdims=True) * score_scale + bias_ref[e]
            own = self_score * (0.5 + 0.5 * jnp.tanh(0.5 * self_score)) * value
            history = hist_ref[u * heads + e].astype(jnp.float32)
            att_ref[:, pl.ds(e * head_dim, head_dim)] = (history + own) / divisor
        attended = att_ref[...]
        centred = attended - jnp.mean(attended, axis=-1, keepdims=True)
        spread = jnp.mean(centred * centred, axis=-1, keepdims=True)
        gate = proj_ref[u, :, pl.ds(0, width)].astype(jnp.float32)
        gated = (centred * lax.rsqrt(spread + 1e-05) * gate).astype(jnp.bfloat16)
        result = x_ref[u].astype(jnp.float32) + jnp.dot(gated, w_ref[...], preferred_element_type=jnp.float32)
        row = lax.broadcasted_iota(jnp.int32, (rows, 1), 0)
        out_ref[u] = jnp.where(row < limit_ref[u], result, 0.0).astype(out_ref.dtype)


def finish(history_back, projected, cand_x, w_out, self_bias, lengths, row_limit, heads, score_scale):
    users, rows, width = cand_x.shape
    smem = pl.BlockSpec(memory_space=pltpu.SMEM)
    vmem = pl.BlockSpec(memory_space=pltpu.VMEM)
    return pl.pallas_call(
        functools.partial(finish_kernel, heads=heads, score_scale=score_scale),
        out_shape=jax.ShapeDtypeStruct(cand_x.shape, cand_x.dtype),
        in_specs=[smem, smem, smem, vmem, vmem, vmem, vmem],
        out_specs=vmem,
        scratch_shapes=[pltpu.VMEM((rows, width), jnp.float32)],
    )(self_bias, lengths, row_limit, history_back, projected, cand_x, w_out)


def local(cand_x, kv_cache, w_uvqk, w_out, self_bias, user_rank, hist_len, cand_count, tile_slot):
    users_here, cand_rows, width = cand_x.shape
    heads = self_bias.shape[0]
    head_dim = width // heads
    score_scale = 1.0 / math.sqrt(head_dim)
    slots_own, tile_len, _ = kv_cache.shape
    user_total, tiles_max = tile_slot.shape
    req_count = lax.axis_size("req")
    hist_count = lax.axis_size("hist")
    req_index = lax.axis_index("req")
    hist_index = lax.axis_index("hist")
    per_hist = tiles_max // hist_count
    capacity = slots_own // req_count + 1
    first_slot = req_index * users_here
    user_ids = lax.dynamic_slice_in_dim(user_rank, first_slot, users_here)
    match_user = user_ids[:, None] == jnp.arange(user_total)[None, :]
    lengths = jnp.sum(jnp.where(match_user, hist_len[None, :], 0), axis=1)
    live_counts = jnp.sum(jnp.where(match_user, cand_count[None, :], 0), axis=1)
    column = lax.dynamic_index_in_dim(
        tile_slot.reshape(user_total, per_hist, hist_count), hist_index, axis=2, keepdims=False
    )
    codes = column.reshape(-1)
    owners = codes // slots_own
    local_slot = codes % slots_own
    dests = jnp.repeat(jnp.arange(user_total) // users_here, per_hist)
    entry_ids = jnp.arange(codes.shape[0])
    same_pair = (
        (owners[:, None] == owners[None, :])
        & (dests[:, None] == dests[None, :])
        & (entry_ids[:, None] > entry_ids[None, :])
    )
    places = jnp.sum(jnp.where(same_pair, 1, 0), axis=1)
    picked = (
        (owners[None, None, :] == req_index)
        & (dests[None, None, :] == jnp.arange(req_count)[:, None, None])
        & (places[None, None, :] == jnp.arange(capacity)[None, :, None])
    )
    source_slot = jnp.sum(jnp.where(picked, local_slot[None, None, :], 0), axis=2).reshape(-1)
    first_entry = first_slot * per_hist
    my_owner = lax.dynamic_slice_in_dim(owners, first_entry, users_here * per_hist)
    my_place = lax.dynamic_slice_in_dim(places, first_entry, users_here * per_hist)
    picked_slot = (my_owner * capacity + my_place).astype(jnp.int32)
    first_len = tile_len * 5 // 8
    bounds = [(0, first_len), (first_len, tile_len)]
    sending = []
    for lo, hi in bounds:
        kv_half = lax.slice_in_dim(kv_cache, lo, hi, axis=1)
        outgoing = kv_half.at[source_slot].get(mode="promise_in_bounds")
        sending.append(outgoing.reshape(req_count, capacity, hi - lo, 2 * width))
    first_in = lax.all_to_all(sending[0], "req", split_axis=0, concat_axis=0, tiled=True)
    normed = layer_norm(cand_x.astype(jnp.float32)).astype(jnp.bfloat16)
    mixed_in = jnp.dot(normed.reshape(-1, width), w_uvqk, preferred_element_type=jnp.float32)
    projected = jax.nn.silu(mixed_in).astype(jnp.bfloat16).reshape(users_here, cand_rows, 4, width)
    projected, second_out = lax.optimization_barrier((projected, sending[1]))
    second_in = req_a2a(second_out, 0)
    halves = [
        first_in.reshape(req_count * capacity, first_len, 2 * width),
        second_in.reshape(req_count * capacity, tile_len - first_len, 2 * width),
    ]
    u_gate = projected[:, :, 0]
    v_self = projected[:, :, 1]
    queries = projected[:, :, 2]
    k_self = projected[:, :, 3]
    my_user = hist_index // heads
    my_length = lax.dynamic_slice_in_dim(lengths, my_user, 1)
    q_row = 2 * per_hist * first_len
    packed_a = lax.all_to_all(
        pack_for_heads(picked_slot, halves[0], queries, users_here, heads),
        "hist", split_axis=0, concat_axis=0, tiled=True,
    )
    history_mine = attend(my_length, packed_a, packed_a, q_row, per_hist, first_len, tile_len, 0, score_scale)
    packed_b = lax.all_to_all(
        pack_for_heads(picked_slot, halves[1], None, users_here, heads),
        "hist", split_axis=0, concat_axis=0, tiled=True,
    )
    history_mine = attend(
        my_length, packed_b, packed_a, q_row, per_hist, tile_len - first_len, tile_len, first_len, score_scale,
        init=history_mine,
    )
    history_back = lax.all_to_all(
        history_mine.reshape(hist_count, cand_rows, head_dim), "hist", split_axis=0, concat_axis=0, tiled=True
    )
    row_limit = (live_counts - hist_index * cand_rows).astype(jnp.int32)
    return finish(
        history_back, projected.reshape(users_here, cand_rows, 4 * width), cand_x, w_out, self_bias,
        lengths.astype(jnp.int32), row_limit, heads, score_scale,
    )


def solution(mesh):
    return jax.shard_map(
        local,
        mesh=mesh,
        in_specs=(
            P("req", "hist", None),
            P(("req", "hist"), None, None),
            P(),
            P(),
            P(),
            P(),
            P(),
            P(),
            P(),
        ),
        out_specs=P("req", "hist", None),
        check_vma=False,
    )
```

```python
import functools
import math

import jax
import jax.numpy as jnp
from jax import lax
from jax.experimental import pallas as pl
from jax.experimental.pallas import tpu as pltpu
from jax.sharding import PartitionSpec as P


def layer_norm(values):
    mean_value = jnp.mean(values, axis=-1, keepdims=True)
    centred = values - mean_value
    spread = jnp.mean(centred * centred, axis=-1, keepdims=True)
    return centred * lax.rsqrt(spread + 1e-05)


def silu_tanh(values):
    return values * (0.5 + 0.5 * jnp.tanh(0.5 * values))


def req_a2a_kernel(send_ref, recv_ref, send_sem, recv_sem, local_sem, *, axis, other_axis):
    n = send_ref.shape[0]
    me = lax.axis_index(axis)
    other = lax.axis_index(other_axis)
    barrier = pltpu.get_barrier_semaphore()
    for k in range(1, n):
        peer = lax.rem(me + k, n)
        pl.semaphore_signal(
            barrier, inc=1, device_id={axis: peer, other_axis: other}, device_id_type=pl.DeviceIdType.MESH
        )
    pl.semaphore_wait(barrier, n - 1)
    copies = []
    for k in range(1, n):
        peer = lax.rem(me + k, n)
        copy = pltpu.make_async_remote_copy(
            src_ref=send_ref.at[peer],
            dst_ref=recv_ref.at[me],
            send_sem=send_sem.at[k],
            recv_sem=recv_sem.at[k],
            device_id={axis: peer, other_axis: other},
            device_id_type=pl.DeviceIdType.MESH,
        )
        copy.start()
        copies.append(copy)
    own = pltpu.make_async_copy(send_ref.at[me], recv_ref.at[me], local_sem)
    own.start()
    own.wait()
    for copy in copies:
        copy.wait_send()
    for k in range(1, n):
        src = lax.rem(me + n - k, n)
        pltpu.make_async_remote_copy(
            src_ref=send_ref.at[src],
            dst_ref=recv_ref.at[src],
            send_sem=send_sem.at[k],
            recv_sem=recv_sem.at[k],
            device_id={axis: src, other_axis: other},
            device_id_type=pl.DeviceIdType.MESH,
        ).wait_recv()


def req_a2a(x, collective_id):
    n = x.shape[0]
    return pl.pallas_call(
        functools.partial(req_a2a_kernel, axis="req", other_axis="hist"),
        out_shape=jax.ShapeDtypeStruct(x.shape, x.dtype),
        in_specs=[pl.BlockSpec(memory_space=pl.ANY)],
        out_specs=pl.BlockSpec(memory_space=pl.ANY),
        scratch_shapes=[
            pltpu.SemaphoreType.DMA((n,)),
            pltpu.SemaphoreType.DMA((n,)),
            pltpu.SemaphoreType.DMA(()),
        ],
        compiler_params=pltpu.CompilerParams(collective_id=collective_id, has_side_effects=True),
    )(x)


def attend_kernel(len_ref, kv_ref, qsrc_ref, *rest, n_tiles, sub, tile_len, offset, q_row, score_scale, chunk):
    if len(rest) == 4:
        init_ref, out_ref, q_ref, o_ref = rest
    else:
        init_ref = out_ref = None
        o_ref, q_ref = rest
    length = len_ref[0]
    n_cls, _, head_dim = kv_ref.shape
    span = n_tiles * sub
    block = q_ref.shape[0] // n_cls
    half_scale = 0.5 * score_scale
    for b in range(n_cls):
        q_ref[pl.ds(b * block, block), :] = qsrc_ref[b, pl.ds(q_row, block), :]
    if init_ref is None:
        o_ref[...] = jnp.zeros_like(o_ref)
    else:
        o_ref[...] = init_ref[...]

    group = 4 if 4 * span <= 1280 else (1 if span % 128 == 0 else 2)

    def one_class(g, carry):
        c = g * group
        key_index = lax.broadcasted_iota(jnp.int32, (1, group * span), 1)
        cls = c + key_index // span
        within = key_index % span
        position = (cls + n_cls * (within // sub)) * tile_len + offset + within % sub
        live = position < length

        def add_class(masked):
            keys = jnp.concatenate([kv_ref[c + j, pl.ds(0, span), :] for j in range(group)], axis=0)
            values = jnp.concatenate([kv_ref[c + j, pl.ds(span, span), :] for j in range(group)], axis=0)
            for ci in range(q_ref.shape[0] // chunk):
                rows = pl.ds(ci * chunk, chunk)
                scores = lax.dot_general(
                    q_ref[rows, :], keys, (((1,), (1,)), ((), ())), preferred_element_type=jnp.float32
                )
                half = scores * half_scale
                weights = half + half * jnp.tanh(half)
                if masked:
                    weights = jnp.where(live, weights, 0.0)
                o_ref[rows, :] += jnp.dot(weights.astype(jnp.bfloat16), values, preferred_element_type=jnp.float32)

        last_key = (c + group - 1 + n_cls * (n_tiles - 1)) * tile_len + offset + sub
        whole = last_key <= length
        pl.when(whole)(lambda: add_class(False))
        pl.when(jnp.logical_and(jnp.logical_not(whole), c * tile_len + offset < length))(lambda: add_class(True))
        return carry

    lax.fori_loop(0, n_cls // group, one_class, 0)
    if out_ref is not None:
        out_ref[...] = o_ref[...].astype(out_ref.dtype)


def attend(length, kv_packed, q_packed, q_row, n_tiles, sub, tile_len, offset, score_scale, init=None):
    n_cls, _, head_dim = q_packed.shape
    rows = n_cls * (q_packed.shape[1] - q_row)
    chunk = 2048
    kernel = functools.partial(
        attend_kernel,
        n_tiles=n_tiles,
        sub=sub,
        tile_len=tile_len,
        offset=offset,
        q_row=q_row,
        score_scale=score_scale,
        chunk=chunk,
    )
    return pl.pallas_call(
        kernel,
        out_shape=jax.ShapeDtypeStruct((rows, head_dim), jnp.float32 if init is None else jnp.bfloat16),
        in_specs=[pl.BlockSpec(memory_space=pltpu.SMEM)]
        + [pl.BlockSpec(memory_space=pltpu.VMEM)] * (2 if init is None else 3),
        out_specs=pl.BlockSpec(memory_space=pltpu.VMEM),
        scratch_shapes=[pltpu.VMEM((rows, head_dim), jnp.bfloat16)]
        + ([] if init is None else [pltpu.VMEM((rows, head_dim), jnp.float32)]),
    )(length, kv_packed, q_packed, *([] if init is None else [init]))


def pack_kernel(picked_ref, tiles_hbm, *rest, heads, users, per_hist, with_q):
    if with_q:
        q_ref, out_ref, staged, in_sem = rest
    else:
        out_ref, staged, in_sem = rest
    width = tiles_hbm.shape[2] // 2
    head_dim = width // heads
    sub = tiles_hbm.shape[1]
    span = per_hist * sub
    n_in = users * per_hist
    reads = []
    for i in range(n_in):
        read = pltpu.make_async_copy(tiles_hbm.at[picked_ref[i]], staged.at[i], in_sem.at[i])
        read.start()
        reads.append(read)
    if with_q:
        cand_rows = q_ref.shape[1]
        for u in range(users):
            for e in range(heads):
                out_ref[u * heads + e, pl.ds(2 * span, cand_rows), :] = q_ref[u, :, pl.ds(e * head_dim, head_dim)]
    for i in range(n_in):
        u, t = divmod(i, per_hist)
        reads[i].wait()
        for piece in range(2 * heads):
            e, kv = divmod(piece, 2)
            out_ref[u * heads + e, pl.ds(kv * span + t * sub, sub), :] = staged[
                i, :, pl.ds(piece * head_dim, head_dim)
            ]


def pack_for_heads(picked_slot, tiles, queries, users, heads):
    n_in = picked_slot.shape[0]
    per_hist = n_in // users
    sub, wide = tiles.shape[1], tiles.shape[2]
    head_dim = wide // (2 * heads)
    rows = 2 * per_hist * sub + (0 if queries is None else queries.shape[1])
    operands = [picked_slot, tiles] + ([] if queries is None else [queries])
    return pl.pallas_call(
        functools.partial(pack_kernel, heads=heads, users=users, per_hist=per_hist, with_q=queries is not None),
        out_shape=jax.ShapeDtypeStruct((users * heads, rows, head_dim), tiles.dtype),
        in_specs=[pl.BlockSpec(memory_space=pltpu.SMEM), pl.BlockSpec(memory_space=pl.ANY)]
        + ([] if queries is None else [pl.BlockSpec(memory_space=pltpu.VMEM)]),
        out_specs=pl.BlockSpec(memory_space=pltpu.VMEM),
        scratch_shapes=[
            pltpu.VMEM((n_in, sub, wide), tiles.dtype),
            pltpu.SemaphoreType.DMA((n_in,)),
        ],
    )(*operands)


def finish_kernel(
    bias_ref, len_ref, limit_ref, hist_ref, proj_ref, x_ref, w_ref, out_ref, att_ref, *, heads, score_scale
):
    users, rows, width = x_ref.shape
    head_dim = width // heads
    for u in range(users):
        divisor = (len_ref[u] + 1).astype(jnp.float32)
        for e in range(heads):
            value = proj_ref[u, :, pl.ds(width + e * head_dim, head_dim)].astype(jnp.float32)
            query = proj_ref[u, :, pl.ds(2 * width + e * head_dim, head_dim)].astype(jnp.float32)
            key = proj_ref[u, :, pl.ds(3 * width + e * head_dim, head_dim)].astype(jnp.float32)
            self_score = jnp.sum(query * key, axis=-1, keepdims=True) * score_scale + bias_ref[e]
            own = self_score * (0.5 + 0.5 * jnp.tanh(0.5 * self_score)) * value
            history = hist_ref[u * heads + e].astype(jnp.float32)
            att_ref[:, pl.ds(e * head_dim, head_dim)] = (history + own) / divisor
        attended = att_ref[...]
        centred = attended - jnp.mean(attended, axis=-1, keepdims=True)
        spread = jnp.mean(centred * centred, axis=-1, keepdims=True)
        gate = proj_ref[u, :, pl.ds(0, width)].astype(jnp.float32)
        gated = (centred * lax.rsqrt(spread + 1e-05) * gate).astype(jnp.bfloat16)
        result = x_ref[u].astype(jnp.float32) + jnp.dot(gated, w_ref[...], preferred_element_type=jnp.float32)
        row = lax.broadcasted_iota(jnp.int32, (rows, 1), 0)
        out_ref[u] = jnp.where(row < limit_ref[u], result, 0.0).astype(out_ref.dtype)


def finish(history_back, projected, cand_x, w_out, self_bias, lengths, row_limit, heads, score_scale):
    users, rows, width = cand_x.shape
    smem = pl.BlockSpec(memory_space=pltpu.SMEM)
    vmem = pl.BlockSpec(memory_space=pltpu.VMEM)
    return pl.pallas_call(
        functools.partial(finish_kernel, heads=heads, score_scale=score_scale),
        out_shape=jax.ShapeDtypeStruct(cand_x.shape, cand_x.dtype),
        in_specs=[smem, smem, smem, vmem, vmem, vmem, vmem],
        out_specs=vmem,
        scratch_shapes=[pltpu.VMEM((rows, width), jnp.float32)],
    )(self_bias, lengths, row_limit, history_back, projected, cand_x, w_out)


def local(cand_x, kv_cache, w_uvqk, w_out, self_bias, user_rank, hist_len, cand_count, tile_slot):
    users_here, cand_rows, width = cand_x.shape
    heads = self_bias.shape[0]
    head_dim = width // heads
    score_scale = 1.0 / math.sqrt(head_dim)
    slots_own, tile_len, _ = kv_cache.shape
    user_total, tiles_max = tile_slot.shape
    req_count = lax.axis_size("req")
    hist_count = lax.axis_size("hist")
    req_index = lax.axis_index("req")
    hist_index = lax.axis_index("hist")
    per_hist = tiles_max // hist_count
    capacity = slots_own // req_count + 1
    first_slot = req_index * users_here
    user_ids = lax.dynamic_slice_in_dim(user_rank, first_slot, users_here)
    match_user = user_ids[:, None] == jnp.arange(user_total)[None, :]
    lengths = jnp.sum(jnp.where(match_user, hist_len[None, :], 0), axis=1)
    live_counts = jnp.sum(jnp.where(match_user, cand_count[None, :], 0), axis=1)
    column = lax.dynamic_index_in_dim(
        tile_slot.reshape(user_total, per_hist, hist_count), hist_index, axis=2, keepdims=False
    )
    codes = column.reshape(-1)
    owners = codes // slots_own
    local_slot = codes % slots_own
    dests = jnp.repeat(jnp.arange(user_total) // users_here, per_hist)
    entry_ids = jnp.arange(codes.shape[0])
    same_pair = (
        (owners[:, None] == owners[None, :])
        & (dests[:, None] == dests[None, :])
        & (entry_ids[:, None] > entry_ids[None, :])
    )
    places = jnp.sum(jnp.where(same_pair, 1, 0), axis=1)
    picked = (
        (owners[None, None, :] == req_index)
        & (dests[None, None, :] == jnp.arange(req_count)[:, None, None])
        & (places[None, None, :] == jnp.arange(capacity)[None, :, None])
    )
    source_slot = jnp.sum(jnp.where(picked, local_slot[None, None, :], 0), axis=2).reshape(-1)
    first_entry = first_slot * per_hist
    my_owner = lax.dynamic_slice_in_dim(owners, first_entry, users_here * per_hist)
    my_place = lax.dynamic_slice_in_dim(places, first_entry, users_here * per_hist)
    picked_slot = (my_owner * capacity + my_place).astype(jnp.int32)
    first_len = tile_len * 5 // 8
    bounds = [(0, first_len), (first_len, tile_len)]
    sending = []
    for lo, hi in bounds:
        kv_half = lax.slice_in_dim(kv_cache, lo, hi, axis=1)
        outgoing = kv_half.at[source_slot].get(mode="promise_in_bounds")
        sending.append(outgoing.reshape(req_count, capacity, hi - lo, 2 * width))
    first_in = lax.all_to_all(sending[0], "req", split_axis=0, concat_axis=0, tiled=True)
    normed = layer_norm(cand_x.astype(jnp.float32)).astype(jnp.bfloat16)
    mixed_in = jnp.dot(normed.reshape(-1, width), w_uvqk, preferred_element_type=jnp.float32)
    projected = jax.nn.silu(mixed_in).astype(jnp.bfloat16).reshape(users_here, cand_rows, 4, width)
    projected, second_out = lax.optimization_barrier((projected, sending[1]))
    second_in = req_a2a(second_out, 0)
    halves = [
        first_in.reshape(req_count * capacity, first_len, 2 * width),
        second_in.reshape(req_count * capacity, tile_len - first_len, 2 * width),
    ]
    u_gate = projected[:, :, 0]
    v_self = projected[:, :, 1]
    queries = projected[:, :, 2]
    k_self = projected[:, :, 3]
    my_user = hist_index // heads
    my_length = lax.dynamic_slice_in_dim(lengths, my_user, 1)
    q_row = 2 * per_hist * first_len
    packed_a = lax.all_to_all(
        pack_for_heads(picked_slot, halves[0], queries, users_here, heads),
        "hist", split_axis=0, concat_axis=0, tiled=True,
    )
    history_mine = attend(my_length, packed_a, packed_a, q_row, per_hist, first_len, tile_len, 0, score_scale)
    packed_b = lax.all_to_all(
        pack_for_heads(picked_slot, halves[1], None, users_here, heads),
        "hist", split_axis=0, concat_axis=0, tiled=True,
    )
    history_mine = attend(
        my_length, packed_b, packed_a, q_row, per_hist, tile_len - first_len, tile_len, first_len, score_scale,
        init=history_mine,
    )
    history_back = lax.all_to_all(
        history_mine.reshape(hist_count, cand_rows, head_dim), "hist", split_axis=0, concat_axis=0, tiled=True
    )
    row_limit = (live_counts - hist_index * cand_rows).astype(jnp.int32)
    return finish(
        history_back, projected.reshape(users_here, cand_rows, 4 * width), cand_x, w_out, self_bias,
        lengths.astype(jnp.int32), row_limit, heads, score_scale,
    )


def solution(mesh):
    return jax.shard_map(
        local,
        mesh=mesh,
        in_specs=(
            P("req", "hist", None),
            P(("req", "hist"), None, None),
            P(),
            P(),
            P(),
            P(),
            P(),
            P(),
            P(),
        ),
        out_specs=P("req", "hist", None),
        check_vma=False,
    )
```

```python
import functools
import math

import jax
import jax.numpy as jnp
from jax import lax
from jax.experimental import pallas as pl
from jax.experimental.pallas import tpu as pltpu
from jax.sharding import PartitionSpec as P


def layer_norm(values):
    mean_value = jnp.mean(values, axis=-1, keepdims=True)
    centred = values - mean_value
    spread = jnp.mean(centred * centred, axis=-1, keepdims=True)
    return centred * lax.rsqrt(spread + 1e-05)


def silu_tanh(values):
    return values * (0.5 + 0.5 * jnp.tanh(0.5 * values))


def req_a2a_kernel(send_ref, recv_ref, send_sem, recv_sem, local_sem, *, axis, other_axis):
    n = send_ref.shape[0]
    me = lax.axis_index(axis)
    other = lax.axis_index(other_axis)
    barrier = pltpu.get_barrier_semaphore()
    for k in range(1, n):
        peer = lax.rem(me + k, n)
        pl.semaphore_signal(
            barrier, inc=1, device_id={axis: peer, other_axis: other}, device_id_type=pl.DeviceIdType.MESH
        )
    pl.semaphore_wait(barrier, n - 1)
    copies = []
    for k in range(1, n):
        peer = lax.rem(me + k, n)
        copy = pltpu.make_async_remote_copy(
            src_ref=send_ref.at[peer],
            dst_ref=recv_ref.at[me],
            send_sem=send_sem.at[k],
            recv_sem=recv_sem.at[k],
            device_id={axis: peer, other_axis: other},
            device_id_type=pl.DeviceIdType.MESH,
        )
        copy.start()
        copies.append(copy)
    own = pltpu.make_async_copy(send_ref.at[me], recv_ref.at[me], local_sem)
    own.start()
    own.wait()
    for copy in copies:
        copy.wait_send()
    for k in range(1, n):
        src = lax.rem(me + n - k, n)
        pltpu.make_async_remote_copy(
            src_ref=send_ref.at[src],
            dst_ref=recv_ref.at[src],
            send_sem=send_sem.at[k],
            recv_sem=recv_sem.at[k],
            device_id={axis: src, other_axis: other},
            device_id_type=pl.DeviceIdType.MESH,
        ).wait_recv()


def req_a2a(x, collective_id):
    n = x.shape[0]
    return pl.pallas_call(
        functools.partial(req_a2a_kernel, axis="req", other_axis="hist"),
        out_shape=jax.ShapeDtypeStruct(x.shape, x.dtype),
        in_specs=[pl.BlockSpec(memory_space=pl.ANY)],
        out_specs=pl.BlockSpec(memory_space=pl.ANY),
        scratch_shapes=[
            pltpu.SemaphoreType.DMA((n,)),
            pltpu.SemaphoreType.DMA((n,)),
            pltpu.SemaphoreType.DMA(()),
        ],
        compiler_params=pltpu.CompilerParams(collective_id=collective_id, has_side_effects=True),
    )(x)


def attend_kernel(len_ref, kv_ref, qsrc_ref, *rest, n_tiles, sub, tile_len, offset, q_row, score_scale, chunk):
    if len(rest) == 4:
        init_ref, out_ref, q_ref, o_ref = rest
    else:
        init_ref = out_ref = None
        o_ref, q_ref = rest
    length = len_ref[0]
    n_cls, _, head_dim = kv_ref.shape
    span = n_tiles * sub
    block = q_ref.shape[0] // n_cls
    half_scale = 0.5 * score_scale
    for b in range(n_cls):
        q_ref[pl.ds(b * block, block), :] = qsrc_ref[b, pl.ds(q_row, block), :]
    if init_ref is None:
        o_ref[...] = jnp.zeros_like(o_ref)
    else:
        o_ref[...] = init_ref[...]

    group = 8 if 8 * span <= 1536 else (4 if 4 * span <= 1280 else (1 if span % 128 == 0 else 2))

    def one_class(g, carry):
        c = g * group
        key_index = lax.broadcasted_iota(jnp.int32, (1, group * span), 1)
        cls = c + key_index // span
        within = key_index % span
        position = (cls + n_cls * (within // sub)) * tile_len + offset + within % sub
        live = position < length

        def add_class(masked):
            keys = jnp.concatenate([kv_ref[c + j, pl.ds(0, span), :] for j in range(group)], axis=0)
            values = jnp.concatenate([kv_ref[c + j, pl.ds(span, span), :] for j in range(group)], axis=0)
            for ci in range(q_ref.shape[0] // chunk):
                rows = pl.ds(ci * chunk, chunk)
                scores = lax.dot_general(
                    q_ref[rows, :], keys, (((1,), (1,)), ((), ())), preferred_element_type=jnp.float32
                )
                half = scores * half_scale
                weights = half + half * jnp.tanh(half)
                if masked:
                    weights = jnp.where(live, weights, 0.0)
                o_ref[rows, :] += jnp.dot(weights.astype(jnp.bfloat16), values, preferred_element_type=jnp.float32)

        last_key = (c + group - 1 + n_cls * (n_tiles - 1)) * tile_len + offset + sub
        whole = last_key <= length
        pl.when(whole)(lambda: add_class(False))
        pl.when(jnp.logical_and(jnp.logical_not(whole), c * tile_len + offset < length))(lambda: add_class(True))
        return carry

    lax.fori_loop(0, n_cls // group, one_class, 0)
    if out_ref is not None:
        out_ref[...] = o_ref[...].astype(out_ref.dtype)


def attend(length, kv_packed, q_packed, q_row, n_tiles, sub, tile_len, offset, score_scale, init=None):
    n_cls, _, head_dim = q_packed.shape
    rows = n_cls * (q_packed.shape[1] - q_row)
    chunk = 2048
    kernel = functools.partial(
        attend_kernel,
        n_tiles=n_tiles,
        sub=sub,
        tile_len=tile_len,
        offset=offset,
        q_row=q_row,
        score_scale=score_scale,
        chunk=chunk,
    )
    return pl.pallas_call(
        kernel,
        out_shape=jax.ShapeDtypeStruct((rows, head_dim), jnp.float32 if init is None else jnp.bfloat16),
        in_specs=[pl.BlockSpec(memory_space=pltpu.SMEM)]
        + [pl.BlockSpec(memory_space=pltpu.VMEM)] * (2 if init is None else 3),
        out_specs=pl.BlockSpec(memory_space=pltpu.VMEM),
        scratch_shapes=[pltpu.VMEM((rows, head_dim), jnp.bfloat16)]
        + ([] if init is None else [pltpu.VMEM((rows, head_dim), jnp.float32)]),
    )(length, kv_packed, q_packed, *([] if init is None else [init]))


def pack_kernel(picked_ref, tiles_hbm, *rest, heads, users, per_hist, with_q):
    if with_q:
        q_ref, out_ref, staged, in_sem = rest
    else:
        out_ref, staged, in_sem = rest
    width = tiles_hbm.shape[2] // 2
    head_dim = width // heads
    sub = tiles_hbm.shape[1]
    span = per_hist * sub
    n_in = users * per_hist
    reads = []
    for i in range(n_in):
        read = pltpu.make_async_copy(tiles_hbm.at[picked_ref[i]], staged.at[i], in_sem.at[i])
        read.start()
        reads.append(read)
    if with_q:
        cand_rows = q_ref.shape[1]
        for u in range(users):
            for e in range(heads):
                out_ref[u * heads + e, pl.ds(2 * span, cand_rows), :] = q_ref[u, :, pl.ds(e * head_dim, head_dim)]
    for i in range(n_in):
        u, t = divmod(i, per_hist)
        reads[i].wait()
        for piece in range(2 * heads):
            e, kv = divmod(piece, 2)
            out_ref[u * heads + e, pl.ds(kv * span + t * sub, sub), :] = staged[
                i, :, pl.ds(piece * head_dim, head_dim)
            ]


def pack_for_heads(picked_slot, tiles, queries, users, heads):
    n_in = picked_slot.shape[0]
    per_hist = n_in // users
    sub, wide = tiles.shape[1], tiles.shape[2]
    head_dim = wide // (2 * heads)
    rows = 2 * per_hist * sub + (0 if queries is None else queries.shape[1])
    operands = [picked_slot, tiles] + ([] if queries is None else [queries])
    return pl.pallas_call(
        functools.partial(pack_kernel, heads=heads, users=users, per_hist=per_hist, with_q=queries is not None),
        out_shape=jax.ShapeDtypeStruct((users * heads, rows, head_dim), tiles.dtype),
        in_specs=[pl.BlockSpec(memory_space=pltpu.SMEM), pl.BlockSpec(memory_space=pl.ANY)]
        + ([] if queries is None else [pl.BlockSpec(memory_space=pltpu.VMEM)]),
        out_specs=pl.BlockSpec(memory_space=pltpu.VMEM),
        scratch_shapes=[
            pltpu.VMEM((n_in, sub, wide), tiles.dtype),
            pltpu.SemaphoreType.DMA((n_in,)),
        ],
    )(*operands)


def finish_kernel(
    bias_ref, len_ref, limit_ref, hist_ref, proj_ref, x_ref, w_ref, out_ref, att_ref, *, heads, score_scale
):
    users, rows, width = x_ref.shape
    head_dim = width // heads
    for u in range(users):
        divisor = (len_ref[u] + 1).astype(jnp.float32)
        for e in range(heads):
            value = proj_ref[u, :, pl.ds(width + e * head_dim, head_dim)].astype(jnp.float32)
            query = proj_ref[u, :, pl.ds(2 * width + e * head_dim, head_dim)].astype(jnp.float32)
            key = proj_ref[u, :, pl.ds(3 * width + e * head_dim, head_dim)].astype(jnp.float32)
            self_score = jnp.sum(query * key, axis=-1, keepdims=True) * score_scale + bias_ref[e]
            own = self_score * (0.5 + 0.5 * jnp.tanh(0.5 * self_score)) * value
            history = hist_ref[u * heads + e].astype(jnp.float32)
            att_ref[:, pl.ds(e * head_dim, head_dim)] = (history + own) / divisor
        attended = att_ref[...]
        centred = attended - jnp.mean(attended, axis=-1, keepdims=True)
        spread = jnp.mean(centred * centred, axis=-1, keepdims=True)
        gate = proj_ref[u, :, pl.ds(0, width)].astype(jnp.float32)
        gated = (centred * lax.rsqrt(spread + 1e-05) * gate).astype(jnp.bfloat16)
        result = x_ref[u].astype(jnp.float32) + jnp.dot(gated, w_ref[...], preferred_element_type=jnp.float32)
        row = lax.broadcasted_iota(jnp.int32, (rows, 1), 0)
        out_ref[u] = jnp.where(row < limit_ref[u], result, 0.0).astype(out_ref.dtype)


def finish(history_back, projected, cand_x, w_out, self_bias, lengths, row_limit, heads, score_scale):
    users, rows, width = cand_x.shape
    smem = pl.BlockSpec(memory_space=pltpu.SMEM)
    vmem = pl.BlockSpec(memory_space=pltpu.VMEM)
    return pl.pallas_call(
        functools.partial(finish_kernel, heads=heads, score_scale=score_scale),
        out_shape=jax.ShapeDtypeStruct(cand_x.shape, cand_x.dtype),
        in_specs=[smem, smem, smem, vmem, vmem, vmem, vmem],
        out_specs=vmem,
        scratch_shapes=[pltpu.VMEM((rows, width), jnp.float32)],
    )(self_bias, lengths, row_limit, history_back, projected, cand_x, w_out)


def local(cand_x, kv_cache, w_uvqk, w_out, self_bias, user_rank, hist_len, cand_count, tile_slot):
    users_here, cand_rows, width = cand_x.shape
    heads = self_bias.shape[0]
    head_dim = width // heads
    score_scale = 1.0 / math.sqrt(head_dim)
    slots_own, tile_len, _ = kv_cache.shape
    user_total, tiles_max = tile_slot.shape
    req_count = lax.axis_size("req")
    hist_count = lax.axis_size("hist")
    req_index = lax.axis_index("req")
    hist_index = lax.axis_index("hist")
    per_hist = tiles_max // hist_count
    capacity = slots_own // req_count + 1
    first_slot = req_index * users_here
    user_ids = lax.dynamic_slice_in_dim(user_rank, first_slot, users_here)
    match_user = user_ids[:, None] == jnp.arange(user_total)[None, :]
    lengths = jnp.sum(jnp.where(match_user, hist_len[None, :], 0), axis=1)
    live_counts = jnp.sum(jnp.where(match_user, cand_count[None, :], 0), axis=1)
    column = lax.dynamic_index_in_dim(
        tile_slot.reshape(user_total, per_hist, hist_count), hist_index, axis=2, keepdims=False
    )
    codes = column.reshape(-1)
    owners = codes // slots_own
    local_slot = codes % slots_own
    dests = jnp.repeat(jnp.arange(user_total) // users_here, per_hist)
    entry_ids = jnp.arange(codes.shape[0])
    same_pair = (
        (owners[:, None] == owners[None, :])
        & (dests[:, None] == dests[None, :])
        & (entry_ids[:, None] > entry_ids[None, :])
    )
    places = jnp.sum(jnp.where(same_pair, 1, 0), axis=1)
    picked = (
        (owners[None, None, :] == req_index)
        & (dests[None, None, :] == jnp.arange(req_count)[:, None, None])
        & (places[None, None, :] == jnp.arange(capacity)[None, :, None])
    )
    source_slot = jnp.sum(jnp.where(picked, local_slot[None, None, :], 0), axis=2).reshape(-1)
    first_entry = first_slot * per_hist
    my_owner = lax.dynamic_slice_in_dim(owners, first_entry, users_here * per_hist)
    my_place = lax.dynamic_slice_in_dim(places, first_entry, users_here * per_hist)
    picked_slot = (my_owner * capacity + my_place).astype(jnp.int32)
    first_len = tile_len * 5 // 8
    bounds = [(0, first_len), (first_len, tile_len)]
    sending = []
    for lo, hi in bounds:
        kv_half = lax.slice_in_dim(kv_cache, lo, hi, axis=1)
        outgoing = kv_half.at[source_slot].get(mode="promise_in_bounds")
        sending.append(outgoing.reshape(req_count, capacity, hi - lo, 2 * width))
    first_in = lax.all_to_all(sending[0], "req", split_axis=0, concat_axis=0, tiled=True)
    normed = layer_norm(cand_x.astype(jnp.float32)).astype(jnp.bfloat16)
    mixed_in = jnp.dot(normed.reshape(-1, width), w_uvqk, preferred_element_type=jnp.float32)
    projected = jax.nn.silu(mixed_in).astype(jnp.bfloat16).reshape(users_here, cand_rows, 4, width)
    projected, second_out = lax.optimization_barrier((projected, sending[1]))
    second_in = req_a2a(second_out, 0)
    halves = [
        first_in.reshape(req_count * capacity, first_len, 2 * width),
        second_in.reshape(req_count * capacity, tile_len - first_len, 2 * width),
    ]
    u_gate = projected[:, :, 0]
    v_self = projected[:, :, 1]
    queries = projected[:, :, 2]
    k_self = projected[:, :, 3]
    my_user = hist_index // heads
    my_length = lax.dynamic_slice_in_dim(lengths, my_user, 1)
    q_row = 2 * per_hist * first_len
    packed_a = lax.all_to_all(
        pack_for_heads(picked_slot, halves[0], queries, users_here, heads),
        "hist", split_axis=0, concat_axis=0, tiled=True,
    )
    history_mine = attend(my_length, packed_a, packed_a, q_row, per_hist, first_len, tile_len, 0, score_scale)
    packed_b = lax.all_to_all(
        pack_for_heads(picked_slot, halves[1], None, users_here, heads),
        "hist", split_axis=0, concat_axis=0, tiled=True,
    )
    history_mine = attend(
        my_length, packed_b, packed_a, q_row, per_hist, tile_len - first_len, tile_len, first_len, score_scale,
        init=history_mine,
    )
    history_back = lax.all_to_all(
        history_mine.reshape(hist_count, cand_rows, head_dim), "hist", split_axis=0, concat_axis=0, tiled=True
    )
    row_limit = (live_counts - hist_index * cand_rows).astype(jnp.int32)
    return finish(
        history_back, projected.reshape(users_here, cand_rows, 4 * width), cand_x, w_out, self_bias,
        lengths.astype(jnp.int32), row_limit, heads, score_scale,
    )


def solution(mesh):
    return jax.shard_map(
        local,
        mesh=mesh,
        in_specs=(
            P("req", "hist", None),
            P(("req", "hist"), None, None),
            P(),
            P(),
            P(),
            P(),
            P(),
            P(),
            P(),
        ),
        out_specs=P("req", "hist", None),
        check_vma=False,
    )
```

```python
import functools
import math

import jax
import jax.numpy as jnp
from jax import lax
from jax.experimental import pallas as pl
from jax.experimental.pallas import tpu as pltpu
from jax.sharding import PartitionSpec as P


def layer_norm(values):
    mean_value = jnp.mean(values, axis=-1, keepdims=True)
    centred = values - mean_value
    spread = jnp.mean(centred * centred, axis=-1, keepdims=True)
    return centred * lax.rsqrt(spread + 1e-05)


def silu_tanh(values):
    return values * (0.5 + 0.5 * jnp.tanh(0.5 * values))


def req_a2a_kernel(send_ref, recv_ref, send_sem, recv_sem, local_sem, *, axis, other_axis):
    n = send_ref.shape[0]
    me = lax.axis_index(axis)
    other = lax.axis_index(other_axis)
    barrier = pltpu.get_barrier_semaphore()
    for k in range(1, n):
        peer = lax.rem(me + k, n)
        pl.semaphore_signal(
            barrier, inc=1, device_id={axis: peer, other_axis: other}, device_id_type=pl.DeviceIdType.MESH
        )
    pl.semaphore_wait(barrier, n - 1)
    copies = []
    for k in range(1, n):
        peer = lax.rem(me + k, n)
        copy = pltpu.make_async_remote_copy(
            src_ref=send_ref.at[peer],
            dst_ref=recv_ref.at[me],
            send_sem=send_sem.at[k],
            recv_sem=recv_sem.at[k],
            device_id={axis: peer, other_axis: other},
            device_id_type=pl.DeviceIdType.MESH,
        )
        copy.start()
        copies.append(copy)
    own = pltpu.make_async_copy(send_ref.at[me], recv_ref.at[me], local_sem)
    own.start()
    own.wait()
    for copy in copies:
        copy.wait_send()
    for k in range(1, n):
        src = lax.rem(me + n - k, n)
        pltpu.make_async_remote_copy(
            src_ref=send_ref.at[src],
            dst_ref=recv_ref.at[src],
            send_sem=send_sem.at[k],
            recv_sem=recv_sem.at[k],
            device_id={axis: src, other_axis: other},
            device_id_type=pl.DeviceIdType.MESH,
        ).wait_recv()


def req_a2a(x, collective_id):
    n = x.shape[0]
    return pl.pallas_call(
        functools.partial(req_a2a_kernel, axis="req", other_axis="hist"),
        out_shape=jax.ShapeDtypeStruct(x.shape, x.dtype),
        in_specs=[pl.BlockSpec(memory_space=pl.ANY)],
        out_specs=pl.BlockSpec(memory_space=pl.ANY),
        scratch_shapes=[
            pltpu.SemaphoreType.DMA((n,)),
            pltpu.SemaphoreType.DMA((n,)),
            pltpu.SemaphoreType.DMA(()),
        ],
        compiler_params=pltpu.CompilerParams(collective_id=collective_id, has_side_effects=True),
    )(x)


def attend_kernel(len_ref, kv_ref, qsrc_ref, *rest, n_tiles, sub, tile_len, offset, q_row, score_scale, chunk):
    if len(rest) == 4:
        init_ref, out_ref, q_ref, o_ref = rest
    else:
        init_ref = out_ref = None
        o_ref, q_ref = rest
    length = len_ref[0]
    n_cls, _, head_dim = kv_ref.shape
    span = n_tiles * sub
    block = q_ref.shape[0] // n_cls
    half_scale = 0.5 * score_scale
    for b in range(n_cls):
        q_ref[pl.ds(b * block, block), :] = qsrc_ref[b, pl.ds(q_row, block), :]
    if init_ref is None:
        o_ref[...] = jnp.zeros_like(o_ref)
    else:
        o_ref[...] = init_ref[...]

    group = 8 if 8 * span <= 2560 else (4 if 4 * span <= 1280 else (1 if span % 128 == 0 else 2))

    def one_class(g, carry):
        c = g * group
        key_index = lax.broadcasted_iota(jnp.int32, (1, group * span), 1)
        cls = c + key_index // span
        within = key_index % span
        position = (cls + n_cls * (within // sub)) * tile_len + offset + within % sub
        live = position < length

        def add_class(masked):
            keys = jnp.concatenate([kv_ref[c + j, pl.ds(0, span), :] for j in range(group)], axis=0)
            values = jnp.concatenate([kv_ref[c + j, pl.ds(span, span), :] for j in range(group)], axis=0)
            for ci in range(q_ref.shape[0] // chunk):
                rows = pl.ds(ci * chunk, chunk)
                scores = lax.dot_general(
                    q_ref[rows, :], keys, (((1,), (1,)), ((), ())), preferred_element_type=jnp.float32
                )
                half = scores * half_scale
                weights = half + half * jnp.tanh(half)
                if masked:
                    weights = jnp.where(live, weights, 0.0)
                o_ref[rows, :] += jnp.dot(weights.astype(jnp.bfloat16), values, preferred_element_type=jnp.float32)

        last_key = (c + group - 1 + n_cls * (n_tiles - 1)) * tile_len + offset + sub
        whole = last_key <= length
        pl.when(whole)(lambda: add_class(False))
        pl.when(jnp.logical_and(jnp.logical_not(whole), c * tile_len + offset < length))(lambda: add_class(True))
        return carry

    lax.fori_loop(0, n_cls // group, one_class, 0)
    if out_ref is not None:
        out_ref[...] = o_ref[...].astype(out_ref.dtype)


def attend(length, kv_packed, q_packed, q_row, n_tiles, sub, tile_len, offset, score_scale, init=None):
    n_cls, _, head_dim = q_packed.shape
    rows = n_cls * (q_packed.shape[1] - q_row)
    chunk = 2048
    kernel = functools.partial(
        attend_kernel,
        n_tiles=n_tiles,
        sub=sub,
        tile_len=tile_len,
        offset=offset,
        q_row=q_row,
        score_scale=score_scale,
        chunk=chunk,
    )
    return pl.pallas_call(
        kernel,
        out_shape=jax.ShapeDtypeStruct((rows, head_dim), jnp.float32 if init is None else jnp.bfloat16),
        in_specs=[pl.BlockSpec(memory_space=pltpu.SMEM)]
        + [pl.BlockSpec(memory_space=pltpu.VMEM)] * (2 if init is None else 3),
        out_specs=pl.BlockSpec(memory_space=pltpu.VMEM),
        scratch_shapes=[pltpu.VMEM((rows, head_dim), jnp.bfloat16)]
        + ([] if init is None else [pltpu.VMEM((rows, head_dim), jnp.float32)]),
    )(length, kv_packed, q_packed, *([] if init is None else [init]))


def pack_kernel(picked_ref, tiles_hbm, *rest, heads, users, per_hist, with_q):
    if with_q:
        q_ref, out_ref, staged, in_sem = rest
    else:
        out_ref, staged, in_sem = rest
    width = tiles_hbm.shape[2] // 2
    head_dim = width // heads
    sub = tiles_hbm.shape[1]
    span = per_hist * sub
    n_in = users * per_hist
    reads = []
    for i in range(n_in):
        read = pltpu.make_async_copy(tiles_hbm.at[picked_ref[i]], staged.at[i], in_sem.at[i])
        read.start()
        reads.append(read)
    if with_q:
        cand_rows = q_ref.shape[1]
        for u in range(users):
            for e in range(heads):
                out_ref[u * heads + e, pl.ds(2 * span, cand_rows), :] = q_ref[u, :, pl.ds(e * head_dim, head_dim)]
    for i in range(n_in):
        u, t = divmod(i, per_hist)
        reads[i].wait()
        for piece in range(2 * heads):
            e, kv = divmod(piece, 2)
            out_ref[u * heads + e, pl.ds(kv * span + t * sub, sub), :] = staged[
                i, :, pl.ds(piece * head_dim, head_dim)
            ]


def pack_for_heads(picked_slot, tiles, queries, users, heads):
    n_in = picked_slot.shape[0]
    per_hist = n_in // users
    sub, wide = tiles.shape[1], tiles.shape[2]
    head_dim = wide // (2 * heads)
    rows = 2 * per_hist * sub + (0 if queries is None else queries.shape[1])
    operands = [picked_slot, tiles] + ([] if queries is None else [queries])
    return pl.pallas_call(
        functools.partial(pack_kernel, heads=heads, users=users, per_hist=per_hist, with_q=queries is not None),
        out_shape=jax.ShapeDtypeStruct((users * heads, rows, head_dim), tiles.dtype),
        in_specs=[pl.BlockSpec(memory_space=pltpu.SMEM), pl.BlockSpec(memory_space=pl.ANY)]
        + ([] if queries is None else [pl.BlockSpec(memory_space=pltpu.VMEM)]),
        out_specs=pl.BlockSpec(memory_space=pltpu.VMEM),
        scratch_shapes=[
            pltpu.VMEM((n_in, sub, wide), tiles.dtype),
            pltpu.SemaphoreType.DMA((n_in,)),
        ],
    )(*operands)


def finish_kernel(
    bias_ref, len_ref, limit_ref, hist_ref, proj_ref, x_ref, w_ref, out_ref, att_ref, *, heads, score_scale
):
    users, rows, width = x_ref.shape
    head_dim = width // heads
    for u in range(users):
        divisor = (len_ref[u] + 1).astype(jnp.float32)
        for e in range(heads):
            value = proj_ref[u, :, pl.ds(width + e * head_dim, head_dim)].astype(jnp.float32)
            query = proj_ref[u, :, pl.ds(2 * width + e * head_dim, head_dim)].astype(jnp.float32)
            key = proj_ref[u, :, pl.ds(3 * width + e * head_dim, head_dim)].astype(jnp.float32)
            self_score = jnp.sum(query * key, axis=-1, keepdims=True) * score_scale + bias_ref[e]
            own = self_score * (0.5 + 0.5 * jnp.tanh(0.5 * self_score)) * value
            history = hist_ref[u * heads + e].astype(jnp.float32)
            att_ref[:, pl.ds(e * head_dim, head_dim)] = (history + own) / divisor
        attended = att_ref[...]
        centred = attended - jnp.mean(attended, axis=-1, keepdims=True)
        spread = jnp.mean(centred * centred, axis=-1, keepdims=True)
        gate = proj_ref[u, :, pl.ds(0, width)].astype(jnp.float32)
        gated = (centred * lax.rsqrt(spread + 1e-05) * gate).astype(jnp.bfloat16)
        result = x_ref[u].astype(jnp.float32) + jnp.dot(gated, w_ref[...], preferred_element_type=jnp.float32)
        row = lax.broadcasted_iota(jnp.int32, (rows, 1), 0)
        out_ref[u] = jnp.where(row < limit_ref[u], result, 0.0).astype(out_ref.dtype)


def finish(history_back, projected, cand_x, w_out, self_bias, lengths, row_limit, heads, score_scale):
    users, rows, width = cand_x.shape
    smem = pl.BlockSpec(memory_space=pltpu.SMEM)
    vmem = pl.BlockSpec(memory_space=pltpu.VMEM)
    return pl.pallas_call(
        functools.partial(finish_kernel, heads=heads, score_scale=score_scale),
        out_shape=jax.ShapeDtypeStruct(cand_x.shape, cand_x.dtype),
        in_specs=[smem, smem, smem, vmem, vmem, vmem, vmem],
        out_specs=vmem,
        scratch_shapes=[pltpu.VMEM((rows, width), jnp.float32)],
    )(self_bias, lengths, row_limit, history_back, projected, cand_x, w_out)


def local(cand_x, kv_cache, w_uvqk, w_out, self_bias, user_rank, hist_len, cand_count, tile_slot):
    users_here, cand_rows, width = cand_x.shape
    heads = self_bias.shape[0]
    head_dim = width // heads
    score_scale = 1.0 / math.sqrt(head_dim)
    slots_own, tile_len, _ = kv_cache.shape
    user_total, tiles_max = tile_slot.shape
    req_count = lax.axis_size("req")
    hist_count = lax.axis_size("hist")
    req_index = lax.axis_index("req")
    hist_index = lax.axis_index("hist")
    per_hist = tiles_max // hist_count
    capacity = slots_own // req_count + 1
    first_slot = req_index * users_here
    user_ids = lax.dynamic_slice_in_dim(user_rank, first_slot, users_here)
    match_user = user_ids[:, None] == jnp.arange(user_total)[None, :]
    lengths = jnp.sum(jnp.where(match_user, hist_len[None, :], 0), axis=1)
    live_counts = jnp.sum(jnp.where(match_user, cand_count[None, :], 0), axis=1)
    column = lax.dynamic_index_in_dim(
        tile_slot.reshape(user_total, per_hist, hist_count), hist_index, axis=2, keepdims=False
    )
    codes = column.reshape(-1)
    owners = codes // slots_own
    local_slot = codes % slots_own
    dests = jnp.repeat(jnp.arange(user_total) // users_here, per_hist)
    entry_ids = jnp.arange(codes.shape[0])
    same_pair = (
        (owners[:, None] == owners[None, :])
        & (dests[:, None] == dests[None, :])
        & (entry_ids[:, None] > entry_ids[None, :])
    )
    places = jnp.sum(jnp.where(same_pair, 1, 0), axis=1)
    picked = (
        (owners[None, None, :] == req_index)
        & (dests[None, None, :] == jnp.arange(req_count)[:, None, None])
        & (places[None, None, :] == jnp.arange(capacity)[None, :, None])
    )
    source_slot = jnp.sum(jnp.where(picked, local_slot[None, None, :], 0), axis=2).reshape(-1)
    first_entry = first_slot * per_hist
    my_owner = lax.dynamic_slice_in_dim(owners, first_entry, users_here * per_hist)
    my_place = lax.dynamic_slice_in_dim(places, first_entry, users_here * per_hist)
    picked_slot = (my_owner * capacity + my_place).astype(jnp.int32)
    first_len = tile_len * 5 // 8
    bounds = [(0, first_len), (first_len, tile_len)]
    sending = []
    for lo, hi in bounds:
        kv_half = lax.slice_in_dim(kv_cache, lo, hi, axis=1)
        outgoing = kv_half.at[source_slot].get(mode="promise_in_bounds")
        sending.append(outgoing.reshape(req_count, capacity, hi - lo, 2 * width))
    first_in = lax.all_to_all(sending[0], "req", split_axis=0, concat_axis=0, tiled=True)
    normed = layer_norm(cand_x.astype(jnp.float32)).astype(jnp.bfloat16)
    mixed_in = jnp.dot(normed.reshape(-1, width), w_uvqk, preferred_element_type=jnp.float32)
    projected = jax.nn.silu(mixed_in).astype(jnp.bfloat16).reshape(users_here, cand_rows, 4, width)
    projected, second_out = lax.optimization_barrier((projected, sending[1]))
    second_in = req_a2a(second_out, 0)
    halves = [
        first_in.reshape(req_count * capacity, first_len, 2 * width),
        second_in.reshape(req_count * capacity, tile_len - first_len, 2 * width),
    ]
    u_gate = projected[:, :, 0]
    v_self = projected[:, :, 1]
    queries = projected[:, :, 2]
    k_self = projected[:, :, 3]
    my_user = hist_index // heads
    my_length = lax.dynamic_slice_in_dim(lengths, my_user, 1)
    q_row = 2 * per_hist * first_len
    packed_a = lax.all_to_all(
        pack_for_heads(picked_slot, halves[0], queries, users_here, heads),
        "hist", split_axis=0, concat_axis=0, tiled=True,
    )
    history_mine = attend(my_length, packed_a, packed_a, q_row, per_hist, first_len, tile_len, 0, score_scale)
    packed_b = lax.all_to_all(
        pack_for_heads(picked_slot, halves[1], None, users_here, heads),
        "hist", split_axis=0, concat_axis=0, tiled=True,
    )
    history_mine = attend(
        my_length, packed_b, packed_a, q_row, per_hist, tile_len - first_len, tile_len, first_len, score_scale,
        init=history_mine,
    )
    history_back = lax.all_to_all(
        history_mine.reshape(hist_count, cand_rows, head_dim), "hist", split_axis=0, concat_axis=0, tiled=True
    )
    row_limit = (live_counts - hist_index * cand_rows).astype(jnp.int32)
    return finish(
        history_back, projected.reshape(users_here, cand_rows, 4 * width), cand_x, w_out, self_bias,
        lengths.astype(jnp.int32), row_limit, heads, score_scale,
    )


def solution(mesh):
    return jax.shard_map(
        local,
        mesh=mesh,
        in_specs=(
            P("req", "hist", None),
            P(("req", "hist"), None, None),
            P(),
            P(),
            P(),
            P(),
            P(),
            P(),
            P(),
        ),
        out_specs=P("req", "hist", None),
        check_vma=False,
    )
```
